128 devices in a mesh: blk: 32 (over z_lo, y, x), head: 4 (over z_hi, core).
Axes of the slice: x: 4, y: 4, z: 4 (z_hi: 2, z_lo: 2; z = z_hi * 2 + z_lo), core: 2. Of those that a mesh axis runs over, the one named last changes fastest.
Arguments:
- query_vectors: bfloat16 [4096, 2560], P('blk', 'head'), may hold values from -8 to 8
- key_vectors: bfloat16 [4096, 2560], P('blk', 'head'), may hold values from -8 to 8, as said below
- value_vectors: bfloat16 [4096, 2560], P('blk', 'head'), may hold values from -6 to 6
- tangent_queries: bfloat16 [4096, 2560], P('blk', 'head'), may hold values from -6 to 6
- tangent_keys: bfloat16 [4096, 2560], P('blk', 'head'), may hold values from -6 to 6
- tangent_values: bfloat16 [4096, 2560], P('blk', 'head'), may hold values from -6 to 6
- target_gap: bfloat16 [4096, 2560], P(('blk', 'head')), may hold values from -6 to 6
Outputs:
- primal_out: bfloat16 [4096, 2560], P(('blk', 'head'))
- tangent_out: bfloat16 [4096, 2560], P(('blk', 'head'))
- query_grad: bfloat16 [4096, 2560], P('blk', 'head')
- key_grad: bfloat16 [4096, 2560], P('blk', 'head')
- value_grad: bfloat16 [4096, 2560], P('blk', 'head')
The draws below stay inside these ranges and needn't reach their ends.
Inputs may be any that keep to these rules, and one draw needn't show every extreme that they name: `key_vectors`: keys are real-valued draws.
All inputs are finite; a program needn't handle non-finite values.
Results may differ from the reference program's by a relative error of at most 0.015.
Values may be sent and summed in bfloat16 or wider, within the bound.
No kernel may reach another device: no remote copies, remote signals or barrier semaphores. Data moves between devices by JAX's collectives and lax.ppermute only.
A program may use at most 128 MiB of HBM per device.

```python
import math
import jax
import jax.numpy as jnp
from jax import lax

HEADS = 20
HD = 128
FEAT = 2560
SEQ = 4096


def paired_fields(key):
    base_queries = jax.random.fold_in(key, 11)
    base_keys = jax.random.fold_in(key, 12)
    queries_drawn = jnp.clip(jax.random.normal(base_queries, (SEQ, FEAT), jnp.float32) * 1.4, -8.0, 8.0)
    keys_drawn = jnp.clip(jax.random.normal(base_keys, (SEQ, FEAT), jnp.float32) * 1.4, -8.0, 8.0)
    return (queries_drawn, keys_drawn)


def draw_query_vectors(key, part):
    return paired_fields(key)[0].astype(jnp.bfloat16)


def draw_key_vectors(key, part):
    return paired_fields(key)[1].astype(jnp.bfloat16)


def block_levels(own_key, dims, pieces, low, high):
    factor_of, own = 1.0, jax.random.fold_in(own_key, 6)
    for axis_at, blocks in pieces:
        draws = jnp.exp(jax.random.uniform(jax.random.fold_in(own, axis_at), (blocks,), jnp.float32, low / len(pieces), high / len(pieces)))
        factor_of = factor_of * jnp.repeat(draws, dims[axis_at] // blocks).reshape([-1 if axis == axis_at else 1 for axis in range(len(dims))])
    return factor_of


def scatter_about(own_key, dims, deviation, most, split=(), held_as=jnp.bfloat16):
    array = jax.random.normal(own_key, dims, jnp.float32) * deviation
    if len(split) > 0:
        array = block_levels(own_key, dims, split, -0.22, 0.18) * array
    return jnp.clip(array, min=-most, max=most).astype(held_as)


def setup_inputs(seed: int = 0) -> dict:
    splits = jax.random.split(jax.random.key(seed), 8)
    query_vectors = draw_query_vectors(jax.random.fold_in(splits[7], 71), 0)
    key_vectors = draw_key_vectors(jax.random.fold_in(splits[7], 71), 0)
    value_vectors = scatter_about(splits[2], (SEQ, FEAT), 1.0, 6.0, ((0, 32), (1, 4)))
    tangent_queries = scatter_about(splits[3], (SEQ, FEAT), 1.0, 6.0, ((0, 32), (1, 4)))
    tangent_keys = scatter_about(splits[4], (SEQ, FEAT), 1.0, 6.0, ((0, 32), (1, 4)))
    tangent_values = scatter_about(splits[5], (SEQ, FEAT), 1.0, 6.0, ((0, 32), (1, 4)))
    target_gap = scatter_about(splits[6], (SEQ, FEAT), 1.0, 6.0, ((0, 128),))
    return {"query_vectors": query_vectors, "key_vectors": key_vectors, "value_vectors": value_vectors, "tangent_queries": tangent_queries, "tangent_keys": tangent_keys, "tangent_values": tangent_values, "target_gap": target_gap}


scale_loss = 64.0

def heads_first(matrix):
    return matrix.reshape(SEQ, HEADS, HD).transpose(1, 0, 2)

def heads_last(matrix):
    return matrix.transpose(1, 0, 2).reshape(SEQ, HEADS * HD)

def one_head(operands):
    q_head, k_head, v_head, tq_head, tk_head, tv_head, gap_head = operands
    inverse = 1.0 / math.sqrt(HD)
    scores = jnp.dot(q_head, k_head.T, preferred_element_type=jnp.float32) * inverse
    tan_scores = (jnp.dot(tq_head, k_head.T, preferred_element_type=jnp.float32) + jnp.dot(q_head, tk_head.T, preferred_element_type=jnp.float32)) * inverse
    row_peak = lax.optimization_barrier(jnp.max(scores, axis=1, keepdims=True))
    weights = jnp.exp(scores - row_peak)
    denominator = lax.optimization_barrier(jnp.sum(weights, axis=1, keepdims=True))
    weighted_tan = weights * tan_scores
    tan_weight = lax.optimization_barrier(jnp.sum(weighted_tan, axis=1, keepdims=True))
    weights_low = weights.astype(jnp.bfloat16)
    tan_low = weighted_tan.astype(jnp.bfloat16)
    primal = jnp.dot(weights_low, v_head, preferred_element_type=jnp.float32) / denominator
    tangent = (jnp.dot(tan_low, v_head, preferred_element_type=jnp.float32) + jnp.dot(weights_low, tv_head, preferred_element_type=jnp.float32)) / denominator
    tangent = tangent - tan_weight / denominator * primal
    primal_low = primal.astype(jnp.bfloat16)
    tangent_low = tangent.astype(jnp.bfloat16)
    cotangent = (scale_loss * (gap_head.astype(jnp.float32) + tangent_low.astype(jnp.float32))).astype(jnp.bfloat16)
    log_total = row_peak + jnp.log(denominator)
    chances = jnp.exp(scores - log_total)
    inner_sums = lax.optimization_barrier(jnp.sum(cotangent.astype(jnp.float32) * primal_low.astype(jnp.float32), axis=1, keepdims=True))
    value_grad = jnp.dot(chances.astype(jnp.bfloat16).T, cotangent, preferred_element_type=jnp.float32)
    prob_grad = jnp.dot(cotangent, v_head.T, preferred_element_type=jnp.float32)
    score_grad = (chances * (prob_grad - inner_sums)).astype(jnp.bfloat16)
    query_grad = jnp.dot(score_grad, k_head, preferred_element_type=jnp.float32) * inverse
    key_grad = jnp.dot(score_grad.T, q_head, preferred_element_type=jnp.float32) * inverse
    return (primal_low, tangent_low, query_grad.astype(jnp.bfloat16), key_grad.astype(jnp.bfloat16), value_grad.astype(jnp.bfloat16))

def reference(query_vectors, key_vectors, value_vectors, tangent_queries, tangent_keys, tangent_values, target_gap):
    stacked = tuple((heads_first(member) for member in (query_vectors, key_vectors, value_vectors, tangent_queries, tangent_keys, tangent_values, target_gap)))
    results = lax.map(one_head, stacked)
    return (heads_last(results[0]), heads_last(results[1]), heads_last(results[2]), heads_last(results[3]), heads_last(results[4]))
```

```python
from functools import partial
import math

import jax
import jax.numpy as jnp
from jax import lax
from jax.experimental import pallas as pl
from jax.experimental.pallas import tpu as pltpu
from jax.sharding import Mesh, PartitionSpec as P

BF = jnp.bfloat16
F32 = jnp.float32
HD = 128
LOSS = 64.0
PARTS = 3
PIECE = 24
KROWS = 64
QPACK = 16
INV = 1.0 / math.sqrt(HD)
EXP_SCALE = INV * math.log2(math.e)
VMEM = pl.BlockSpec(memory_space=pltpu.VMEM)


def call(body, outs, ins, name, limit, scratch=(), aliases=None, cost=None):
    return pl.pallas_call(
        body,
        out_shape=outs,
        in_specs=[VMEM] * ins,
        out_specs=jax.tree.map(lambda _: VMEM, outs),
        scratch_shapes=list(scratch),
        input_output_aliases=aliases or {},
        compiler_params=pltpu.CompilerParams(vmem_limit_bytes=limit * 1024 * 1024),
        cost_estimate=cost,
        name=name,
    )


def nt(a, b):
    return lax.dot_general(a, b, (((1,), (1,)), ((), ())), preferred_element_type=F32)


def nn(a, b):
    return lax.dot_general(a, b, (((1,), (0,)), ((), ())), preferred_element_type=F32)


def split_tokens(*refs):
    ins, out = refs[:-1], refs[-1]
    for at, ref in enumerate(ins):
        for core in range(2):
            out[core, at, 0:32, :] = ref[32 * core : 32 * core + 32, :]
            out[core, at, 32:64, :] = ref[64 + 32 * core : 96 + 32 * core, :]


def pack_heads(e_ref, g_ref, out):
    heads = 2 * (e_ref.shape[3] // HD)
    half = heads // 2
    for chip in range(out.shape[0]):
        head, part = chip // PARTS, chip % PARTS
        if head >= heads:
            out[chip] = jnp.zeros(out.shape[1:], BF)
            continue
        core, cols = head // half, slice((head % half) * HD, (head % half + 1) * HD)
        out[chip, 0:64, 0:HD] = e_ref[core, 1, :, cols]
        out[chip, 0:64, HD:] = e_ref[core, 4, :, cols]
        out[chip, 64:128, 0:HD] = e_ref[core, 2, :, cols]
        out[chip, 64:128, HD:] = e_ref[core, 5, :, cols]
        low = PIECE * part
        rows = min(PIECE, KROWS - low)
        for side, at in ((0, 0), (1, 3)):
            lanes = slice(side * HD, side * HD + HD)
            out[chip, 128 : 128 + rows, lanes] = e_ref[core, at, low : low + rows, cols]
            if rows < PIECE:
                out[chip, 128 + rows : 128 + PIECE, lanes] = jnp.zeros((PIECE - rows, HD), BF)
        gcols = slice(head * HD, head * HD + HD)
        for eight in range(PIECE // 8):
            lanes = slice(0, HD) if eight < 2 else slice(HD, 2 * HD)
            to = 152 + 8 * (eight % 2)
            row = low + 8 * eight
            if row < KROWS:
                out[chip, to : to + 8, lanes] = g_ref[row // 32, row % 32 : row % 32 + 8, gcols]
            else:
                out[chip, to : to + 8, lanes] = jnp.zeros((8, HD), BF)
        out[chip, 160:168, HD:] = jnp.zeros((8, HD), BF)


def attention(
    mine, theirs, mask, out, out_theirs,
    s_ref, stage, vt_ref, kt_ref, qq_ref, q_ref, cot_ref, acc_ref, acct_ref, dq_ref, *, kc, qt
):
    slots = mine.shape[0]
    rows = slots * PIECE
    per = kc // KROWS
    steps = slots // per
    tiles = rows // qt
    sides = ((mine, out, 0), (theirs, out_theirs, slots * KROWS))
    for s in range(slots):
        at = slice(PIECE * s, PIECE * s + PIECE)
        stage[at, 0 : 2 * HD] = mine[s, 128:152, :].astype(F32)
        stage[PIECE * s : PIECE * s + 16, 2 * HD :] = mine[s, 152:168, 0:HD].astype(F32)
        stage[PIECE * s + 16 : PIECE * s + 24, 2 * HD :] = mine[s, 152:160, HD:].astype(F32)
    q_ref[...] = stage[:, 0:HD].astype(BF)
    qq_ref[:, 0:HD] = stage[:, HD : 2 * HD].astype(BF)
    qq_ref[:, HD:] = stage[:, 0:HD].astype(BF)

    def keys(ref, i, low, lanes):
        return ref[pl.ds(i * per, per), low : low + KROWS, lanes].reshape(kc, -1)

    left, right, both = slice(0, HD), slice(HD, 2 * HD), slice(0, 2 * HD)

    peak = jnp.full((8, rows), -jnp.inf, F32)
    for ref, _, base in sides:

        def scores_step(i, peak, ref=ref, base=base):
            at = pl.multiple_of(base + i * kc, kc)
            step = base // kc + i
            k = keys(ref, i, 0, left)
            kt_ref[step] = k.astype(F32).T.astype(BF)
            vt_ref[step] = keys(ref, i, KROWS, both).astype(F32).T.astype(BF)
            new = []
            for t in range(tiles):
                cols = slice(t * qt, t * qt + qt)
                s = nt(k, q_ref[cols, :])
                s_ref[pl.ds(at, kc), cols] = s
                new.append(jnp.maximum(peak[:, cols], jnp.max(s.reshape(kc // 8, 8, qt), axis=0)))
            return jnp.concatenate(new, axis=1)

        peak = lax.fori_loop(0, steps, scores_step, peak)
    peak = jnp.max(peak, axis=0, keepdims=True)

    acc_ref[...] = jnp.zeros_like(acc_ref)
    acct_ref[...] = jnp.zeros_like(acct_ref)
    sums = (jnp.zeros((8, rows), F32), jnp.zeros((8, rows), F32))
    for ref, _, base in sides:

        def forward_step(i, sums, ref=ref, base=base):
            at = pl.multiple_of(base + i * kc, kc)
            step = base // kc + i
            total, tan_total = sums
            kk = keys(ref, i, 0, both)
            vt = vt_ref[step]
            new, new_tan = [], []
            for t in range(tiles):
                cols = slice(t * qt, t * qt + qt)
                ts = nt(kk, qq_ref[cols, :])
                w = jnp.exp2((s_ref[pl.ds(at, kc), cols] - peak[:, cols]) * EXP_SCALE)
                s_ref[pl.ds(at, kc), cols] = w
                wt = w * ts
                new.append(total[:, cols] + jnp.sum(w.reshape(kc // 8, 8, qt), axis=0))
                new_tan.append(tan_total[:, cols] + jnp.sum(wt.reshape(kc // 8, 8, qt), axis=0))
                acc_ref[:, cols] += nn(vt, w.astype(BF))
                acct_ref[:, cols] += nn(vt[0:HD, :], wt.astype(BF))
            return jnp.concatenate(new, axis=1), jnp.concatenate(new_tan, axis=1)

        sums = lax.fori_loop(0, steps, forward_step, sums)
    total = jnp.sum(sums[0], axis=0, keepdims=True)
    tan_total = jnp.sum(sums[1], axis=0, keepdims=True) * INV
    share = 1.0 / total
    primal = acc_ref[0:HD, :] * share
    tangent = (acct_ref[...] * INV + acc_ref[HD:, :]) * share - (tan_total * share) * primal
    primal_low = primal.astype(BF).astype(F32)
    tangent_low = tangent.astype(BF).astype(F32)
    cot = (LOSS * (stage[:, 2 * HD :].T + tangent_low)) * mask[...]
    cot = cot.astype(BF).astype(F32)
    inner = jnp.sum(cot * primal_low, axis=0, keepdims=True)
    cot_ref[...] = cot.T.astype(BF)
    stage[:, 0:HD] = primal_low.T
    stage[:, HD : 2 * HD] = tangent_low.T

    dq_ref[...] = jnp.zeros_like(dq_ref)
    for ref, dst, base in sides:

        def backward_step(i, carry, ref=ref, dst=dst, base=base):
            at = pl.multiple_of(base + i * kc, kc)
            step = base // kc + i
            v = keys(ref, i, KROWS, left)
            kt = kt_ref[step]
            dk = jnp.zeros((kc, HD), F32)
            dv = jnp.zeros((kc, HD), F32)
            for t in range(tiles):
                cols = slice(t * qt, t * qt + qt)
                p = s_ref[pl.ds(at, kc), cols] * share[:, cols]
                ds = (p * (nt(v, cot_ref[cols, :]) - inner[:, cols])).astype(BF)
                dv = dv + nn(p.astype(BF), cot_ref[cols, :])
                dk = dk + nn(ds, q_ref[cols, :])
                dq_ref[:, cols] += nn(kt, ds)
            dst[pl.ds(i * per, per), 0:KROWS, left] = (dk * INV).astype(BF).reshape(per, KROWS, HD)
            dst[pl.ds(i * per, per), 0:KROWS, right] = dv.astype(BF).reshape(per, KROWS, HD)
            return carry

        lax.fori_loop(0, steps, backward_step, 0)
    stage[:, 2 * HD :] = (dq_ref[...] * INV).T
    for s in range(slots):
        at = slice(PIECE * s, PIECE * s + PIECE)
        out[s, 64:88, :] = stage[at, 0 : 2 * HD].astype(BF)
        out[s, 88:104, left] = stage[PIECE * s : PIECE * s + 16, 2 * HD :].astype(BF)
        out[s, 88:96, right] = stage[PIECE * s + 16 : PIECE * s + 24, 2 * HD :].astype(BF)
        out[s, 96:104, right] = jnp.zeros((8, HD), BF)


def add_partner(b_ref, d_ref, out):
    for s in range(d_ref.shape[0]):
        out[s, 0:KROWS, :] = (
            b_ref[s, 0:KROWS, :].astype(F32) + d_ref[s].astype(F32)
        ).astype(BF)


def unpack_heads(r_ref, f_ref, o_ref):
    half = f_ref.shape[3] // HD
    for head in range(2 * half):
        core, cols = head // half, slice((head % half) * HD, (head % half + 1) * HD)
        first = PARTS * head
        both = sum(r_ref[first + part, 0:KROWS, :].astype(F32) for part in range(PARTS))
        f_ref[core, 1, :, cols] = both[:, 0:HD].astype(BF)
        f_ref[core, 2, :, cols] = both[:, HD:].astype(BF)
        ocols = slice(head * HD, head * HD + HD)
        for eight in range(KROWS // 8):
            chip, low = first + eight // 3, 8 * (eight % 3)
            row = 8 * eight
            lanes = slice(0, HD) if low < 16 else slice(HD, 2 * HD)
            f_ref[core, 0, row : row + 8, cols] = r_ref[chip, 88 + low % 16 : 96 + low % 16, lanes]
            for side in range(2):
                o_ref[row // 32, side, row % 32 : row % 32 + 8, ocols] = r_ref[
                    chip, 64 + low : 72 + low, side * HD : side * HD + HD
                ]


def finish(f_ref, o_ref, primal, tangent, dq, dk, dv):
    for core in range(2):
        for at, ref in enumerate((dq, dk, dv)):
            ref[32 * core : 32 * core + 32, :] = f_ref[core, at, 0:32, :]
            ref[64 + 32 * core : 96 + 32 * core, :] = f_ref[core, at, 32:64, :]
    wide = o_ref.shape[3]
    for side, ref in enumerate((primal, tangent)):
        for group in range(2):
            ref[:, group * wide : group * wide + wide] = o_ref[group, side]


def shape(*dims, dtype=BF):
    return jax.ShapeDtypeStruct(dims, dtype)


SWAP = [(0, 1), (1, 0)]
BLOCK_AXES = ("zl", "y", "x")


def main_kernel(chips, kc, qt):
    rows = chips * PIECE
    keys = 2 * chips * KROWS
    steps = keys // kc
    flops = 2 * 8 * rows * keys * HD
    return call(
        partial(attention, kc=kc, qt=qt),
        (shape(chips, 104, 2 * HD), shape(chips, KROWS, 2 * HD)),
        3,
        "attention",
        48,
        scratch=(
            pltpu.VMEM((keys, rows), F32),
            pltpu.VMEM((rows, 3 * HD), F32),
            pltpu.VMEM((steps, 2 * HD, kc), BF),
            pltpu.VMEM((steps, HD, kc), BF),
            pltpu.VMEM((rows, 2 * HD), BF),
            pltpu.VMEM((rows, HD), BF),
            pltpu.VMEM((rows, HD), BF),
            pltpu.VMEM((2 * HD, rows), F32),
            pltpu.VMEM((HD, rows), F32),
            pltpu.VMEM((HD, rows), F32),
        ),
        cost=pl.CostEstimate(flops=flops, bytes_accessed=9_000_000, transcendentals=rows * keys),
    )


def per_device(q, k, v, tq, tk, tv, gap):
    chips = lax.axis_size(BLOCK_AXES)
    local, feat = q.shape
    wide = gap.shape[1] // 2
    group = lax.axis_index("zh")
    low, high = gap[:, :wide], gap[:, wide:]
    got = lax.ppermute(jnp.where(group == 0, high, low), "zh", SWAP)
    sent = call(split_tokens, shape(2, 6, KROWS, feat), 6, "split_tokens", 8)(q, k, v, tq, tk, tv)
    here = lax.all_to_all(sent, "c", 0, 0, tiled=True)
    own = jnp.where(group == 0, low, high)
    gaps = jnp.stack([jnp.where(group == 0, own, got), jnp.where(group == 0, got, own)])
    packed = call(pack_heads, shape(chips, 168, 2 * HD), 2, "pack_heads", 12)(here, gaps)
    mine = lax.all_to_all(packed, BLOCK_AXES, 0, 0, tiled=True)
    theirs = lax.ppermute(mine, "c", SWAP)
    rows = chips * PIECE
    part = lax.axis_index(BLOCK_AXES) % PARTS
    short = (jnp.arange(rows) % PIECE >= KROWS - PIECE * (PARTS - 1)) & (part == PARTS - 1)
    mask = jnp.where(short, 0.0, 1.0).astype(F32)[None]
    out, out_theirs = main_kernel(chips, 256, 256)(mine, theirs, mask)
    partner = lax.ppermute(out_theirs, "c", SWAP)
    back = call(add_partner, shape(chips, 104, 2 * HD), 2, "add_partner", 8, aliases={0: 0})(out, partner)
    back = lax.all_to_all(back, BLOCK_AXES, 0, 0, tiled=True)
    grads, outs = call(
        unpack_heads, (shape(2, 3, KROWS, feat), shape(2, 2, 32, wide)), 1, "unpack_heads", 12
    )(back)
    other = jnp.where(group == 0, outs[1], outs[0])
    got = lax.ppermute(other, "zh", SWAP)
    grads = lax.all_to_all(grads, "c", 0, 0, tiled=True)
    own = jnp.where(group == 0, outs[0], outs[1])
    outs = jnp.stack([jnp.where(group == 0, own, got), jnp.where(group == 0, got, own)])
    small, large = shape(32, 2 * wide), shape(local, feat)
    return call(finish, (small, small, large, large, large), 2, "finish", 8)(grads, outs)


def solution(mesh):
    zl, y, x, zh, c = 2, 4, 4, 2, 2
    inner = Mesh(mesh.devices.reshape(zl, y, x, zh, c), BLOCK_AXES + ("zh", "c"))
    both = P(BLOCK_AXES, ("zh", "c"))
    rows = P(BLOCK_AXES + ("zh", "c"), None)
    return jax.shard_map(
        per_device,
        mesh=inner,
        in_specs=(both,) * 6 + (rows,),
        out_specs=(rows, rows, both, both, both),
        check_vma=False,
    )
```

```python
from functools import partial
import math

import jax
import jax.numpy as jnp
from jax import lax
from jax.experimental import pallas as pl
from jax.experimental.pallas import tpu as pltpu
from jax.sharding import Mesh, PartitionSpec as P

BF = jnp.bfloat16
F32 = jnp.float32
HD = 128
LOSS = 64.0
PARTS = 3
PIECE = 24
KROWS = 64
QPACK = 16
INV = 1.0 / math.sqrt(HD)
EXP_SCALE = INV * math.log2(math.e)
VMEM = pl.BlockSpec(memory_space=pltpu.VMEM)


HBM = pl.BlockSpec(memory_space=pltpu.HBM)


def call(body, outs, ins, name, limit, scratch=(), cost=None, aliases=None):
    return pl.pallas_call(
        body,
        out_shape=[one for one, _ in outs],
        in_specs=ins,
        out_specs=[place for _, place in outs],
        scratch_shapes=list(scratch),
        input_output_aliases=aliases or {},
        compiler_params=pltpu.CompilerParams(vmem_limit_bytes=limit * 1024 * 1024),
        cost_estimate=cost,
        name=name,
    )


def nt(a, b):
    return lax.dot_general(a, b, (((1,), (1,)), ((), ())), preferred_element_type=F32)


def nn(a, b):
    return lax.dot_general(a, b, (((1,), (0,)), ((), ())), preferred_element_type=F32)


def core():
    return lax.axis_index("c")


def group():
    return lax.axis_index("zh")


def split_tokens(*refs):
    *arrays, gap, sent, kept, gap_sent, gap_kept, sems, gap_sems = refs
    wide = gap_sent.shape[1]
    copies = []
    for at, (dst, who) in enumerate(((gap_sent, 1 - group()), (gap_kept, group()))):
        lanes = pl.ds(pl.multiple_of(who * wide, HD), wide)
        copies.append(pltpu.make_async_copy(gap.at[:, lanes], dst, gap_sems.at[at]))
    for at, ref in enumerate(arrays):
        for half in range(2):
            for side, (dst, who) in enumerate(((sent, 1 - core()), (kept, core()))):
                low = pl.multiple_of(64 * half + 32 * who, 32)
                copies.append(
                    pltpu.make_async_copy(
                        ref.at[pl.ds(low, 32), :],
                        dst.at[at, 32 * half : 32 * half + 32, :],
                        sems.at[at, half, side],
                    )
                )
    for copy in copies:
        copy.start()
    for copy in copies:
        copy.wait()


def pack_heads(kept, got, gap, got_gap, out, e_ref, g_ref):
    e_ref[core()] = kept[...]
    e_ref[1 - core()] = got[...]
    g_ref[group()] = gap[...]
    g_ref[1 - group()] = got_gap[...]
    heads = 2 * (e_ref.shape[3] // HD)
    half = heads // 2
    for chip in range(out.shape[0]):
        head, part = chip // PARTS, chip % PARTS
        if head >= heads:
            out[chip] = jnp.zeros(out.shape[1:], BF)
            continue
        at_core, cols = head // half, slice((head % half) * HD, (head % half + 1) * HD)
        out[chip, 0:64, 0:HD] = e_ref[at_core, 1, :, cols]
        out[chip, 0:64, HD:] = e_ref[at_core, 4, :, cols]
        out[chip, 64:128, 0:HD] = e_ref[at_core, 2, :, cols]
        out[chip, 64:128, HD:] = e_ref[at_core, 5, :, cols]
        low = PIECE * part
        rows = min(PIECE, KROWS - low)
        for side, at in ((0, 0), (1, 3)):
            lanes = slice(side * HD, side * HD + HD)
            out[chip, 128 : 128 + rows, lanes] = e_ref[at_core, at, low : low + rows, cols]
            if rows < PIECE:
                out[chip, 128 + rows : 128 + PIECE, lanes] = jnp.zeros((PIECE - rows, HD), BF)
        gcols = slice(head * HD, head * HD + HD)
        for eight in range(PIECE // 8):
            lanes = slice(0, HD) if eight < 2 else slice(HD, 2 * HD)
            to = 152 + 8 * (eight % 2)
            row = low + 8 * eight
            if row < KROWS:
                out[chip, to : to + 8, lanes] = g_ref[row // 32, row % 32 : row % 32 + 8, gcols]
            else:
                out[chip, to : to + 8, lanes] = jnp.zeros((8, HD), BF)
        out[chip, 160:168, HD:] = jnp.zeros((8, HD), BF)


def attention(
    mine, theirs, mask, out, out_theirs,
    s_ref, stage, vt_ref, kt_ref, qq_ref, q_ref, cot_ref, acc_ref, acct_ref, dq_ref, *, kc, qt
):
    slots = mine.shape[0]
    rows = slots * PIECE
    per = kc // KROWS
    steps = slots // per
    tiles = rows // qt
    sides = ((mine, out, 0), (theirs, out_theirs, slots * KROWS))
    for s in range(slots):
        at = slice(PIECE * s, PIECE * s + PIECE)
        stage[at, 0 : 2 * HD] = mine[s, 128:152, :].astype(F32)
        stage[PIECE * s : PIECE * s + 16, 2 * HD :] = mine[s, 152:168, 0:HD].astype(F32)
        stage[PIECE * s + 16 : PIECE * s + 24, 2 * HD :] = mine[s, 152:160, HD:].astype(F32)
    q_ref[...] = stage[:, 0:HD].astype(BF)
    qq_ref[:, 0:HD] = stage[:, HD : 2 * HD].astype(BF)
    qq_ref[:, HD:] = stage[:, 0:HD].astype(BF)

    def keys(ref, i, low, lanes):
        return ref[pl.ds(i * per, per), low : low + KROWS, lanes].reshape(kc, -1)

    left, right, both = slice(0, HD), slice(HD, 2 * HD), slice(0, 2 * HD)

    peak = jnp.full((8, rows), -jnp.inf, F32)
    for ref, _, base in sides:

        def scores_step(i, peak, ref=ref, base=base):
            at = pl.multiple_of(base + i * kc, kc)
            step = base // kc + i
            k = keys(ref, i, 0, left)
            kt_ref[step] = k.astype(F32).T.astype(BF)
            vt_ref[step] = keys(ref, i, KROWS, both).astype(F32).T.astype(BF)
            new = []
            for t in range(tiles):
                cols = slice(t * qt, t * qt + qt)
                s = nt(k, q_ref[cols, :])
                s_ref[pl.ds(at, kc), cols] = s
                new.append(jnp.maximum(peak[:, cols], jnp.max(s.reshape(kc // 8, 8, qt), axis=0)))
            return jnp.concatenate(new, axis=1)

        peak = lax.fori_loop(0, steps, scores_step, peak)
    peak = jnp.max(peak, axis=0, keepdims=True)

    acc_ref[...] = jnp.zeros_like(acc_ref)
    acct_ref[...] = jnp.zeros_like(acct_ref)
    sums = (jnp.zeros((8, rows), F32), jnp.zeros((8, rows), F32))
    for ref, _, base in sides:

        def forward_step(i, sums, ref=ref, base=base):
            at = pl.multiple_of(base + i * kc, kc)
            step = base // kc + i
            total, tan_total = sums
            kk = keys(ref, i, 0, both)
            vt = vt_ref[step]
            new, new_tan = [], []
            for t in range(tiles):
                cols = slice(t * qt, t * qt + qt)
                ts = nt(kk, qq_ref[cols, :])
                w = jnp.exp2((s_ref[pl.ds(at, kc), cols] - peak[:, cols]) * EXP_SCALE)
                s_ref[pl.ds(at, kc), cols] = w
                wt = w * ts
                new.append(total[:, cols] + jnp.sum(w.reshape(kc // 8, 8, qt), axis=0))
                new_tan.append(tan_total[:, cols] + jnp.sum(wt.reshape(kc // 8, 8, qt), axis=0))
                acc_ref[:, cols] += nn(vt, w.astype(BF))
                acct_ref[:, cols] += nn(vt[0:HD, :], wt.astype(BF))
            return jnp.concatenate(new, axis=1), jnp.concatenate(new_tan, axis=1)

        sums = lax.fori_loop(0, steps, forward_step, sums)
    total = jnp.sum(sums[0], axis=0, keepdims=True)
    tan_total = jnp.sum(sums[1], axis=0, keepdims=True) * INV
    share = 1.0 / total
    primal = acc_ref[0:HD, :] * share
    tangent = (acct_ref[...] * INV + acc_ref[HD:, :]) * share - (tan_total * share) * primal
    primal_low = primal.astype(BF).astype(F32)
    tangent_low = tangent.astype(BF).astype(F32)
    cot = (LOSS * (stage[:, 2 * HD :].T + tangent_low)) * mask[...]
    cot = cot.astype(BF).astype(F32)
    inner = jnp.sum(cot * primal_low, axis=0, keepdims=True)
    cot_ref[...] = cot.T.astype(BF)
    stage[:, 0:HD] = primal_low.T
    stage[:, HD : 2 * HD] = tangent_low.T

    dq_ref[...] = jnp.zeros_like(dq_ref)
    for ref, dst, base in sides:

        def backward_step(i, carry, ref=ref, dst=dst, base=base):
            at = pl.multiple_of(base + i * kc, kc)
            step = base // kc + i
            v = keys(ref, i, KROWS, left)
            kt = kt_ref[step]
            dk = jnp.zeros((kc, HD), F32)
            dv = jnp.zeros((kc, HD), F32)
            for t in range(tiles):
                cols = slice(t * qt, t * qt + qt)
                p = s_ref[pl.ds(at, kc), cols] * share[:, cols]
                ds = (p * (nt(v, cot_ref[cols, :]) - inner[:, cols])).astype(BF)
                dv = dv + nn(p.astype(BF), cot_ref[cols, :])
                dk = dk + nn(ds, q_ref[cols, :])
                dq_ref[:, cols] += nn(kt, ds)
            dst[pl.ds(i * per, per), 0:KROWS, left] = (dk * INV).astype(BF).reshape(per, KROWS, HD)
            dst[pl.ds(i * per, per), 0:KROWS, right] = dv.astype(BF).reshape(per, KROWS, HD)
            return carry

        lax.fori_loop(0, steps, backward_step, 0)
    stage[:, 2 * HD :] = (dq_ref[...] * INV).T
    for s in range(slots):
        at = slice(PIECE * s, PIECE * s + PIECE)
        out[s, 64:88, :] = stage[at, 0 : 2 * HD].astype(BF)
        out[s, 88:104, left] = stage[PIECE * s : PIECE * s + 16, 2 * HD :].astype(BF)
        out[s, 88:96, right] = stage[PIECE * s + 16 : PIECE * s + 24, 2 * HD :].astype(BF)
        out[s, 96:104, right] = jnp.zeros((8, HD), BF)


def add_partner(b_ref, d_ref, out):
    for s in range(d_ref.shape[0]):
        out[s, 0:KROWS, :] = (
            b_ref[s, 0:KROWS, :].astype(F32) + d_ref[s].astype(F32)
        ).astype(BF)


def unpack_heads(r_ref, sent, kept, o_sent, o_kept, f_ref, o_ref):
    half = f_ref.shape[3] // HD
    for head in range(2 * half):
        at_core, cols = head // half, slice((head % half) * HD, (head % half + 1) * HD)
        first = PARTS * head
        both = sum(r_ref[first + part, 0:KROWS, :].astype(F32) for part in range(PARTS))
        f_ref[at_core, 1, :, cols] = both[:, 0:HD].astype(BF)
        f_ref[at_core, 2, :, cols] = both[:, HD:].astype(BF)
        ocols = slice(head * HD, head * HD + HD)
        for eight in range(KROWS // 8):
            chip, low = first + eight // 3, 8 * (eight % 3)
            row = 8 * eight
            lanes = slice(0, HD) if low < 16 else slice(HD, 2 * HD)
            f_ref[at_core, 0, row : row + 8, cols] = r_ref[chip, 88 + low % 16 : 96 + low % 16, lanes]
            for side in range(2):
                o_ref[row // 32, side, row % 32 : row % 32 + 8, ocols] = r_ref[
                    chip, 64 + low : 72 + low, side * HD : side * HD + HD
                ]
    sent[...] = f_ref[1 - core()]
    kept[...] = f_ref[core()]
    o_sent[...] = o_ref[1 - group()]
    o_kept[...] = o_ref[group()]


def finish(kept, got, o_kept, o_got, primal, tangent, dq, dk, dv):
    for at, ref in enumerate((dq, dk, dv)):
        for half in range(2):
            rows = slice(32 * half, 32 * half + 32)
            for piece, who in ((kept, core()), (got, 1 - core())):
                low = pl.multiple_of(64 * half + 32 * who, 32)
                ref[pl.ds(low, 32), :] = piece[at, rows, :]
    wide = o_kept.shape[2]
    for side, ref in enumerate((primal, tangent)):
        for piece, who in ((o_kept, group()), (o_got, 1 - group())):
            ref[:, pl.ds(pl.multiple_of(wide * who, HD), wide)] = piece[side]


def shape(*dims, dtype=BF):
    return jax.ShapeDtypeStruct(dims, dtype)


SWAP = [(0, 1), (1, 0)]
BLOCK_AXES = ("zl", "y", "x")


def main_kernel(chips, kc, qt):
    rows = chips * PIECE
    keys = 2 * chips * KROWS
    steps = keys // kc
    flops = 2 * 8 * rows * keys * HD
    return call(
        partial(attention, kc=kc, qt=qt),
        ((shape(chips, 104, 2 * HD), VMEM), (shape(chips, KROWS, 2 * HD), VMEM)),
        [VMEM] * 3,
        "attention",
        34,
        scratch=(
            pltpu.VMEM((keys, rows), F32),
            pltpu.VMEM((rows, 3 * HD), F32),
            pltpu.VMEM((steps, 2 * HD, kc), BF),
            pltpu.VMEM((steps, HD, kc), BF),
            pltpu.VMEM((rows, 2 * HD), BF),
            pltpu.VMEM((rows, HD), BF),
            pltpu.VMEM((rows, HD), BF),
            pltpu.VMEM((2 * HD, rows), F32),
            pltpu.VMEM((HD, rows), F32),
            pltpu.VMEM((HD, rows), F32),
        ),
        cost=pl.CostEstimate(flops=flops, bytes_accessed=9_000_000, transcendentals=rows * keys),
    )


def per_device(q, k, v, tq, tk, tv, gap):
    chips = lax.axis_size(BLOCK_AXES)
    local, feat = q.shape
    wide = gap.shape[1] // 2
    piece = shape(6, KROWS, feat)
    arrays = (q, k, v, tq, tk, tv, gap)
    sent, kept, gap_sent, gap_kept = call(
        split_tokens,
        ((piece, VMEM), (piece, VMEM), (shape(32, wide), VMEM), (shape(32, wide), VMEM)),
        [HBM] * 7,
        "split_tokens",
        6,
        scratch=(pltpu.SemaphoreType.DMA((6, 2, 2)), pltpu.SemaphoreType.DMA((2,))),
    )(*(pltpu.with_memory_space_constraint(one, pltpu.HBM) for one in arrays))
    got_gap = lax.ppermute(gap_sent, "zh", SWAP)
    got = lax.ppermute(sent, "c", SWAP)
    packed = call(
        pack_heads,
        ((shape(chips, 168, 2 * HD), VMEM),),
        [VMEM] * 4,
        "pack_heads",
        12,
        scratch=(pltpu.VMEM((2, 6, KROWS, feat), BF), pltpu.VMEM((2, 32, wide), BF)),
    )(kept, got, gap_kept, got_gap)[0]
    mine = lax.all_to_all(packed, BLOCK_AXES, 0, 0, tiled=True)
    theirs = lax.ppermute(mine, "c", SWAP)
    rows = chips * PIECE
    part = lax.axis_index(BLOCK_AXES) % PARTS
    short = (jnp.arange(rows) % PIECE >= KROWS - PIECE * (PARTS - 1)) & (part == PARTS - 1)
    mask = jnp.where(short, 0.0, 1.0).astype(F32)[None]
    out, out_theirs = main_kernel(chips, 1024, 256)(mine, theirs, mask)
    partner = lax.ppermute(out_theirs, "c", SWAP)
    back = call(
        add_partner, ((shape(chips, 104, 2 * HD), VMEM),), [VMEM] * 2, "add_partner", 8, aliases={0: 0}
    )(out, partner)[0]
    back = lax.all_to_all(back, BLOCK_AXES, 0, 0, tiled=True)
    piece, opiece = shape(3, KROWS, feat), shape(2, 32, wide)
    sent, kept, o_sent, o_kept = call(
        unpack_heads,
        ((piece, VMEM), (piece, VMEM), (opiece, VMEM), (opiece, VMEM)),
        [VMEM],
        "unpack_heads",
        12,
        scratch=(pltpu.VMEM((2, 3, KROWS, feat), BF), pltpu.VMEM((2, 2, 32, wide), BF)),
    )(back)
    o_got = lax.ppermute(o_sent, "zh", SWAP)
    got = lax.ppermute(sent, "c", SWAP)
    small, large = shape(32, 2 * wide), shape(local, feat)
    return tuple(
        call(
            finish,
            ((small, VMEM), (small, VMEM), (large, VMEM), (large, VMEM), (large, VMEM)),
            [VMEM] * 4,
            "finish",
            8,
        )(kept, got, o_kept, o_got)
    )


def solution(mesh):
    zl, y, x, zh, c = 2, 4, 4, 2, 2
    inner = Mesh(mesh.devices.reshape(zl, y, x, zh, c), BLOCK_AXES + ("zh", "c"))
    both = P(BLOCK_AXES, ("zh", "c"))
    rows = P(BLOCK_AXES + ("zh", "c"), None)
    return jax.shard_map(
        per_device,
        mesh=inner,
        in_specs=(both,) * 6 + (rows,),
        out_specs=(rows, rows, both, both, both),
        check_vma=False,
    )
```

```python
import math

import jax
import jax.numpy as jnp
from jax import lax
from jax.experimental import pallas as pl
from jax.experimental.pallas import tpu as pltpu
from jax.sharding import Mesh, PartitionSpec as P


BF = jnp.bfloat16
F32 = jnp.float32
HD = 128
LOSS = 64.0
PARTS = 3
PIECE = 24
KROWS = 64
QT = 256
SUB = 512
INV = 1.0 / math.sqrt(HD)
EXP_SCALE = INV * math.log2(math.e)
VMEM = pl.BlockSpec(memory_space=pltpu.VMEM)
HBM = pl.BlockSpec(memory_space=pltpu.HBM)


def call(body, outs, ins, limit, scratch=(), flops=0, exps=0, moved=1_000_000):
    return pl.pallas_call(
        body,
        out_shape=[
            pltpu.HBM(one.shape, one.dtype) if place is HBM else one for one, place in outs
        ],
        in_specs=ins,
        out_specs=[place for _, place in outs],
        scratch_shapes=list(scratch),
        compiler_params=pltpu.CompilerParams(vmem_limit_bytes=limit * 1024 * 1024),
        cost_estimate=pl.CostEstimate(flops=flops, bytes_accessed=moved, transcendentals=exps),
    )


def nt(a, b):
    return lax.dot_general(a, b, (((1,), (1,)), ((), ())), preferred_element_type=F32)


def nn(a, b):
    return lax.dot_general(a, b, (((1,), (0,)), ((), ())), preferred_element_type=F32)


def core():
    return lax.axis_index("c")


def group():
    return lax.axis_index("zh")


def split_tokens(*refs):
    *arrays, gap, sent, kept, gap_sent, gap_kept, sems, gap_sems = refs
    wide = gap_sent.shape[1]
    copies = []
    for at, (dst, who) in enumerate(((gap_sent, 1 - group()), (gap_kept, group()))):
        lanes = pl.ds(pl.multiple_of(who * wide, HD), wide)
        copies.append(pltpu.make_async_copy(gap.at[:, lanes], dst, gap_sems.at[at]))
    for at, ref in enumerate(arrays):
        for half in range(2):
            for side, (dst, who) in enumerate(((sent, 1 - core()), (kept, core()))):
                low = pl.multiple_of(64 * half + 32 * who, 32)
                copies.append(
                    pltpu.make_async_copy(
                        ref.at[pl.ds(low, 32), :],
                        dst.at[at, 32 * half : 32 * half + 32, :],
                        sems.at[at, half, side],
                    )
                )
    for copy in copies:
        copy.start()
    for copy in copies:
        copy.wait()


def spread(out, stage, sems, fill):
    lot = out.shape[0] // sems.shape[0]
    copies = []
    for at in range(sems.shape[0]):
        for chip in range(lot * at, lot * at + lot):
            fill(chip)
        rows = pl.ds(lot * at, lot)
        copies.append(pltpu.make_async_copy(stage.at[rows], out.at[rows], sems.at[at]))
        copies[-1].start()
    for copy in copies:
        copy.wait()


def pack_heads(kept, got, out, e_ref, stage, sems):
    e_ref[core()] = kept[...]
    e_ref[1 - core()] = got[...]
    half = e_ref.shape[3] // HD

    def fill(chip):
        head, part = chip // PARTS, chip % PARTS
        if head >= 2 * half:
            stage[chip] = jnp.zeros(stage.shape[1:], BF)
            return
        at, cols = head // half, slice((head % half) * HD, (head % half + 1) * HD)
        stage[chip, 0:64, 0:HD] = e_ref[at, 1, :, cols]
        stage[chip, 0:64, HD:] = e_ref[at, 4, :, cols]
        stage[chip, 64:128, 0:HD] = e_ref[at, 2, :, cols]
        stage[chip, 64:128, HD:] = e_ref[at, 5, :, cols]
        low = PIECE * part
        rows = min(PIECE, KROWS - low)
        for side, array in ((0, 0), (1, 3)):
            lanes = slice(side * HD, side * HD + HD)
            stage[chip, 128 : 128 + rows, lanes] = e_ref[at, array, low : low + rows, cols]
            if rows < PIECE:
                stage[chip, 128 + rows : 152, lanes] = jnp.zeros((PIECE - rows, HD), BF)

    spread(out, stage, sems, fill)


def pack_gaps(gap, got_gap, out, g_ref, stage, sems):
    g_ref[group()] = gap[...]
    g_ref[1 - group()] = got_gap[...]
    heads = gap.shape[1] // HD

    def fill(chip):
        head, low = chip // PARTS, PIECE * (chip % PARTS)
        stage[chip] = jnp.zeros(stage.shape[1:], BF)
        if head >= heads:
            return
        gcols = slice(head * HD, head * HD + HD)
        for eight in range(PIECE // 8):
            lanes = slice(0, HD) if eight < 2 else slice(HD, 2 * HD)
            to, row = 8 * (eight % 2), low + 8 * eight
            if row < KROWS:
                stage[chip, to : to + 8, lanes] = g_ref[row // 32, row % 32 : row % 32 + 8, gcols]

    spread(out, stage, sems, fill)


def fold(x, op):
    return op(x.reshape(x.shape[0] // 8, 8, x.shape[1]), axis=0)


def rows_of(ref, slot, count, low):
    return ref[slot : slot + count, low : low + KROWS, :].reshape(count * KROWS, 2 * HD)


def forward(keys, q_ref, qq_ref, w_ref, m_ref, sums_ref, acc_ref, s_ref, wt_ref, kk_ref, vt_ref):
    tiles = q_ref.shape[0]
    length = kk_ref.shape[0]
    per = SUB // KROWS
    subs = length // SUB
    for i in range(subs):
        at = slice(SUB * i, SUB * i + SUB)
        kk_ref[at, :] = rows_of(keys, per * i, per, 0)
        vt_ref[:, at] = rows_of(keys, per * i, per, KROWS).astype(F32).T.astype(BF)

    def tile(t, carry):
        q, qq = q_ref[t], qq_ref[t]
        peak = jnp.full((8, QT), -jnp.inf, F32)
        for i in range(subs):
            at = slice(SUB * i, SUB * i + SUB)
            s = nt(kk_ref[at, 0:HD], q)
            s_ref[at, :] = s
            peak = jnp.maximum(peak, fold(s, jnp.max))
        peak = jnp.max(peak, axis=0, keepdims=True)
        total = jnp.zeros((8, QT), F32)
        tan_total = jnp.zeros((8, QT), F32)
        for i in range(subs):
            at = slice(SUB * i, SUB * i + SUB)
            w = jnp.exp2((s_ref[at, :] - peak) * EXP_SCALE)
            wt = w * nt(kk_ref[at, :], qq)
            total = total + fold(w, jnp.sum)
            tan_total = tan_total + fold(wt, jnp.sum)
            w_ref[t, at, :] = w.astype(BF)
            wt_ref[at, :] = wt.astype(BF)
        m_ref[t] = peak
        sums_ref[t, 0:1, :] = jnp.sum(total, axis=0, keepdims=True)
        sums_ref[t, 1:2, :] = jnp.sum(tan_total, axis=0, keepdims=True) * INV
        both = nn(vt_ref[...], w_ref[t])
        acc_ref[t, 0:HD, :] = both[0:HD, :]
        acc_ref[t, HD:, :] = both[HD:, :] + nn(vt_ref[0:HD, :], wt_ref[...]) * INV
        return carry

    lax.fori_loop(0, tiles, tile, 0)


def forward_mine(mine, q_ref, qq_ref, w_ref, m_ref, sums_ref, acc_ref, stage, *scratch):
    for s in range(mine.shape[0]):
        stage[PIECE * s : PIECE * s + PIECE, :] = mine[s, 2 * KROWS :, :].astype(F32)
    for t in range(q_ref.shape[0]):
        rows = slice(QT * t, QT * t + QT)
        q_ref[t] = stage[rows, 0:HD].astype(BF)
        qq_ref[t, :, 0:HD] = stage[rows, HD:].astype(BF)
        qq_ref[t, :, HD:] = stage[rows, 0:HD].astype(BF)
    forward(mine, q_ref, qq_ref, w_ref, m_ref, sums_ref, acc_ref, *scratch)


def forward_theirs(
    theirs, q_ref, qq_ref, m1_ref, sums1_ref, acc1_ref,
    out, w_ref, o_ref, share_ref,
    m_ref, sums_ref, acc_ref, stage, pieces, sem, *scratch
):
    forward(theirs, q_ref, qq_ref, w_ref, m_ref, sums_ref, acc_ref, *scratch)
    for t in range(q_ref.shape[0]):
        top = jnp.maximum(m1_ref[t], m_ref[t])
        f1 = jnp.exp2((m1_ref[t] - top) * EXP_SCALE)
        f2 = jnp.exp2((m_ref[t] - top) * EXP_SCALE)
        sums = sums1_ref[t] * f1 + sums_ref[t] * f2
        inverse = 1.0 / sums[0:1]
        s1, s2 = f1 * inverse, f2 * inverse
        share_ref[0, t] = s1
        share_ref[1, t] = s2
        both = acc1_ref[t] * s1 + acc_ref[t] * s2
        primal = both[0:HD]
        tangent = both[HD:] - (sums[1:2] * inverse) * primal
        o_ref[t, 0:HD, :] = primal.astype(BF).astype(F32)
        o_ref[t, HD:, :] = tangent.astype(BF).astype(F32)
        stage[QT * t : QT * t + QT, :] = o_ref[t].T
    for s in range(out.shape[0]):
        pieces[s] = stage[PIECE * s : PIECE * s + PIECE, :].astype(BF)
    copy = pltpu.make_async_copy(pieces, out, sem)
    copy.start()
    copy.wait()


def backward(keys, q_ref, cot_ref, inner_ref, w_ref, share_ref, side, dst, dq_ref, kt_ref, ds_ref, p_ref):
    tiles = q_ref.shape[0]
    per = SUB // KROWS
    subs = keys.shape[0] // per

    def some(i, carry):
        at = pl.ds(pl.multiple_of(SUB * i, SUB), SUB)
        slots = pl.ds(per * i, per)
        k = keys[slots, 0:KROWS, 0:HD].reshape(SUB, HD)
        v = keys[slots, KROWS : 2 * KROWS, 0:HD].reshape(SUB, HD)
        kt_ref[i] = k.astype(F32).T.astype(BF)
        for t in range(tiles):
            cols = slice(QT * t, QT * t + QT)
            p = w_ref[t, at, :].astype(F32) * share_ref[side, t]
            ds = p * (nt(v, cot_ref[cols, :]) - inner_ref[t])
            p_ref[:, cols] = p.astype(BF)
            ds_ref[i, :, cols] = ds.astype(BF)
        dk = nn(ds_ref[i], q_ref[...].reshape(tiles * QT, HD)) * INV
        dv = nn(p_ref[...], cot_ref[...])
        dst[slots, 0:KROWS, 0:HD] = dk.astype(BF).reshape(per, KROWS, HD)
        dst[slots, 0:KROWS, HD:] = dv.astype(BF).reshape(per, KROWS, HD)
        return carry

    lax.fori_loop(0, subs, some, 0)
    dq = dq_ref[...]
    for i in range(subs):
        dq = dq + nn(kt_ref[i], ds_ref[i])
    dq_ref[...] = dq


def backward_theirs(
    theirs, gaps, mask, q_ref, o_ref, w_ref, share_ref, dst, cot_ref, inner_ref, dq_ref, stage, *scratch
):
    for s in range(gaps.shape[0]):
        stage[PIECE * s : PIECE * s + 16, :] = gaps[s, :, 0:HD].astype(F32)
        stage[PIECE * s + 16 : PIECE * s + 24, :] = gaps[s, 0:8, HD:].astype(F32)
    for t in range(q_ref.shape[0]):
        rows = slice(QT * t, QT * t + QT)
        cot = (LOSS * (stage[rows, :].T + o_ref[t, HD:, :])) * mask[:, rows]
        cot = cot.astype(BF).astype(F32)
        inner_ref[t] = jnp.sum(cot * o_ref[t, 0:HD, :], axis=0, keepdims=True)
        cot_ref[rows, :] = cot.T.astype(BF)
    dq_ref[...] = jnp.zeros_like(dq_ref)
    backward(theirs, q_ref, cot_ref, inner_ref, w_ref, share_ref, 1, dst, dq_ref, *scratch)


def backward_mine(
    mine, q_ref, cot_ref, inner_ref, w_ref, share_ref, dq1_ref, out, dq_ref, stage, *scratch
):
    dq_ref[...] = dq1_ref[...]
    backward(mine, q_ref, cot_ref, inner_ref, w_ref, share_ref, 0, out, dq_ref, *scratch)
    stage[...] = (dq_ref[...] * INV).T
    for s in range(out.shape[0]):
        low = PIECE * s
        out[s, 64:80, 0:HD] = stage[low : low + 16, :].astype(BF)
        out[s, 64:72, HD:] = stage[low + 16 : low + 24, :].astype(BF)
        out[s, 72:80, HD:] = jnp.zeros((8, HD), BF)


def add_partner(mine, theirs, out, stage, sems):
    def fill(chip):
        stage[chip, 0:KROWS, :] = (
            mine[chip, 0:KROWS, :].astype(F32) + theirs[chip].astype(F32)
        ).astype(BF)
        stage[chip, KROWS:, :] = mine[chip, KROWS:, :]

    spread(out, stage, sems, fill)


def unpack_outs(r_ref, sent, kept, o_ref):
    heads = o_ref.shape[3] // HD
    for head in range(heads):
        cols = slice(head * HD, head * HD + HD)
        for eight in range(KROWS // 8):
            chip, low = PARTS * head + eight // 3, 8 * (eight % 3)
            row = 8 * eight
            for side in range(2):
                o_ref[row // 32, side, row % 32 : row % 32 + 8, cols] = r_ref[
                    chip, low : low + 8, side * HD : side * HD + HD
                ]
    sent[...] = o_ref[1 - group()]
    kept[...] = o_ref[group()]


def unpack_grads(r_ref, sent, kept, f_ref):
    half = f_ref.shape[3] // HD
    for head in range(2 * half):
        at, cols = head // half, slice((head % half) * HD, (head % half + 1) * HD)
        first = PARTS * head
        both = sum(r_ref[first + part, 0:KROWS, :].astype(F32) for part in range(PARTS))
        f_ref[at, 1, :, cols] = both[:, 0:HD].astype(BF)
        f_ref[at, 2, :, cols] = both[:, HD:].astype(BF)
        for eight in range(KROWS // 8):
            chip, low = first + eight // 3, 8 * (eight % 3)
            row = 8 * eight
            lanes = slice(0, HD) if low < 16 else slice(HD, 2 * HD)
            f_ref[at, 0, row : row + 8, cols] = r_ref[chip, 64 + low % 16 : 72 + low % 16, lanes]
    sent[...] = f_ref[1 - core()]
    kept[...] = f_ref[core()]


def finish_outs(kept, got, primal, tangent):
    wide = kept.shape[2]
    for side, ref in enumerate((primal, tangent)):
        for piece, who in ((kept, group()), (got, 1 - group())):
            ref[:, pl.ds(pl.multiple_of(wide * who, HD), wide)] = piece[side]


def finish_grads(kept, got, dq, dk, dv):
    for at, ref in enumerate((dq, dk, dv)):
        for half in range(2):
            rows = slice(32 * half, 32 * half + 32)
            for piece, who in ((kept, core()), (got, 1 - core())):
                low = pl.multiple_of(64 * half + 32 * who, 32)
                ref[pl.ds(low, 32), :] = piece[at, rows, :]


def shape(*dims, dtype=BF):
    return jax.ShapeDtypeStruct(dims, dtype)


SWAP = [(0, 1), (1, 0)]
BLOCK_AXES = ("zl", "y", "x")


def exchange(array):
    return lax.all_to_all(array, BLOCK_AXES, 0, 0, tiled=True)


def swap(array, axis):
    return lax.ppermute(array, axis, SWAP)


def out_stage(chips, rows):
    return (pltpu.VMEM((chips, rows, 2 * HD), BF), pltpu.SemaphoreType.DMA((4,)))


def attention(chips, mine, theirs, gaps, mask):
    length, tiles = chips * KROWS, chips * PIECE // QT
    rows = tiles * QT
    flops = 2 * length * rows * HD
    q, qq = shape(tiles, QT, HD), shape(tiles, QT, 2 * HD)
    w = shape(tiles, length, QT)
    stats, sums, acc = (shape(tiles, n, QT, dtype=F32) for n in (1, 2, 2 * HD))
    scratch = (
        pltpu.VMEM((length, QT), F32),
        pltpu.VMEM((length, QT), BF),
        pltpu.VMEM((length, 2 * HD), BF),
        pltpu.VMEM((2 * HD, length), BF),
    )
    stage = pltpu.VMEM((rows, 2 * HD), F32)
    q, qq, w1, m1, sums1, acc1 = call(
        forward_mine,
        [(one, VMEM) for one in (q, qq, w, stats, sums, acc)],
        [VMEM],
        24,
        (stage,) + scratch,
        6 * flops, length * rows, 7_000_000,
    )(mine)
    out, w2, o, share = call(
        forward_theirs,
        [
            (shape(chips, PIECE, 2 * HD), HBM),
            (w, VMEM), (acc, VMEM), (shape(2, tiles, 1, QT, dtype=F32), VMEM),
        ],
        [VMEM] * 6,
        28,
        (
            pltpu.VMEM(stats.shape, F32), pltpu.VMEM(sums.shape, F32), pltpu.VMEM(acc.shape, F32),
            stage, pltpu.VMEM((chips, PIECE, 2 * HD), BF), pltpu.SemaphoreType.DMA,
        ) + scratch,
        6 * flops, length * rows, 7_000_000,
    )(theirs, q, qq, m1, sums1, acc1)
    outs = exchange(out)
    subs = length // SUB
    scratch = (
        pltpu.VMEM((rows, HD), F32),
        pltpu.VMEM((subs, HD, SUB), BF),
        pltpu.VMEM((subs, SUB, rows), BF),
        pltpu.VMEM((SUB, rows), BF),
    )
    out_theirs, cot, inner, dq = call(
        backward_theirs,
        [
            (shape(chips, KROWS, 2 * HD), VMEM), (shape(rows, HD), VMEM),
            (stats, VMEM), (shape(HD, rows, dtype=F32), VMEM),
        ],
        [VMEM] * 7,
        24,
        scratch,
        8 * flops, 0, 7_000_000,
    )(theirs, gaps, mask, q, o, w2, share)
    partner = swap(out_theirs, "c")
    out = call(
        backward_mine,
        [(shape(chips, KROWS + 16, 2 * HD), VMEM)],
        [VMEM] * 7,
        24,
        (pltpu.VMEM((HD, rows), F32),) + scratch,
        8 * flops, 0, 7_000_000,
    )(mine, q, cot, inner, w1, share, dq)[0]
    back = call(
        add_partner, [(shape(chips, KROWS + 16, 2 * HD), HBM)], [VMEM] * 2, 8,
        out_stage(chips, KROWS + 16),
    )(out, partner)[0]
    return outs, exchange(back)


def per_device(q, k, v, tq, tk, tv, gap):
    chips = lax.axis_size(BLOCK_AXES)
    local, feat = q.shape
    wide = gap.shape[1] // 2
    piece, gpiece = shape(6, KROWS, feat), shape(32, wide)
    arrays = (q, k, v, tq, tk, tv, gap)
    sent, kept, gap_sent, gap_kept = call(
        split_tokens,
        [(piece, VMEM), (piece, VMEM), (gpiece, VMEM), (gpiece, VMEM)],
        [HBM] * 7,
        4,
        (pltpu.SemaphoreType.DMA((6, 2, 2)), pltpu.SemaphoreType.DMA((2,))),
    )(*(pltpu.with_memory_space_constraint(one, pltpu.HBM) for one in arrays))
    got = swap(sent, "c")
    packed = call(
        pack_heads,
        [(shape(chips, 152, 2 * HD), HBM)],
        [VMEM] * 2,
        8,
        (pltpu.VMEM((2,) + piece.shape, BF),) + out_stage(chips, 152),
    )(kept, got)[0]
    mine = exchange(packed)

    got_gap = swap(gap_sent, "zh")
    packed = call(
        pack_gaps,
        [(shape(chips, 16, 2 * HD), HBM)],
        [VMEM] * 2,
        4,
        (pltpu.VMEM((2,) + gpiece.shape, BF),) + out_stage(chips, 16),
    )(gap_kept, got_gap)[0]
    gaps = exchange(packed)
    theirs = swap(mine, "c")

    rows = chips * PIECE
    part = lax.axis_index(BLOCK_AXES) % PARTS
    short = (jnp.arange(rows) % PIECE >= KROWS - PIECE * (PARTS - 1)) & (part == PARTS - 1)
    mask = jnp.where(short, 0.0, 1.0).astype(F32)[None]
    outs, back = attention(chips, mine, theirs, gaps, mask)

    opiece, fpiece = shape(2, 32, wide), shape(3, KROWS, feat)
    sent, kept = call(
        unpack_outs, [(opiece, VMEM), (opiece, VMEM)], [VMEM], 4,
        (pltpu.VMEM((2,) + opiece.shape, BF),),
    )(outs)
    got = swap(sent, "zh")
    small, large = shape(32, 2 * wide), shape(local, feat)
    primal, tangent = call(finish_outs, [(small, VMEM), (small, VMEM)], [VMEM] * 2, 4)(kept, got)
    sent, kept = call(
        unpack_grads, [(fpiece, VMEM), (fpiece, VMEM)], [VMEM], 6,
        (pltpu.VMEM((2,) + fpiece.shape, BF),),
    )(back)
    got = swap(sent, "c")
    dq, dk, dv = call(finish_grads, [(large, VMEM)] * 3, [VMEM] * 2, 4)(kept, got)
    return primal, tangent, dq, dk, dv


def solution(mesh):
    sizes = (2, 4, 4, 2, 2)
    inner = Mesh(mesh.devices.reshape(sizes), BLOCK_AXES + ("zh", "c"))
    both = P(BLOCK_AXES, ("zh", "c"))
    rows = P(BLOCK_AXES + ("zh", "c"), None)

    return jax.shard_map(
        per_device,
        mesh=inner,
        in_specs=(both,) * 6 + (rows,),
        out_specs=(rows, rows, both, both, both),
        check_vma=False,
    )
```

```python
import math

import jax
import jax.numpy as jnp
from jax import lax
from jax.experimental import pallas as pl
from jax.experimental.pallas import tpu as pltpu
from jax.sharding import Mesh, PartitionSpec as P


BF = jnp.bfloat16
F32 = jnp.float32
HD = 128
LOSS = 64.0
PARTS = 3
PIECE = 24
EIGHTS = ((0, 1, 4), (2, 5, None), (3, 6, 7))
KROWS = 64
QT = 256
SUB = 512
INV = 1.0 / math.sqrt(HD)
EXP_SCALE = INV * math.log2(math.e)
VMEM = pl.BlockSpec(memory_space=pltpu.VMEM)
HBM = pl.BlockSpec(memory_space=pltpu.HBM)
ANY = pl.BlockSpec(memory_space=pl.ANY)


def call(body, outs, ins, limit, scratch=(), flops=0, exps=0, moved=1_000_000):
    return pl.pallas_call(
        body,
        out_shape=[
            pltpu.HBM(one.shape, one.dtype) if place is HBM else one for one, place in outs
        ],
        in_specs=ins,
        out_specs=[place for _, place in outs],
        scratch_shapes=list(scratch),
        compiler_params=pltpu.CompilerParams(vmem_limit_bytes=limit * 1024 * 1024),
        cost_estimate=pl.CostEstimate(flops=flops, bytes_accessed=moved, transcendentals=exps),
    )


def nt(a, b):
    return lax.dot_general(a, b, (((1,), (1,)), ((), ())), preferred_element_type=F32)


def nn(a, b):
    return lax.dot_general(a, b, (((1,), (0,)), ((), ())), preferred_element_type=F32)


def core():
    return lax.axis_index("c")


def group():
    return lax.axis_index("zh")


def split_tokens(*refs):
    *arrays, gap, sent, kept, gap_here, sems, gap_sem = refs
    copies = []
    for at, ref in enumerate(arrays):
        for half in range(2):
            for side, (dst, who) in enumerate(((sent, 1 - core()), (kept, core()))):
                low = pl.multiple_of(64 * half + 32 * who, 32)
                copies.append(
                    pltpu.make_async_copy(
                        ref.at[pl.ds(low, 32), :],
                        dst.at[at, 32 * half : 32 * half + 32, :],
                        sems.at[at, half, side],
                    )
                )
    copies.append(pltpu.make_async_copy(gap, gap_here, gap_sem))
    for copy in copies:
        copy.start()
    for copy in copies:
        copy.wait()


def pack_heads(kept, got, gap, out, e_ref):
    e_ref[core()] = kept[...]
    e_ref[1 - core()] = got[...]
    half = e_ref.shape[3] // HD
    zero = jnp.zeros((8, HD), BF)
    for chip in range(out.shape[0]):
        head, part = chip // PARTS, chip % PARTS
        if head >= 2 * half:
            out[chip] = jnp.zeros(out.shape[1:], BF)
            continue
        at, cols = head // half, slice((head % half) * HD, (head % half + 1) * HD)
        out[chip, 0:64, 0:HD] = e_ref[at, 1, :, cols]
        out[chip, 0:64, HD:] = e_ref[at, 4, :, cols]
        out[chip, 64:128, 0:HD] = e_ref[at, 2, :, cols]
        out[chip, 64:128, HD:] = e_ref[at, 5, :, cols]
        for to, eight in enumerate(EIGHTS[part]):
            rows = slice(128 + 8 * to, 136 + 8 * to)
            for side, array in ((0, 0), (1, 3)):
                lanes = slice(side * HD, side * HD + HD)
                if eight is None:
                    out[chip, rows, lanes] = zero
                else:
                    out[chip, rows, lanes] = e_ref[at, array, 8 * eight : 8 * eight + 8, cols]
    for mine in range(2):

        @pl.when(group() == mine)
        def _():
            for chip in range(2 * half * PARTS):
                head, part = chip // PARTS, chip % PARTS
                for place in range(2):
                    eight = EIGHTS[part][mine + place]
                    rows = slice(152 + 8 * place, 160 + 8 * place)
                    for other in range(2):
                        lanes = slice(other * HD, other * HD + HD)
                        low = (2 * half * other + head) * HD
                        if eight is None or eight // 4 != mine:
                            out[chip, rows, lanes] = zero
                        else:
                            at = 8 * (eight % 4)
                            out[chip, rows, lanes] = gap[at : at + 8, low : low + HD]


def split_gaps(mine, sent, kept, sems):
    copies = []
    for at, (dst, who) in enumerate(((sent, 1 - group()), (kept, group()))):
        lanes = pl.ds(pl.multiple_of(who * HD, HD), HD)
        copies.append(pltpu.make_async_copy(mine.at[:, 152:168, lanes], dst, sems.at[at]))
    for copy in copies:
        copy.start()
    for copy in copies:
        copy.wait()


def fold(x, op):
    return op(x.reshape(x.shape[0] // 8, 8, x.shape[1]), axis=0)


def forward(keys, q_ref, qq_ref, w_ref, m_ref, sums_ref, acc_ref, s_ref, wt_ref, kk_ref, vt_ref,
            ready=None, done=None):
    tiles = q_ref.shape[0]
    per = SUB // KROWS
    subs = kk_ref.shape[0] // SUB
    ats = [slice(SUB * i, SUB * i + SUB) for i in range(subs)]

    def scores(t, i, peak):
        s = nt(kk_ref[ats[i], 0:HD], q_ref[t])
        s_ref[t % 2, ats[i], :] = s
        return jnp.maximum(peak, fold(s, jnp.max))

    def values(t, i):
        both = nn(vt_ref[:, ats[i]], w_ref[t, ats[i], :])
        tan = nn(vt_ref[0:HD, ats[i]], wt_ref[t % 2, ats[i], :]) * INV
        if i == 0:
            acc_ref[t, 0:HD, :] = both[0:HD]
            acc_ref[t, HD:, :] = both[HD:] + tan
        else:
            acc_ref[t, 0:HD, :] += both[0:HD]
            acc_ref[t, HD:, :] += both[HD:] + tan

    lowest = jnp.full((8, QT), -jnp.inf, F32)
    peak = lowest
    for i in range(subs):
        if ready is not None:
            ready(i)
        slots = slice(per * i, per * i + per)
        kk_ref[ats[i], :] = keys[slots, 0:KROWS, :].reshape(SUB, 2 * HD)
        v = keys[slots, KROWS : 2 * KROWS, :].reshape(SUB, 2 * HD)
        vt_ref[:, ats[i]] = v.astype(F32).T.astype(BF)
        peak = scores(0, i, peak)
    for t in range(tiles):
        top = jnp.max(peak, axis=0, keepdims=True)
        m_ref[t] = top
        peak = lowest
        total = jnp.zeros((8, QT), F32)
        tan_total = jnp.zeros((8, QT), F32)
        for i in range(subs):
            w = jnp.exp2((s_ref[t % 2, ats[i], :] - top) * EXP_SCALE)
            wt = w * nt(kk_ref[ats[i], :], qq_ref[t])
            total = total + fold(w, jnp.sum)
            tan_total = tan_total + fold(wt, jnp.sum)
            w_ref[t, ats[i], :] = w.astype(BF)
            wt_ref[t % 2, ats[i], :] = wt.astype(BF)
            if t + 1 < tiles:
                peak = scores(t + 1, i, peak)
            if t > 0:
                values(t - 1, i)
        sums_ref[t, 0:1, :] = jnp.sum(total, axis=0, keepdims=True)
        sums_ref[t, 1:2, :] = jnp.sum(tan_total, axis=0, keepdims=True) * INV
        if done is not None:
            done(t)
    for i in range(subs):
        values(tiles - 1, i)


def forward_mine(mine, q_ref, qq_ref, w_hbm, m_ref, sums_ref, acc_ref, stage, w_ref, sems, *scratch):
    for s in range(mine.shape[0]):
        stage[PIECE * s : PIECE * s + PIECE, :] = mine[s, 128:152, :].astype(F32)
    tiles = q_ref.shape[0]
    for t in range(tiles):
        rows = slice(QT * t, QT * t + QT)
        q_ref[t] = stage[rows, 0:HD].astype(BF)
        qq_ref[t, :, 0:HD] = stage[rows, HD:].astype(BF)
        qq_ref[t, :, HD:] = stage[rows, 0:HD].astype(BF)
    copies = [pltpu.make_async_copy(w_ref.at[t], w_hbm.at[t], sems.at[t]) for t in range(tiles)]
    forward(
        mine, q_ref, qq_ref, w_ref, m_ref, sums_ref, acc_ref, *scratch,
        done=lambda t: copies[t].start(),
    )
    for copy in copies:
        copy.wait()


def backward(keys, q_ref, cot_ref, inner_ref, w_ref, share_ref, side, dst, dq, kt_ref, ds_ref, p_ref,
             ready=None):
    tiles = q_ref.shape[0]
    per = SUB // KROWS
    subs = ds_ref.shape[0]
    q_all = q_ref[...].reshape(tiles * QT, HD)
    for i in range(subs):
        if ready is not None:
            ready(i)
        at, slots = slice(SUB * i, SUB * i + SUB), slice(per * i, per * i + per)
        k = keys[slots, 0:KROWS, 0:HD].reshape(SUB, HD)
        v = keys[slots, KROWS : 2 * KROWS, 0:HD].reshape(SUB, HD)
        kt_ref[i] = k.astype(F32).T.astype(BF)
        for t in range(tiles):
            cols = slice(QT * t, QT * t + QT)
            p = w_ref[t, at, :].astype(F32) * share_ref[side, t]
            ds = p * (nt(v, cot_ref[cols, :]) - inner_ref[t])
            p_ref[:, cols] = p.astype(BF)
            ds_ref[i, :, cols] = ds.astype(BF)
        dk = nn(ds_ref[i], q_all) * INV
        dv = nn(p_ref[...], cot_ref[...])
        dst[slots, 0:KROWS, 0:HD] = dk.astype(BF).reshape(per, KROWS, HD)
        dst[slots, 0:KROWS, HD:] = dv.astype(BF).reshape(per, KROWS, HD)
    for i in range(subs):
        dq = dq + nn(kt_ref[i], ds_ref[i])
    return dq


def theirs_both_ways(
    theirs_hbm, q_ref, qq_ref, m1_ref, sums1_ref, acc1_ref, gap_kept, gap_got, mask,
    dst, pieces, cot_ref, inner_ref, dq_ref, share_ref,
    theirs, sems, w_ref, m_ref, sums_ref, acc_ref, g_ref, stage, kt_ref, ds_ref, p_ref, *scratch
):
    per = SUB // KROWS
    copies = [
        pltpu.make_async_copy(
            theirs_hbm.at[per * i : per * i + per, 0:128, :],
            theirs.at[per * i : per * i + per],
            sems.at[i],
        )
        for i in range(ds_ref.shape[0])
    ]
    for copy in copies:
        copy.start()
    forward(
        theirs, q_ref, qq_ref, w_ref, m_ref, sums_ref, acc_ref, *scratch,
        ready=lambda i: copies[i].wait(),
    )
    g_ref[group()] = gap_kept[...]
    g_ref[1 - group()] = gap_got[...]
    for s in range(gap_kept.shape[0]):
        low = PIECE * s
        first, second = g_ref[0, s].astype(F32), g_ref[1, s].astype(F32)
        stage[low : low + 8, 0:HD] = first[0:8]
        stage[low + 8 : low + 16, 0:HD] = first[8:16] + second[0:8]
        stage[low + 16 : low + 24, 0:HD] = second[8:16]
    for t in range(q_ref.shape[0]):
        rows = slice(QT * t, QT * t + QT)
        top = jnp.maximum(m1_ref[t], m_ref[t])
        f1 = jnp.exp2((m1_ref[t] - top) * EXP_SCALE)
        f2 = jnp.exp2((m_ref[t] - top) * EXP_SCALE)
        sums = sums1_ref[t] * f1 + sums_ref[t] * f2
        inverse = 1.0 / sums[0:1]
        s1, s2 = f1 * inverse, f2 * inverse
        share_ref[0, t] = s1
        share_ref[1, t] = s2
        both = acc1_ref[t] * s1 + acc_ref[t] * s2
        tangent = both[HD:] - (sums[1:2] * inverse) * both[0:HD]
        primal = both[0:HD].astype(BF).astype(F32)
        tangent = tangent.astype(BF).astype(F32)
        cot = (LOSS * (stage[rows, 0:HD].T + tangent)) * mask[:, rows]
        cot = cot.astype(BF).astype(F32)
        inner_ref[t] = jnp.sum(cot * primal, axis=0, keepdims=True)
        cot_ref[rows, :] = cot.T.astype(BF)
        stage[rows, 0:HD] = primal.T
        stage[rows, HD:] = tangent.T
    for s in range(pieces.shape[0]):
        pieces[s] = stage[PIECE * s : PIECE * s + PIECE, :].astype(BF)
    dq_ref[...] = backward(
        theirs, q_ref, cot_ref, inner_ref, w_ref, share_ref, 1, dst, jnp.zeros(dq_ref.shape, F32),
        kt_ref, ds_ref, p_ref,
    )


def backward_mine(
    mine, q_ref, cot_ref, inner_ref, w_hbm, share_ref, dq_ref, out, w_ref, sems, stage, *scratch
):
    ats = [slice(SUB * i, SUB * i + SUB) for i in range(w_ref.shape[1] // SUB)]
    copies = [
        pltpu.make_async_copy(w_hbm.at[:, at, :], w_ref.at[:, at, :], sems.at[i])
        for i, at in enumerate(ats)
    ]
    for copy in copies:
        copy.start()
    dq = backward(
        mine, q_ref, cot_ref, inner_ref, w_ref, share_ref, 0, out, dq_ref[...], *scratch,
        ready=lambda i: copies[i].wait(),
    )
    stage[...] = (dq * INV).T
    for s in range(out.shape[0]):
        low = PIECE * s
        out[s, 64:80, 0:HD] = stage[low : low + 16, :].astype(BF)
        out[s, 64:72, HD:] = stage[low + 16 : low + 24, :].astype(BF)
        out[s, 72:80, HD:] = jnp.zeros((8, HD), BF)


def gather_out(mine, pieces, theirs, out):
    for s in range(out.shape[0]):
        out[s, 0:KROWS, :] = (
            mine[s, 0:KROWS, :].astype(F32) + theirs[s].astype(F32)
        ).astype(BF)
        out[s, 64:88, :] = pieces[s]
        out[s, 88:104, :] = mine[s, 64:80, :]


def unpack_heads(r_ref, sent, kept, o_sent, o_kept, f_ref, o_ref):
    half = f_ref.shape[3] // HD
    for head in range(2 * half):
        at, cols = head // half, slice((head % half) * HD, (head % half + 1) * HD)
        first = PARTS * head
        both = sum(r_ref[first + part, 0:KROWS, :].astype(F32) for part in range(PARTS))
        f_ref[at, 1, :, cols] = both[:, 0:HD].astype(BF)
        f_ref[at, 2, :, cols] = both[:, HD:].astype(BF)
        ocols = slice(head * HD, head * HD + HD)
        for part in range(PARTS):
            for place, eight in enumerate(EIGHTS[part]):
                if eight is None:
                    continue
                row, low = 8 * eight, 8 * place
                lanes = slice(0, HD) if place < 2 else slice(HD, 2 * HD)
                from_row = 88 + low % 16
                f_ref[at, 0, row : row + 8, cols] = r_ref[first + part, from_row : from_row + 8, lanes]
                for side in range(2):
                    o_ref[row // 32, side, row % 32 : row % 32 + 8, ocols] = r_ref[
                        first + part, 64 + low : 72 + low, side * HD : side * HD + HD
                    ]
    sent[...] = f_ref[1 - core()]
    kept[...] = f_ref[core()]
    o_sent[...] = o_ref[1 - group()]
    o_kept[...] = o_ref[group()]


def finish(kept, got, o_kept, o_got, primal, tangent, dq, dk, dv):
    for at, ref in enumerate((dq, dk, dv)):
        for half in range(2):
            rows = slice(32 * half, 32 * half + 32)
            for piece, who in ((kept, core()), (got, 1 - core())):
                low = pl.multiple_of(64 * half + 32 * who, 32)
                ref[pl.ds(low, 32), :] = piece[at, rows, :]
    wide = o_kept.shape[2]
    for side, ref in enumerate((primal, tangent)):
        for piece, who in ((o_kept, group()), (o_got, 1 - group())):
            ref[:, pl.ds(pl.multiple_of(wide * who, HD), wide)] = piece[side]


def shape(*dims, dtype=BF):
    return jax.ShapeDtypeStruct(dims, dtype)


SWAP = [(0, 1), (1, 0)]
BLOCK_AXES = ("zl", "y", "x")


def exchange(array):
    return lax.all_to_all(array, BLOCK_AXES, 0, 0, tiled=True)


def swap(array, axis):
    return lax.ppermute(array, axis, SWAP)


def attention(chips, mine, mask):
    length, tiles = chips * KROWS, chips * PIECE // QT
    rows, subs = tiles * QT, length // SUB
    flops = 2 * length * rows * HD
    gpiece = shape(chips, 16, HD)
    gap_sent, gap_kept = call(
        split_gaps, [(gpiece, VMEM), (gpiece, VMEM)], [ANY], 2, (pltpu.SemaphoreType.DMA((2,)),),
        moved=500_000,
    )(mine)
    gap_got = swap(gap_sent, "zh")
    theirs = swap(mine, "c")
    q, qq = shape(tiles, QT, HD), shape(tiles, QT, 2 * HD)
    w = shape(tiles, length, QT)
    stats, sums, acc = (shape(tiles, n, QT, dtype=F32) for n in (1, 2, 2 * HD))
    tiles_of = (pltpu.VMEM(w.shape, BF), pltpu.SemaphoreType.DMA((tiles,)))
    scratch = (
        pltpu.VMEM((2, length, QT), F32),
        pltpu.VMEM((2, length, QT), BF),
        pltpu.VMEM((length, 2 * HD), BF),
        pltpu.VMEM((2 * HD, length), BF),
    )
    back_scratch = (
        pltpu.VMEM((subs, HD, SUB), BF),
        pltpu.VMEM((subs, SUB, rows), BF),
        pltpu.VMEM((SUB, rows), BF),
    )
    stage = pltpu.VMEM((rows, 2 * HD), F32)
    q, qq, w1, m1, sums1, acc1 = call(
        forward_mine,
        [(q, VMEM), (qq, VMEM), (w, HBM), (stats, VMEM), (sums, VMEM), (acc, VMEM)],
        [VMEM],
        30,
        (stage,) + tiles_of + scratch,
        6 * flops, length * rows, 7_000_000,
    )(mine)
    key_piece = shape(chips, KROWS, 2 * HD)
    dst, pieces, cot, inner, dq, share = call(
        theirs_both_ways,
        [
            (key_piece, VMEM), (shape(chips, PIECE, 2 * HD), VMEM), (shape(rows, HD), VMEM),
            (stats, VMEM), (shape(HD, rows, dtype=F32), VMEM),
            (shape(2, tiles, 1, QT, dtype=F32), VMEM),
        ],
        [ANY] + [VMEM] * 8,
        30,
        (
            pltpu.VMEM((chips, 2 * KROWS, 2 * HD), BF), pltpu.SemaphoreType.DMA((subs,)),
            pltpu.VMEM(w.shape, BF), pltpu.VMEM(stats.shape, F32), pltpu.VMEM(sums.shape, F32),
            pltpu.VMEM(acc.shape, F32), pltpu.VMEM((2,) + gpiece.shape, BF), stage,
        ) + back_scratch + scratch,
        14 * flops, length * rows, 7_000_000,
    )(theirs, q, qq, m1, sums1, acc1, gap_kept, gap_got, mask)
    partner = swap(dst, "c")
    out = call(
        backward_mine,
        [(shape(chips, KROWS + 16, 2 * HD), VMEM)],
        [VMEM] * 4 + [HBM] + [VMEM] * 2,
        30,
        (
            pltpu.VMEM(w.shape, BF), pltpu.SemaphoreType.DMA((subs,)), pltpu.VMEM((rows, HD), F32),
        ) + back_scratch,
        8 * flops, 0, 7_000_000,
    )(mine, q, cot, inner, w1, share, dq)[0]
    return call(gather_out, [(shape(chips, 104, 2 * HD), VMEM)], [VMEM] * 3, 8)(out, pieces, partner)[0]


def per_device(q, k, v, tq, tk, tv, gap):
    chips = lax.axis_size(BLOCK_AXES)
    local, feat = q.shape
    wide = gap.shape[1] // 2
    piece = shape(6, KROWS, feat)
    arrays = (q, k, v, tq, tk, tv, gap)
    sent, kept, gap_here = call(
        split_tokens,
        [(piece, VMEM), (piece, VMEM), (shape(*gap.shape), VMEM)],
        [HBM] * 7,
        4,
        (pltpu.SemaphoreType.DMA((6, 2, 2)), pltpu.SemaphoreType.DMA),
    )(*(pltpu.with_memory_space_constraint(one, pltpu.HBM) for one in arrays))
    got = swap(sent, "c")
    packed = call(
        pack_heads,
        [(shape(chips, 168, 2 * HD), VMEM)],
        [VMEM] * 3,
        8,
        (pltpu.VMEM((2,) + piece.shape, BF),),
    )(kept, got, gap_here)[0]
    mine = exchange(packed)

    rows = chips * PIECE
    part = lax.axis_index(BLOCK_AXES) % PARTS
    short = (jnp.arange(rows) % PIECE >= 16) & (part == 1)
    mask = jnp.where(short, 0.0, 1.0).astype(F32)[None]
    back = exchange(attention(chips, mine, mask))

    opiece, fpiece = shape(2, 32, wide), shape(3, KROWS, feat)
    sent, kept, o_sent, o_kept = call(
        unpack_heads,
        [(fpiece, VMEM), (fpiece, VMEM), (opiece, VMEM), (opiece, VMEM)],
        [VMEM],
        8,
        (pltpu.VMEM((2,) + fpiece.shape, BF), pltpu.VMEM((2,) + opiece.shape, BF)),
    )(back)
    o_got = swap(o_sent, "zh")
    got = swap(sent, "c")
    small, large = shape(32, 2 * wide), shape(local, feat)
    return tuple(
        call(finish, [(small, VMEM)] * 2 + [(large, VMEM)] * 3, [VMEM] * 4, 8)(
            kept, got, o_kept, o_got
        )
    )


def solution(mesh):
    sizes = (2, 4, 4, 2, 2)
    inner = Mesh(mesh.devices.reshape(sizes), BLOCK_AXES + ("zh", "c"))
    both = P(BLOCK_AXES, ("zh", "c"))
    rows = P(BLOCK_AXES + ("zh", "c"), None)

    return jax.shard_map(
        per_device,
        mesh=inner,
        in_specs=(both,) * 6 + (rows,),
        out_specs=(rows, rows, both, both, both),
        check_vma=False,
    )
```

```python
import math

import jax
import jax.numpy as jnp
from jax import lax
from jax.experimental import pallas as pl
from jax.experimental.pallas import tpu as pltpu
from jax.sharding import Mesh, PartitionSpec as P


BF = jnp.bfloat16
F32 = jnp.float32
HD = 128
LOSS = 64.0
PARTS = 3
PIECE = 24
EIGHTS = ((0, 1, 4), (2, 5, None), (3, 6, 7))
KROWS = 64
QT = 256
SUB = 512
INV = 1.0 / math.sqrt(HD)
EXP_SCALE = INV * math.log2(math.e)
VMEM = pl.BlockSpec(memory_space=pltpu.VMEM)
HBM = pl.BlockSpec(memory_space=pltpu.HBM)
ANY = pl.BlockSpec(memory_space=pl.ANY)


def call(body, outs, ins, limit, scratch=(), flops=0, exps=0, moved=1_000_000):
    return pl.pallas_call(
        body,
        out_shape=[
            pltpu.HBM(one.shape, one.dtype) if place is HBM else one for one, place in outs
        ],
        in_specs=ins,
        out_specs=[place for _, place in outs],
        scratch_shapes=list(scratch),
        compiler_params=pltpu.CompilerParams(vmem_limit_bytes=limit * 1024 * 1024),
        cost_estimate=pl.CostEstimate(flops=flops, bytes_accessed=moved, transcendentals=exps),
    )


def nt(a, b):
    return lax.dot_general(a, b, (((1,), (1,)), ((), ())), preferred_element_type=F32)


def nn(a, b):
    return lax.dot_general(a, b, (((1,), (0,)), ((), ())), preferred_element_type=F32)


def core():
    return lax.axis_index("c")


def group():
    return lax.axis_index("zh")


def split_tokens(*refs):
    *arrays, gap, sent, kept, gap_here, sems, gap_sem = refs
    copies = []
    for at, ref in enumerate(arrays):
        for half in range(2):
            for side, (dst, who) in enumerate(((sent, 1 - core()), (kept, core()))):
                low = pl.multiple_of(64 * half + 32 * who, 32)
                copies.append(
                    pltpu.make_async_copy(
                        ref.at[pl.ds(low, 32), :],
                        dst.at[at, 32 * half : 32 * half + 32, :],
                        sems.at[at, half, side],
                    )
                )
    copies.append(pltpu.make_async_copy(gap, gap_here, gap_sem))
    for copy in copies:
        copy.start()
    for copy in copies:
        copy.wait()


def pack_heads(kept, got, gap, out, e_ref):
    e_ref[core()] = kept[...]
    e_ref[1 - core()] = got[...]
    half = e_ref.shape[3] // HD
    zero = jnp.zeros((8, HD), BF)
    for chip in range(out.shape[0]):
        head, part = chip // PARTS, chip % PARTS
        if head >= 2 * half:
            out[chip] = jnp.zeros(out.shape[1:], BF)
            continue
        at, cols = head // half, slice((head % half) * HD, (head % half + 1) * HD)
        out[chip, 0:64, 0:HD] = e_ref[at, 1, :, cols]
        out[chip, 0:64, HD:] = e_ref[at, 4, :, cols]
        out[chip, 64:128, 0:HD] = e_ref[at, 2, :, cols]
        out[chip, 64:128, HD:] = e_ref[at, 5, :, cols]
        for to, eight in enumerate(EIGHTS[part]):
            rows = slice(128 + 8 * to, 136 + 8 * to)
            for side, array in ((0, 0), (1, 3)):
                lanes = slice(side * HD, side * HD + HD)
                if eight is None:
                    out[chip, rows, lanes] = zero
                else:
                    out[chip, rows, lanes] = e_ref[at, array, 8 * eight : 8 * eight + 8, cols]
    for mine in range(2):

        @pl.when(group() == mine)
        def _():
            for chip in range(2 * half * PARTS):
                head, part = chip // PARTS, chip % PARTS
                for place in range(2):
                    eight = EIGHTS[part][mine + place]
                    rows = slice(152 + 8 * place, 160 + 8 * place)
                    for other in range(2):
                        lanes = slice(other * HD, other * HD + HD)
                        low = (2 * half * other + head) * HD
                        if eight is None or eight // 4 != mine:
                            out[chip, rows, lanes] = zero
                        else:
                            at = 8 * (eight % 4)
                            out[chip, rows, lanes] = gap[at : at + 8, low : low + HD]


def split_gaps(mine, sent, kept, sems):
    copies = []
    for at, (dst, who) in enumerate(((sent, 1 - group()), (kept, group()))):
        lanes = pl.ds(pl.multiple_of(who * HD, HD), HD)
        copies.append(pltpu.make_async_copy(mine.at[:, 152:168, lanes], dst, sems.at[at]))
    for copy in copies:
        copy.start()
    for copy in copies:
        copy.wait()


def fold(x, op):
    return op(x.reshape(x.shape[0] // 8, 8, x.shape[1]), axis=0)


def forward(keys, q_ref, qq_ref, w_ref, m_ref, sums_ref, acc_ref, s_ref, wt_ref, kk_ref, vt_ref,
            ready=None, done=None):
    tiles = q_ref.shape[0]
    per = SUB // KROWS
    subs = kk_ref.shape[0] // SUB
    ats = [slice(SUB * i, SUB * i + SUB) for i in range(subs)]

    def scores(t, i, peak):
        s = nt(kk_ref[ats[i], 0:HD], q_ref[t])
        s_ref[t % 2, ats[i], :] = s
        return jnp.maximum(peak, fold(s, jnp.max))

    def values(t, i):
        both = nn(vt_ref[:, ats[i]], w_ref[t, ats[i], :])
        tan = nn(vt_ref[0:HD, ats[i]], wt_ref[t % 2, ats[i], :]) * INV
        if i == 0:
            acc_ref[t, 0:HD, :] = both[0:HD]
            acc_ref[t, HD:, :] = both[HD:] + tan
        else:
            acc_ref[t, 0:HD, :] += both[0:HD]
            acc_ref[t, HD:, :] += both[HD:] + tan

    lowest = jnp.full((8, QT), -jnp.inf, F32)
    peak = lowest
    for i in range(subs):
        if ready is not None:
            ready(i)
        slots = slice(per * i, per * i + per)
        kk_ref[ats[i], :] = keys[slots, 0:KROWS, :].reshape(SUB, 2 * HD)
        v = keys[slots, KROWS : 2 * KROWS, :].reshape(SUB, 2 * HD)
        vt_ref[:, ats[i]] = v.astype(F32).T.astype(BF)
        peak = scores(0, i, peak)
    for t in range(tiles):
        top = jnp.max(peak, axis=0, keepdims=True)
        m_ref[t] = top
        peak = lowest
        total = jnp.zeros((8, QT), F32)
        tan_total = jnp.zeros((8, QT), F32)
        for i in range(subs):
            w = jnp.exp2((s_ref[t % 2, ats[i], :] - top) * EXP_SCALE)
            wt = w * nt(kk_ref[ats[i], :], qq_ref[t])
            total = total + fold(w, jnp.sum)
            tan_total = tan_total + fold(wt, jnp.sum)
            w_ref[t, ats[i], :] = w.astype(BF)
            wt_ref[t % 2, ats[i], :] = wt.astype(BF)
            if t + 1 < tiles:
                peak = scores(t + 1, i, peak)
            if t > 0:
                values(t - 1, i)
        sums_ref[t, 0:1, :] = jnp.sum(total, axis=0, keepdims=True)
        sums_ref[t, 1:2, :] = jnp.sum(tan_total, axis=0, keepdims=True) * INV
        if done is not None:
            done(t)
    for i in range(subs):
        values(tiles - 1, i)


def forward_mine(mine, q_ref, qq_ref, w_hbm, m_ref, sums_ref, acc_ref, stage, w_ref, sems, *scratch):
    for s in range(mine.shape[0]):
        stage[PIECE * s : PIECE * s + PIECE, :] = mine[s, 128:152, :].astype(F32)
    tiles = q_ref.shape[0]
    for t in range(tiles):
        rows = slice(QT * t, QT * t + QT)
        q_ref[t] = stage[rows, 0:HD].astype(BF)
        qq_ref[t, :, 0:HD] = stage[rows, HD:].astype(BF)
        qq_ref[t, :, HD:] = stage[rows, 0:HD].astype(BF)
    copies = [pltpu.make_async_copy(w_ref.at[t], w_hbm.at[t], sems.at[t]) for t in range(tiles)]
    forward(
        mine, q_ref, qq_ref, w_ref, m_ref, sums_ref, acc_ref, *scratch,
        done=lambda t: copies[t].start(),
    )
    for copy in copies:
        copy.wait()


def backward(keys, q_ref, cot_ref, inner_ref, w_ref, share_ref, side, dst, dq, kt_ref, ds_ref, p_ref,
             ready=None):
    tiles = q_ref.shape[0]
    per = SUB // KROWS
    subs = ds_ref.shape[0]
    q_all = q_ref[...].reshape(tiles * QT, HD)
    for i in range(subs):
        if ready is not None:
            ready(i)
        at, slots = slice(SUB * i, SUB * i + SUB), slice(per * i, per * i + per)
        k = keys[slots, 0:KROWS, 0:HD].reshape(SUB, HD)
        v = keys[slots, KROWS : 2 * KROWS, 0:HD].reshape(SUB, HD)
        kt_ref[i] = k.astype(F32).T.astype(BF)
        for t in range(tiles):
            cols = slice(QT * t, QT * t + QT)
            p = w_ref[t, at, :].astype(F32) * share_ref[side, t]
            ds = p * (nt(v, cot_ref[cols, :]) - inner_ref[t])
            p_ref[:, cols] = p.astype(BF)
            ds_ref[i, :, cols] = ds.astype(BF)
        dk = nn(ds_ref[i], q_all) * INV
        dv = nn(p_ref[...], cot_ref[...])
        dst[slots, 0:KROWS, 0:HD] = dk.astype(BF).reshape(per, KROWS, HD)
        dst[slots, 0:KROWS, HD:] = dv.astype(BF).reshape(per, KROWS, HD)
    for i in range(subs):
        dq = dq + nn(kt_ref[i], ds_ref[i])
    return dq


def theirs_both_ways(
    theirs_hbm, q_ref, qq_ref, m1_ref, sums1_ref, acc1_ref, gap_kept, gap_got, mask,
    dst, pieces, cot_ref, inner_ref, dq_ref, share_ref,
    theirs, sems, w_ref, m_ref, sums_ref, acc_ref, g_ref, stage, kt_ref, ds_ref, p_ref, *scratch
):
    per = SUB // KROWS
    copies = [
        pltpu.make_async_copy(
            theirs_hbm.at[per * i : per * i + per, 0:128, :],
            theirs.at[per * i : per * i + per],
            sems.at[i],
        )
        for i in range(ds_ref.shape[0])
    ]
    for copy in copies:
        copy.start()
    forward(
        theirs, q_ref, qq_ref, w_ref, m_ref, sums_ref, acc_ref, *scratch,
        ready=lambda i: copies[i].wait(),
    )
    g_ref[group()] = gap_kept[...]
    g_ref[1 - group()] = gap_got[...]
    for s in range(gap_kept.shape[0]):
        low = PIECE * s
        first, second = g_ref[0, s].astype(F32), g_ref[1, s].astype(F32)
        stage[low : low + 8, 0:HD] = first[0:8]
        stage[low + 8 : low + 16, 0:HD] = first[8:16] + second[0:8]
        stage[low + 16 : low + 24, 0:HD] = second[8:16]
    for t in range(q_ref.shape[0]):
        rows = slice(QT * t, QT * t + QT)
        top = jnp.maximum(m1_ref[t], m_ref[t])
        f1 = jnp.exp2((m1_ref[t] - top) * EXP_SCALE)
        f2 = jnp.exp2((m_ref[t] - top) * EXP_SCALE)
        sums = sums1_ref[t] * f1 + sums_ref[t] * f2
        inverse = 1.0 / sums[0:1]
        s1, s2 = f1 * inverse, f2 * inverse
        share_ref[0, t] = s1
        share_ref[1, t] = s2
        both = acc1_ref[t] * s1 + acc_ref[t] * s2
        tangent = both[HD:] - (sums[1:2] * inverse) * both[0:HD]
        primal = both[0:HD].astype(BF).astype(F32)
        tangent = tangent.astype(BF).astype(F32)
        cot = (LOSS * (stage[rows, 0:HD].T + tangent)) * mask[:, rows]
        cot = cot.astype(BF).astype(F32)
        inner_ref[t] = jnp.sum(cot * primal, axis=0, keepdims=True)
        cot_ref[rows, :] = cot.T.astype(BF)
        stage[rows, 0:HD] = primal.T
        stage[rows, HD:] = tangent.T
    for s in range(pieces.shape[0]):
        pieces[s] = stage[PIECE * s : PIECE * s + PIECE, :].astype(BF)
    dq_ref[...] = backward(
        theirs, q_ref, cot_ref, inner_ref, w_ref, share_ref, 1, dst, jnp.zeros(dq_ref.shape, F32),
        kt_ref, ds_ref, p_ref,
    )


def backward_mine(
    mine, q_ref, cot_ref, inner_ref, w_ref, share_ref, dq_ref, out, dq_out, stage, *scratch
):
    dq = backward(
        mine, q_ref, cot_ref, inner_ref, w_ref, share_ref, 0, out, dq_ref[...], *scratch
    )
    stage[...] = (dq * INV).T
    for s in range(out.shape[0]):
        dq_out[s] = stage[PIECE * s : PIECE * s + PIECE, :].astype(BF)


def gather_out(mine, dq, pieces, theirs, out):
    for s in range(out.shape[0]):
        both = (mine[s].astype(F32) + theirs[s].astype(F32)).astype(BF)
        out[s, 0:64, :] = both[:, 0:HD]
        out[s, 64:128, :] = both[:, HD:]
        out[s, 128:152, :] = pieces[s, :, 0:HD]
        out[s, 152:176, :] = pieces[s, :, HD:]
        out[s, 176:200, :] = dq[s]


def unpack_heads(r_ref, sent, kept, o_sent, o_kept, f_ref, o_ref):
    half = f_ref.shape[3] // HD
    for head in range(2 * half):
        at, cols = head // half, slice((head % half) * HD, (head % half + 1) * HD)
        first = PARTS * head
        for array, low in ((1, 0), (2, KROWS)):
            rows = slice(low, low + KROWS)
            both = sum(r_ref[first + part, rows, :].astype(F32) for part in range(PARTS))
            f_ref[at, array, :, cols] = both.astype(BF)
        ocols = slice(head * HD, head * HD + HD)
        for part in range(PARTS):
            for place, eight in enumerate(EIGHTS[part]):
                if eight is None:
                    continue
                row, low = 8 * eight, 8 * place
                f_ref[at, 0, row : row + 8, cols] = r_ref[first + part, 176 + low : 184 + low, :]
                for side in range(2):
                    from_row = 128 + PIECE * side + low
                    o_ref[row // 32, side, row % 32 : row % 32 + 8, ocols] = r_ref[
                        first + part, from_row : from_row + 8, :
                    ]
    sent[...] = f_ref[1 - core()]
    kept[...] = f_ref[core()]
    o_sent[...] = o_ref[1 - group()]
    o_kept[...] = o_ref[group()]


def finish(kept, got, o_kept, o_got, primal, tangent, dq, dk, dv):
    for at, ref in enumerate((dq, dk, dv)):
        for half in range(2):
            rows = slice(32 * half, 32 * half + 32)
            for piece, who in ((kept, core()), (got, 1 - core())):
                low = pl.multiple_of(64 * half + 32 * who, 32)
                ref[pl.ds(low, 32), :] = piece[at, rows, :]
    wide = o_kept.shape[2]
    for side, ref in enumerate((primal, tangent)):
        for piece, who in ((o_kept, group()), (o_got, 1 - group())):
            ref[:, pl.ds(pl.multiple_of(wide * who, HD), wide)] = piece[side]


def shape(*dims, dtype=BF):
    return jax.ShapeDtypeStruct(dims, dtype)


SWAP = [(0, 1), (1, 0)]
BLOCK_AXES = ("zl", "y", "x")


def exchange(array):
    return lax.all_to_all(array, BLOCK_AXES, 0, 0, tiled=True)


def swap(array, axis):
    return lax.ppermute(array, axis, SWAP)


def attention(chips, mine, mask):
    length, tiles = chips * KROWS, chips * PIECE // QT
    rows, subs = tiles * QT, length // SUB
    flops = 2 * length * rows * HD
    gpiece = shape(chips, 16, HD)
    gap_sent, gap_kept = call(
        split_gaps, [(gpiece, VMEM), (gpiece, VMEM)], [ANY], 2, (pltpu.SemaphoreType.DMA((2,)),),
        moved=500_000,
    )(mine)
    gap_got = swap(gap_sent, "zh")
    theirs = swap(mine, "c")
    q, qq = shape(tiles, QT, HD), shape(tiles, QT, 2 * HD)
    w = shape(tiles, length, QT)
    stats, sums, acc = (shape(tiles, n, QT, dtype=F32) for n in (1, 2, 2 * HD))
    tiles_of = (pltpu.VMEM(w.shape, BF), pltpu.SemaphoreType.DMA((tiles,)))
    scratch = (
        pltpu.VMEM((2, length, QT), F32),
        pltpu.VMEM((2, length, QT), BF),
        pltpu.VMEM((length, 2 * HD), BF),
        pltpu.VMEM((2 * HD, length), BF),
    )
    back_scratch = (
        pltpu.VMEM((subs, HD, SUB), BF),
        pltpu.VMEM((subs, SUB, rows), BF),
        pltpu.VMEM((SUB, rows), BF),
    )
    stage = pltpu.VMEM((rows, 2 * HD), F32)
    q, qq, w1, m1, sums1, acc1 = call(
        forward_mine,
        [(q, VMEM), (qq, VMEM), (w, HBM), (stats, VMEM), (sums, VMEM), (acc, VMEM)],
        [VMEM],
        30,
        (stage,) + tiles_of + scratch,
        6 * flops, length * rows, 7_000_000,
    )(mine)
    key_piece = shape(chips, KROWS, 2 * HD)
    dst, pieces, cot, inner, dq, share = call(
        theirs_both_ways,
        [
            (key_piece, VMEM), (shape(chips, PIECE, 2 * HD), VMEM), (shape(rows, HD), VMEM),
            (stats, VMEM), (shape(HD, rows, dtype=F32), VMEM),
            (shape(2, tiles, 1, QT, dtype=F32), VMEM),
        ],
        [ANY] + [VMEM] * 8,
        30,
        (
            pltpu.VMEM((chips, 2 * KROWS, 2 * HD), BF), pltpu.SemaphoreType.DMA((subs,)),
            pltpu.VMEM(w.shape, BF), pltpu.VMEM(stats.shape, F32), pltpu.VMEM(sums.shape, F32),
            pltpu.VMEM(acc.shape, F32), pltpu.VMEM((2,) + gpiece.shape, BF), stage,
        ) + back_scratch + scratch,
        14 * flops, length * rows, 7_000_000,
    )(theirs, q, qq, m1, sums1, acc1, gap_kept, gap_got, mask)
    partner = swap(dst, "c")
    out, dq = call(
        backward_mine,
        [(key_piece, VMEM), (shape(chips, PIECE, HD), VMEM)],
        [VMEM] * 7,
        26,
        (pltpu.VMEM((rows, HD), F32),) + back_scratch,
        8 * flops, 0, 7_000_000,
    )(mine, q, cot, inner, w1, share, dq)
    return call(gather_out, [(shape(chips, 200, HD), VMEM)], [VMEM] * 4, 8)(
        out, dq, pieces, partner
    )[0]


def per_device(q, k, v, tq, tk, tv, gap):
    chips = lax.axis_size(BLOCK_AXES)
    local, feat = q.shape
    wide = gap.shape[1] // 2
    piece = shape(6, KROWS, feat)
    arrays = (q, k, v, tq, tk, tv, gap)
    sent, kept, gap_here = call(
        split_tokens,
        [(piece, VMEM), (piece, VMEM), (shape(*gap.shape), VMEM)],
        [HBM] * 7,
        4,
        (pltpu.SemaphoreType.DMA((6, 2, 2)), pltpu.SemaphoreType.DMA),
    )(*(pltpu.with_memory_space_constraint(one, pltpu.HBM) for one in arrays))
    got = swap(sent, "c")
    packed = call(
        pack_heads,
        [(shape(chips, 168, 2 * HD), VMEM)],
        [VMEM] * 3,
        8,
        (pltpu.VMEM((2,) + piece.shape, BF),),
    )(kept, got, gap_here)[0]
    mine = exchange(packed)

    rows = chips * PIECE
    part = lax.axis_index(BLOCK_AXES) % PARTS
    short = (jnp.arange(rows) % PIECE >= 16) & (part == 1)
    mask = jnp.where(short, 0.0, 1.0).astype(F32)[None]
    back = exchange(attention(chips, mine, mask))

    opiece, fpiece = shape(2, 32, wide), shape(3, KROWS, feat)
    sent, kept, o_sent, o_kept = call(
        unpack_heads,
        [(fpiece, VMEM), (fpiece, VMEM), (opiece, VMEM), (opiece, VMEM)],
        [VMEM],
        8,
        (pltpu.VMEM((2,) + fpiece.shape, BF), pltpu.VMEM((2,) + opiece.shape, BF)),
    )(back)
    o_got = swap(o_sent, "zh")
    got = swap(sent, "c")
    small, large = shape(32, 2 * wide), shape(local, feat)
    return tuple(
        call(finish, [(small, VMEM)] * 2 + [(large, VMEM)] * 3, [VMEM] * 4, 8)(
            kept, got, o_kept, o_got
        )
    )


def solution(mesh):
    sizes = (2, 4, 4, 2, 2)
    inner = Mesh(mesh.devices.reshape(sizes), BLOCK_AXES + ("zh", "c"))
    both = P(BLOCK_AXES, ("zh", "c"))
    rows = P(BLOCK_AXES + ("zh", "c"), None)

    return jax.shard_map(
        per_device,
        mesh=inner,
        in_specs=(both,) * 6 + (rows,),
        out_specs=(rows, rows, both, both, both),
        check_vma=False,
    )
```

```python
import math

import jax
import jax.numpy as jnp
from jax import lax
from jax.experimental import pallas as pl
from jax.experimental.pallas import tpu as pltpu
from jax.sharding import Mesh, PartitionSpec as P


BF = jnp.bfloat16
F32 = jnp.float32
HD = 128
LOSS = 64.0
PARTS = 3
PIECE = 24
EIGHTS = ((0, 1, 4), (2, 5, None), (3, 6, 7))
GAPS = (((0, 0), (0, 1), (1, 0)), ((0, 2), (1, 1), None), ((0, 3), (1, 2), (1, 3)))
SLOT = 328
KROWS = 64
QT = 256
SUB = 512
INV = 1.0 / math.sqrt(HD)
EXP_SCALE = INV * math.log2(math.e)
VMEM = pl.BlockSpec(memory_space=pltpu.VMEM)
HBM = pl.BlockSpec(memory_space=pltpu.HBM)
ANY = pl.BlockSpec(memory_space=pl.ANY)


def call(body, outs, ins, limit, scratch=(), flops=0, exps=0, moved=1_000_000):
    return pl.pallas_call(
        body,
        out_shape=[
            pltpu.HBM(one.shape, one.dtype) if place is HBM else one for one, place in outs
        ],
        in_specs=ins,
        out_specs=[place for _, place in outs],
        scratch_shapes=list(scratch),
        compiler_params=pltpu.CompilerParams(vmem_limit_bytes=limit * 1024 * 1024),
        cost_estimate=pl.CostEstimate(flops=flops, bytes_accessed=moved, transcendentals=exps),
    )


def nt(a, b):
    return lax.dot_general(a, b, (((1,), (1,)), ((), ())), preferred_element_type=F32)


def nn(a, b):
    return lax.dot_general(a, b, (((1,), (0,)), ((), ())), preferred_element_type=F32)


def core():
    return lax.axis_index("c")


def group():
    return lax.axis_index("zh")


def half_row(half, who):
    return pl.multiple_of(64 * lax.rem(group() + half, 2) + 32 * who, 32)


def part_here():
    place = lax.axis_index("zl") * 16 + lax.axis_index("y") * 4 + lax.axis_index("x")
    return lax.rem(place, PARTS)


def split_tokens(*refs):
    *arrays, gap, sent, kept, gap_here, sems, gap_sems = refs
    copies = []
    for at, ref in enumerate(arrays):
        for half in range(2):
            for side, (dst, who) in enumerate(((sent, 1 - core()), (kept, core()))):
                copies.append(
                    pltpu.make_async_copy(
                        ref.at[pl.ds(half_row(half, who), 32), :],
                        dst.at[at, 32 * half : 32 * half + 32, :],
                        sems.at[at, half, side],
                    )
                )
    wide = gap_here.shape[2]
    for at, who in enumerate((group(), 1 - group())):
        lanes = pl.ds(pl.multiple_of(who * wide, HD), wide)
        copies.append(pltpu.make_async_copy(gap.at[:, lanes], gap_here.at[at], gap_sems.at[at]))
    for copy in copies:
        copy.start()
    for copy in copies:
        copy.wait()


def pack_heads(kept, got, gap, out, e_ref):
    e_ref[core()] = kept[...]
    e_ref[1 - core()] = got[...]
    half = e_ref.shape[3] // HD
    zero = jnp.zeros((8, HD), BF)
    for chip in range(out.shape[0]):
        head, part = chip // PARTS, chip % PARTS
        if head >= 2 * half:
            out[chip] = jnp.zeros(out.shape[1:], BF)
            continue
        at, cols = head // half, slice((head % half) * HD, (head % half + 1) * HD)
        for to, array in enumerate((1, 4, 2, 5)):
            out[chip, KROWS * to : KROWS * to + KROWS, :] = e_ref[at, array, :, cols]
        gcols = slice(head * HD, head * HD + HD)
        for to in range(3):
            eight = EIGHTS[part][to]
            for low, array in ((256, 0), (280, 3)):
                rows = slice(low + 8 * to, low + 8 * to + 8)
                if eight is None:
                    out[chip, rows, :] = zero
                else:
                    out[chip, rows, :] = e_ref[at, array, 8 * eight : 8 * eight + 8, cols]
            rows = slice(304 + 8 * to, 312 + 8 * to)
            if GAPS[part][to] is None:
                out[chip, rows, :] = zero
            else:
                which, eight = GAPS[part][to]
                out[chip, rows, :] = gap[which, 8 * eight : 8 * eight + 8, gcols]


def split_gaps(mine, sent, kept, sems):
    copies = [
        pltpu.make_async_copy(mine.at[:, low : low + 16, :], dst, sems.at[at])
        for at, (dst, low) in enumerate(((sent, 312), (kept, 304)))
    ]
    for copy in copies:
        copy.start()
    for copy in copies:
        copy.wait()


def fold(x, op):
    return op(x.reshape(x.shape[0] // 8, 8, x.shape[1]), axis=0)


def forward(keys, q_ref, qq_ref, w_ref, m_ref, sums_ref, acc_ref, s_ref, wt_ref, kk_ref, vt_ref,
            ready=None, done=None, close=None):
    tiles = q_ref.shape[0]
    per = SUB // KROWS
    subs = kk_ref.shape[0] // SUB
    ats = [slice(SUB * i, SUB * i + SUB) for i in range(subs)]

    def scores(t, i, peak):
        s = nt(kk_ref[ats[i], 0:HD], q_ref[t])
        s_ref[t % 2, ats[i], :] = s
        return jnp.maximum(peak, fold(s, jnp.max))

    def values(t, i):
        both = nn(vt_ref[:, ats[i]], w_ref[t, ats[i], :])
        tan = nn(vt_ref[0:HD, ats[i]], wt_ref[t % 2, ats[i], :]) * INV
        if i == 0:
            acc_ref[t, 0:HD, :] = both[0:HD]
            acc_ref[t, HD:, :] = both[HD:] + tan
        else:
            acc_ref[t, 0:HD, :] += both[0:HD]
            acc_ref[t, HD:, :] += both[HD:] + tan

    lowest = jnp.full((8, QT), -jnp.inf, F32)
    peak = lowest
    for i in range(subs):
        if ready is not None:
            ready(i)
        slots = slice(per * i, per * i + per)
        for half in range(2):
            lanes = slice(HD * half, HD * half + HD)
            kk_ref[ats[i], lanes] = keys[slots, KROWS * half : KROWS * half + KROWS, :].reshape(SUB, HD)
            v = keys[slots, KROWS * (2 + half) : KROWS * (3 + half), :].reshape(SUB, HD)
            vt_ref[lanes, ats[i]] = v.astype(F32).T.astype(BF)
        peak = scores(0, i, peak)
    for t in range(tiles):
        top = jnp.max(peak, axis=0, keepdims=True)
        m_ref[t] = top
        peak = lowest
        total = jnp.zeros((8, QT), F32)
        tan_total = jnp.zeros((8, QT), F32)
        for i in range(subs):
            w = jnp.exp2((s_ref[t % 2, ats[i], :] - top) * EXP_SCALE)
            wt = w * nt(kk_ref[ats[i], :], qq_ref[t])
            total = total + fold(w, jnp.sum)
            tan_total = tan_total + fold(wt, jnp.sum)
            w_ref[t, ats[i], :] = w.astype(BF)
            wt_ref[t % 2, ats[i], :] = wt.astype(BF)
            if t + 1 < tiles:
                peak = scores(t + 1, i, peak)
            if t > 0:
                values(t - 1, i)
        sums_ref[t, 0:1, :] = jnp.sum(total, axis=0, keepdims=True)
        sums_ref[t, 1:2, :] = jnp.sum(tan_total, axis=0, keepdims=True) * INV
        if done is not None:
            done(t)
        if close is not None and t > 0:
            close(t - 1)
    for i in range(subs):
        values(tiles - 1, i)
    if close is not None:
        close(tiles - 1)


def forward_mine(mine, q_ref, qq_ref, w_hbm, m_ref, sums_ref, acc_ref, stage, w_ref, sems, *scratch):
    for s in range(mine.shape[0]):
        stage[PIECE * s : PIECE * s + PIECE, 0:HD] = mine[s, 256:280, :].astype(F32)
        stage[PIECE * s : PIECE * s + PIECE, HD:] = mine[s, 280:304, :].astype(F32)
    tiles = q_ref.shape[0]
    for t in range(tiles):
        rows = slice(QT * t, QT * t + QT)
        q_ref[t] = stage[rows, 0:HD].astype(BF)
        qq_ref[t, :, 0:HD] = stage[rows, HD:].astype(BF)
        qq_ref[t, :, HD:] = stage[rows, 0:HD].astype(BF)
    copies = [pltpu.make_async_copy(w_ref.at[t], w_hbm.at[t], sems.at[t]) for t in range(tiles)]
    forward(
        mine, q_ref, qq_ref, w_ref, m_ref, sums_ref, acc_ref, *scratch,
        done=lambda t: copies[t].start(),
    )
    for copy in copies:
        copy.wait()


def backward(key, value, q_ref, cot_ref, inner_ref, w_ref, share_ref, side, dst, dq, kt_ref, ds_ref, p_ref):
    tiles = q_ref.shape[0]
    per = SUB // KROWS
    subs = ds_ref.shape[0]
    q_all = q_ref[...].reshape(tiles * QT, HD)
    for i in range(subs):
        at, slots = slice(SUB * i, SUB * i + SUB), slice(per * i, per * i + per)
        v = value(at, slots)
        kt_ref[i] = key(at, slots).astype(F32).T.astype(BF)
        for t in range(tiles):
            cols = slice(QT * t, QT * t + QT)
            p = w_ref[t, at, :].astype(F32) * share_ref[side, t]
            ds = p * (nt(v, cot_ref[cols, :]) - inner_ref[t])
            p_ref[:, cols] = p.astype(BF)
            ds_ref[i, :, cols] = ds.astype(BF)
        dk = nn(ds_ref[i], q_all) * INV
        dv = nn(p_ref[...], cot_ref[...])
        dst[slots, 0:KROWS, 0:HD] = dk.astype(BF).reshape(per, KROWS, HD)
        dst[slots, 0:KROWS, HD:] = dv.astype(BF).reshape(per, KROWS, HD)
    for i in range(subs):
        dq = dq + nn(kt_ref[i], ds_ref[i])
    return dq


def forward_theirs(
    theirs_hbm, q_ref, qq_ref, m1_ref, sums1_ref, acc1_ref,
    w_ref, pieces, cross, o_ref, share_ref, kv_ref,
    theirs, sems, m_ref, sums_ref, acc_ref, stage, *scratch
):
    per = SUB // KROWS
    copies = [
        pltpu.make_async_copy(
            theirs_hbm.at[per * i : per * i + per, 0 : 4 * KROWS, :],
            theirs.at[per * i : per * i + per],
            sems.at[i],
        )
        for i in range(theirs.shape[0] // per)
    ]
    for copy in copies:
        copy.start()

    def close(t):
        rows = slice(QT * t, QT * t + QT)
        top = jnp.maximum(m1_ref[t], m_ref[t])
        f1 = jnp.exp2((m1_ref[t] - top) * EXP_SCALE)
        f2 = jnp.exp2((m_ref[t] - top) * EXP_SCALE)
        sums = sums1_ref[t] * f1 + sums_ref[t] * f2
        inverse = 1.0 / sums[0:1]
        s1, s2 = f1 * inverse, f2 * inverse
        share_ref[0, t] = s1
        share_ref[1, t] = s2
        both = acc1_ref[t] * s1 + acc_ref[t] * s2
        tangent = both[HD:] - (sums[1:2] * inverse) * both[0:HD]
        o_ref[t, 0:HD, :] = both[0:HD].astype(BF).astype(F32)
        o_ref[t, HD:, :] = tangent.astype(BF).astype(F32)
        stage[rows, :] = o_ref[t].T

    forward(
        theirs, q_ref, qq_ref, w_ref, m_ref, sums_ref, acc_ref, *scratch,
        ready=lambda i: copies[i].wait(), close=close,
    )
    for i in range(len(copies)):
        at, slots = slice(SUB * i, SUB * i + SUB), slice(per * i, per * i + per)
        kv_ref[at, 0:HD] = theirs[slots, 0:KROWS, :].reshape(SUB, HD)
        kv_ref[at, HD:] = theirs[slots, 2 * KROWS : 3 * KROWS, :].reshape(SUB, HD)
    for s in range(pieces.shape[0]):
        low = PIECE * s
        pieces[s] = stage[low : low + PIECE, :].astype(BF)
        cross[s] = stage[low + 8 : low + PIECE, :].astype(BF)


def backward_theirs(
    kv, gap_kept, gap_got, mask, q_ref, o_ref, w_ref, share_ref,
    dst, cot_ref, inner_ref, dq_ref, stage, *scratch
):
    first = part_here() == 0
    for s in range(gap_kept.shape[0]):
        low = PIECE * s
        own, got = gap_kept[s].astype(F32), gap_got[s].astype(F32)
        stage[low : low + 8, :] = own[0:8]
        stage[low + 8 : low + 16, :] = jnp.where(first, own[8:16], got[0:8])
        stage[low + 16 : low + 24, :] = got[8:16]
    for t in range(q_ref.shape[0]):
        rows = slice(QT * t, QT * t + QT)
        cot = (LOSS * (stage[rows, :].T + o_ref[t, HD:, :])) * mask[:, rows]
        cot = cot.astype(BF).astype(F32)
        inner_ref[t] = jnp.sum(cot * o_ref[t, 0:HD, :], axis=0, keepdims=True)
        cot_ref[rows, :] = cot.T.astype(BF)
    dq_ref[...] = backward(
        lambda at, slots: kv[at, 0:HD], lambda at, slots: kv[at, HD:],
        q_ref, cot_ref, inner_ref, w_ref, share_ref, 1, dst, jnp.zeros(dq_ref.shape, F32), *scratch,
    )


def backward_mine(
    mine, q_ref, cot_ref, inner_ref, w_ref, share_ref, dq_ref, out, dq_out, stage, *scratch
):
    def rows_of(low):
        return lambda at, slots: mine[slots, low : low + KROWS, :].reshape(SUB, HD)

    dq = backward(
        rows_of(0), rows_of(2 * KROWS),
        q_ref, cot_ref, inner_ref, w_ref, share_ref, 0, out, dq_ref[...], *scratch,
    )
    stage[...] = (dq * INV).T
    for s in range(out.shape[0]):
        dq_out[s] = stage[PIECE * s : PIECE * s + PIECE, :].astype(BF)


def gather_out(mine, dq, pieces, got, theirs, out):
    first = part_here() == 0
    for s in range(out.shape[0]):
        both = (mine[s].astype(F32) + theirs[s].astype(F32)).astype(BF)
        out[s, 0:64, :] = both[:, 0:HD]
        out[s, 64:128, :] = both[:, HD:]
        second = jnp.where(first, pieces[s, 8:16, :].astype(F32), got[s, 0:8, :].astype(F32)).astype(BF)
        for low, lanes in ((128, slice(0, HD)), (152, slice(HD, 2 * HD))):
            out[s, low : low + 8, :] = pieces[s, 0:8, lanes]
            out[s, low + 8 : low + 16, :] = second[:, lanes]
            out[s, low + 16 : low + 24, :] = got[s, 8:16, lanes]
        out[s, 176:200, :] = dq[s]


def unpack_grads(r_ref, sent, kept, f_ref):
    half = f_ref.shape[3] // HD
    for head in range(2 * half):
        at, cols = head // half, slice((head % half) * HD, (head % half + 1) * HD)
        first = PARTS * head
        for array, low in ((1, 0), (2, KROWS)):
            rows = slice(low, low + KROWS)
            both = sum(r_ref[first + part, rows, :].astype(F32) for part in range(PARTS))
            f_ref[at, array, :, cols] = both.astype(BF)
        for part in range(PARTS):
            for place, eight in enumerate(EIGHTS[part]):
                if eight is not None:
                    row, low = 8 * eight, 176 + 8 * place
                    f_ref[at, 0, row : row + 8, cols] = r_ref[first + part, low : low + 8, :]
    sent[...] = f_ref[1 - core()]
    kept[...] = f_ref[core()]


def finish_outs(r_ref, primal, tangent, o_ref):
    wide = o_ref.shape[3]
    for head in range(wide // HD):
        cols = slice(head * HD, head * HD + HD)
        for part in range(PARTS):
            for place, unit in enumerate(GAPS[part]):
                if unit is None:
                    continue
                which, eight = unit
                for side in range(2):
                    low = 128 + PIECE * side + 8 * place
                    o_ref[which, side, 8 * eight : 8 * eight + 8, cols] = r_ref[
                        PARTS * head + part, low : low + 8, :
                    ]
    for side, ref in enumerate((primal, tangent)):
        for which, who in enumerate((group(), 1 - group())):
            ref[:, pl.ds(pl.multiple_of(wide * who, HD), wide)] = o_ref[which, side]


def finish_grads(kept, got, dq, dk, dv):
    for at, ref in enumerate((dq, dk, dv)):
        for half in range(2):
            rows = slice(32 * half, 32 * half + 32)
            for piece, who in ((kept, core()), (got, 1 - core())):
                ref[pl.ds(half_row(half, who), 32), :] = piece[at, rows, :]


def shape(*dims, dtype=BF):
    return jax.ShapeDtypeStruct(dims, dtype)


SWAP = [(0, 1), (1, 0)]
BLOCK_AXES = ("zl", "y", "x")


def exchange(array):
    return lax.all_to_all(array, BLOCK_AXES, 0, 0, tiled=True)


def swap(array, axis):
    return lax.ppermute(array, axis, SWAP)


def attention(chips, mine, mask):
    length, tiles = chips * KROWS, chips * PIECE // QT
    rows, subs = tiles * QT, length // SUB
    flops = 2 * length * rows * HD
    gpiece = shape(chips, 16, HD)
    gap_sent, gap_kept = call(
        split_gaps, [(gpiece, VMEM), (gpiece, VMEM)], [ANY], 2, (pltpu.SemaphoreType.DMA((2,)),),
        moved=500_000,
    )(mine)
    gap_got = swap(gap_sent, "zh")
    theirs = swap(mine, "c")
    q, qq = shape(tiles, QT, HD), shape(tiles, QT, 2 * HD)
    w = shape(tiles, length, QT)
    stats, sums, acc = (shape(tiles, n, QT, dtype=F32) for n in (1, 2, 2 * HD))
    tiles_of = (pltpu.VMEM(w.shape, BF), pltpu.SemaphoreType.DMA((tiles,)))
    scratch = (
        pltpu.VMEM((2, length, QT), F32),
        pltpu.VMEM((2, length, QT), BF),
        pltpu.VMEM((length, 2 * HD), BF),
        pltpu.VMEM((2 * HD, length), BF),
    )
    back_scratch = (
        pltpu.VMEM((subs, HD, SUB), BF),
        pltpu.VMEM((subs, SUB, rows), BF),
        pltpu.VMEM((SUB, rows), BF),
    )
    stage = pltpu.VMEM((rows, 2 * HD), F32)
    q, qq, w1, m1, sums1, acc1 = call(
        forward_mine,
        [(q, VMEM), (qq, VMEM), (w, HBM), (stats, VMEM), (sums, VMEM), (acc, VMEM)],
        [VMEM],
        30,
        (stage,) + tiles_of + scratch,
        6 * flops, length * rows, 7_000_000,
    )(mine)
    key_piece = shape(chips, KROWS, 2 * HD)
    w2, pieces, cross, o, share, kv = call(
        forward_theirs,
        [
            (w, VMEM), (shape(chips, PIECE, 2 * HD), VMEM), (shape(chips, 16, 2 * HD), VMEM),
            (acc, VMEM), (shape(2, tiles, 1, QT, dtype=F32), VMEM), (shape(length, 2 * HD), VMEM),
        ],
        [ANY] + [VMEM] * 5,
        30,
        (
            pltpu.VMEM((chips, 4 * KROWS, HD), BF), pltpu.SemaphoreType.DMA((subs,)),
            pltpu.VMEM(stats.shape, F32), pltpu.VMEM(sums.shape, F32), pltpu.VMEM(acc.shape, F32),
            stage,
        ) + scratch,
        6 * flops, length * rows, 7_000_000,
    )(theirs, q, qq, m1, sums1, acc1)
    cross = swap(cross, "zh")
    dst, cot, inner, dq = call(
        backward_theirs,
        [
            (key_piece, VMEM), (shape(rows, HD), VMEM), (stats, VMEM),
            (shape(HD, rows, dtype=F32), VMEM),
        ],
        [VMEM] * 8,
        30,
        (pltpu.VMEM((rows, HD), F32),) + back_scratch,
        8 * flops, 0, 7_000_000,
    )(kv, gap_kept, gap_got, mask, q, o, w2, share)
    partner = swap(dst, "c")
    out, dq = call(
        backward_mine,
        [(key_piece, VMEM), (shape(chips, PIECE, HD), VMEM)],
        [VMEM] * 7,
        30,
        (pltpu.VMEM((rows, HD), F32),) + back_scratch,
        8 * flops, 0, 7_000_000,
    )(mine, q, cot, inner, w1, share, dq)
    return call(gather_out, [(shape(chips, 200, HD), VMEM)], [VMEM] * 5, 8)(
        out, dq, pieces, cross, partner
    )[0]


def per_device(q, k, v, tq, tk, tv, gap):
    chips = lax.axis_size(BLOCK_AXES)
    local, feat = q.shape
    wide = gap.shape[1] // 2
    piece = shape(6, KROWS, feat)
    arrays = (q, k, v, tq, tk, tv, gap)
    sent, kept, gap_here = call(
        split_tokens,
        [(piece, VMEM), (piece, VMEM), (shape(2, 32, wide), VMEM)],
        [HBM] * 7,
        4,
        (pltpu.SemaphoreType.DMA((6, 2, 2)), pltpu.SemaphoreType.DMA((2,))),
    )(*(pltpu.with_memory_space_constraint(one, pltpu.HBM) for one in arrays))
    got = swap(sent, "c")
    packed = call(
        pack_heads,
        [(shape(chips, SLOT, HD), VMEM)],
        [VMEM] * 3,
        8,
        (pltpu.VMEM((2,) + piece.shape, BF),),
    )(kept, got, gap_here)[0]
    mine = exchange(packed)

    rows = chips * PIECE
    part = lax.axis_index(BLOCK_AXES) % PARTS
    short = (jnp.arange(rows) % PIECE >= 16) & (part == 1)
    mask = jnp.where(short, 0.0, 1.0).astype(F32)[None]
    back = exchange(attention(chips, mine, mask))

    fpiece = shape(3, KROWS, feat)
    sent, kept = call(
        unpack_grads, [(fpiece, VMEM), (fpiece, VMEM)], [VMEM], 8,
        (pltpu.VMEM((2,) + fpiece.shape, BF),),
    )(back)
    got = swap(sent, "c")
    small, large = shape(32, 2 * wide), shape(local, feat)
    primal, tangent = call(
        finish_outs, [(small, VMEM)] * 2, [VMEM], 8, (pltpu.VMEM((2, 2, 32, wide), BF),)
    )(back)
    dq, dk, dv = call(finish_grads, [(large, VMEM)] * 3, [VMEM] * 2, 8)(kept, got)
    return primal, tangent, dq, dk, dv


def solution(mesh):
    sizes = (2, 4, 4, 2, 2)
    inner = Mesh(mesh.devices.reshape(sizes), BLOCK_AXES + ("zh", "c"))
    both = P(BLOCK_AXES, ("zh", "c"))
    rows = P(BLOCK_AXES + ("zh", "c"), None)

    return jax.shard_map(
        per_device,
        mesh=inner,
        in_specs=(both,) * 6 + (rows,),
        out_specs=(rows, rows, both, both, both),
        check_vma=False,
    )
```

```python
import math

import jax
import jax.numpy as jnp
from jax import lax
from jax.experimental import pallas as pl
from jax.experimental.pallas import tpu as pltpu
from jax.sharding import Mesh, PartitionSpec as P


BF = jnp.bfloat16
F32 = jnp.float32
HD = 128
LOSS = 64.0
PARTS = 3
PIECE = 24
EIGHTS = ((0, 1, 4), (2, 5, None), (3, 6, 7))
GAPS = (((0, 0), (0, 1), (1, 0)), ((0, 2), (1, 1), None), ((0, 3), (1, 2), (1, 3)))
SLOT = 328
KROWS = 64
QT = 256
SUB = 512
INV = 1.0 / math.sqrt(HD)
EXP_SCALE = INV * math.log2(math.e)
VMEM = pl.BlockSpec(memory_space=pltpu.VMEM)
HBM = pl.BlockSpec(memory_space=pltpu.HBM)
ANY = pl.BlockSpec(memory_space=pl.ANY)


def call(body, outs, ins, limit, scratch=(), flops=0, exps=0, moved=1_000_000):
    return pl.pallas_call(
        body,
        out_shape=[
            pltpu.HBM(one.shape, one.dtype) if place is HBM else one for one, place in outs
        ],
        in_specs=ins,
        out_specs=[place for _, place in outs],
        scratch_shapes=list(scratch),
        compiler_params=pltpu.CompilerParams(vmem_limit_bytes=limit * 1024 * 1024),
        cost_estimate=pl.CostEstimate(flops=flops, bytes_accessed=moved, transcendentals=exps),
    )


def nt(a, b):
    return lax.dot_general(a, b, (((1,), (1,)), ((), ())), preferred_element_type=F32)


def nn(a, b):
    return lax.dot_general(a, b, (((1,), (0,)), ((), ())), preferred_element_type=F32)


def core():
    return lax.axis_index("c")


def group():
    return lax.axis_index("zh")


def half_row(half, who):
    return pl.multiple_of(64 * lax.rem(group() + half, 2) + 32 * who, 32)


def part_here():
    place = lax.axis_index("zl") * 16 + lax.axis_index("y") * 4 + lax.axis_index("x")
    return lax.rem(place, PARTS)


def split_tokens(arrays, dst, who, sems):
    return [
        pltpu.make_async_copy(
            ref.at[pl.ds(half_row(half, who), 32), :],
            dst.at[at, 32 * half : 32 * half + 32, :],
            sems.at[at, half],
        )
        for at, ref in enumerate(arrays)
        for half in range(2)
    ]


def run_all(copies):
    for copy in copies:
        copy.start()
    for copy in copies:
        copy.wait()


def send_tokens(*refs):
    *arrays, sent, sems = refs
    run_all(split_tokens(arrays, sent, 1 - core(), sems))


def keep_tokens(*refs):
    *arrays, gap, kept, gap_here, sems, gap_sems = refs
    copies = split_tokens(arrays, kept, core(), sems)
    wide = gap_here.shape[2]
    for at, who in enumerate((group(), 1 - group())):
        lanes = pl.ds(pl.multiple_of(who * wide, HD), wide)
        copies.append(pltpu.make_async_copy(gap.at[:, lanes], gap_here.at[at], gap_sems.at[at]))
    run_all(copies)


def pack_heads(kept, got, gap, out, e_ref):
    e_ref[core()] = kept[...]
    e_ref[1 - core()] = got[...]
    half = e_ref.shape[3] // HD
    zero = jnp.zeros((8, HD), BF)
    for chip in range(out.shape[0]):
        head, part = chip // PARTS, chip % PARTS
        if head >= 2 * half:
            out[chip] = jnp.zeros(out.shape[1:], BF)
            continue
        at, cols = head // half, slice((head % half) * HD, (head % half + 1) * HD)
        for to, array in enumerate((1, 4, 2, 5)):
            out[chip, KROWS * to : KROWS * to + KROWS, :] = e_ref[at, array, :, cols]
        gcols = slice(head * HD, head * HD + HD)
        for to in range(3):
            eight = EIGHTS[part][to]
            for low, array in ((256, 0), (280, 3)):
                rows = slice(low + 8 * to, low + 8 * to + 8)
                if eight is None:
                    out[chip, rows, :] = zero
                else:
                    out[chip, rows, :] = e_ref[at, array, 8 * eight : 8 * eight + 8, cols]
            rows = slice(304 + 8 * to, 312 + 8 * to)
            if GAPS[part][to] is None:
                out[chip, rows, :] = zero
            else:
                which, eight = GAPS[part][to]
                out[chip, rows, :] = gap[which, 8 * eight : 8 * eight + 8, gcols]


def split_gaps(mine, sent, kept, sems):
    run_all(
        [
            pltpu.make_async_copy(mine.at[:, low : low + 16, :], dst, sems.at[at])
            for at, (dst, low) in enumerate(((sent, 312), (kept, 304)))
        ]
    )


def fold(x, op):
    return op(x.reshape(x.shape[0] // 8, 8, x.shape[1]), axis=0)


def forward(keys, q_ref, qq_ref, w_ref, m_ref, sums_ref, acc_ref, s_ref, wt_ref, kk_ref, vt_ref,
            done=None, close=None):
    tiles = q_ref.shape[0]
    per = SUB // KROWS
    subs = kk_ref.shape[0] // SUB
    ats = [slice(SUB * i, SUB * i + SUB) for i in range(subs)]

    def scores(t, i, peak):
        s = nt(kk_ref[ats[i], 0:HD], q_ref[t])
        s_ref[t % 2, ats[i], :] = s
        return jnp.maximum(peak, fold(s, jnp.max))

    def values(t, i):
        both = nn(vt_ref[:, ats[i]], w_ref[t, ats[i], :])
        tan = nn(vt_ref[0:HD, ats[i]], wt_ref[t % 2, ats[i], :]) * INV
        if i == 0:
            acc_ref[t, 0:HD, :] = both[0:HD]
            acc_ref[t, HD:, :] = both[HD:] + tan
        else:
            acc_ref[t, 0:HD, :] += both[0:HD]
            acc_ref[t, HD:, :] += both[HD:] + tan

    lowest = jnp.full((8, QT), -jnp.inf, F32)
    peak = lowest
    for i in range(subs):
        slots = slice(per * i, per * i + per)
        for half in range(2):
            lanes = slice(HD * half, HD * half + HD)
            kk_ref[ats[i], lanes] = keys[slots, KROWS * half : KROWS * half + KROWS, :].reshape(SUB, HD)
            v = keys[slots, KROWS * (2 + half) : KROWS * (3 + half), :].reshape(SUB, HD)
            vt_ref[lanes, ats[i]] = v.astype(F32).T.astype(BF)
        peak = scores(0, i, peak)
    for t in range(tiles):
        top = jnp.max(peak, axis=0, keepdims=True)
        m_ref[t] = top
        peak = lowest
        total = jnp.zeros((8, QT), F32)
        tan_total = jnp.zeros((8, QT), F32)
        for i in range(subs):
            w = jnp.exp2((s_ref[t % 2, ats[i], :] - top) * EXP_SCALE)
            wt = w * nt(kk_ref[ats[i], :], qq_ref[t])
            total = total + fold(w, jnp.sum)
            tan_total = tan_total + fold(wt, jnp.sum)
            w_ref[t, ats[i], :] = w.astype(BF)
            wt_ref[t % 2, ats[i], :] = wt.astype(BF)
            if t + 1 < tiles:
                peak = scores(t + 1, i, peak)
            if t > 0:
                values(t - 1, i)
        sums_ref[t, 0:1, :] = jnp.sum(total, axis=0, keepdims=True)
        sums_ref[t, 1:2, :] = jnp.sum(tan_total, axis=0, keepdims=True) * INV
        if done is not None:
            done(t)
        if close is not None and t > 0:
            close(t - 1)
    for i in range(subs):
        values(tiles - 1, i)
    if close is not None:
        close(tiles - 1)


def forward_mine(mine, q_ref, qq_ref, w_hbm, m_ref, sums_ref, acc_ref, stage, w_ref, sems, *scratch):
    for s in range(mine.shape[0]):
        stage[PIECE * s : PIECE * s + PIECE, 0:HD] = mine[s, 256:280, :].astype(F32)
        stage[PIECE * s : PIECE * s + PIECE, HD:] = mine[s, 280:304, :].astype(F32)
    tiles = q_ref.shape[0]
    for t in range(tiles):
        rows = slice(QT * t, QT * t + QT)
        q_ref[t] = stage[rows, 0:HD].astype(BF)
        qq_ref[t, :, 0:HD] = stage[rows, HD:].astype(BF)
        qq_ref[t, :, HD:] = stage[rows, 0:HD].astype(BF)
    copies = [pltpu.make_async_copy(w_ref.at[t], w_hbm.at[t], sems.at[t]) for t in range(tiles)]
    forward(
        mine, q_ref, qq_ref, w_ref, m_ref, sums_ref, acc_ref, *scratch,
        done=lambda t: copies[t].start(),
    )
    for copy in copies:
        copy.wait()


def rows_of(ref, low):
    return lambda at, slots: ref[slots, low : low + KROWS, :].reshape(SUB, HD)


def backward(key, value, q_ref, cot_ref, inner_ref, w_ref, share_ref, side, dst, dq, kt_ref, ds_ref, p_ref):
    tiles = q_ref.shape[0]
    per = SUB // KROWS
    subs = ds_ref.shape[0]
    q_all = q_ref[...].reshape(tiles * QT, HD)
    for i in range(subs):
        at, slots = slice(SUB * i, SUB * i + SUB), slice(per * i, per * i + per)
        v = value(at, slots)
        kt_ref[i] = key(at, slots).astype(F32).T.astype(BF)
        for t in range(tiles):
            cols = slice(QT * t, QT * t + QT)
            p = w_ref[t, at, :].astype(F32) * share_ref[side, t]
            ds = p * (nt(v, cot_ref[cols, :]) - inner_ref[t])
            p_ref[:, cols] = p.astype(BF)
            ds_ref[i, :, cols] = ds.astype(BF)
        dk = nn(ds_ref[i], q_all) * INV
        dv = nn(p_ref[...], cot_ref[...])
        dst[slots, 0:KROWS, 0:HD] = dk.astype(BF).reshape(per, KROWS, HD)
        dst[slots, 0:KROWS, HD:] = dv.astype(BF).reshape(per, KROWS, HD)
    for i in range(subs):
        dq = dq + nn(kt_ref[i], ds_ref[i])
    return dq


def forward_theirs(
    theirs, q_ref, qq_ref, m1_ref, sums1_ref, acc1_ref,
    w_ref, pieces, cross, o_ref, share_ref,
    m_ref, sums_ref, acc_ref, stage, *scratch
):
    def close(t):
        rows = slice(QT * t, QT * t + QT)
        top = jnp.maximum(m1_ref[t], m_ref[t])
        f1 = jnp.exp2((m1_ref[t] - top) * EXP_SCALE)
        f2 = jnp.exp2((m_ref[t] - top) * EXP_SCALE)
        sums = sums1_ref[t] * f1 + sums_ref[t] * f2
        inverse = 1.0 / sums[0:1]
        s1, s2 = f1 * inverse, f2 * inverse
        share_ref[0, t] = s1
        share_ref[1, t] = s2
        both = acc1_ref[t] * s1 + acc_ref[t] * s2
        tangent = both[HD:] - (sums[1:2] * inverse) * both[0:HD]
        o_ref[t, 0:HD, :] = both[0:HD].astype(BF).astype(F32)
        o_ref[t, HD:, :] = tangent.astype(BF).astype(F32)
        stage[rows, :] = o_ref[t].T

    forward(
        theirs, q_ref, qq_ref, w_ref, m_ref, sums_ref, acc_ref, *scratch, close=close
    )
    for s in range(pieces.shape[0]):
        low = PIECE * s
        pieces[s] = stage[low : low + PIECE, :].astype(BF)
        cross[s] = stage[low + 8 : low + PIECE, :].astype(BF)


def backward_theirs(
    theirs, gap_kept, gap_got, q_ref, o_ref, w_ref, share_ref,
    dst, cot_ref, inner_ref, dq_ref, stage, *scratch
):
    first = part_here() == 0
    for s in range(gap_kept.shape[0]):
        low = PIECE * s
        own, got = gap_kept[s].astype(F32), gap_got[s].astype(F32)
        stage[low : low + 8, :] = own[0:8]
        stage[low + 8 : low + 16, :] = jnp.where(first, own[8:16], got[0:8])
        stage[low + 16 : low + 24, :] = got[8:16]
    for t in range(q_ref.shape[0]):
        rows = slice(QT * t, QT * t + QT)
        place = lax.rem(QT * t + lax.broadcasted_iota(jnp.int32, (1, QT), 1), PIECE)
        short = jnp.where(place >= 16, 1, 0) * jnp.where(part_here() == 1, 1, 0)
        mask = jnp.where(short == 1, 0.0, 1.0)
        cot = (LOSS * (stage[rows, :].T + o_ref[t, HD:, :])) * mask
        cot = cot.astype(BF).astype(F32)
        inner_ref[t] = jnp.sum(cot * o_ref[t, 0:HD, :], axis=0, keepdims=True)
        cot_ref[rows, :] = cot.T.astype(BF)
    dq_ref[...] = backward(
        rows_of(theirs, 0), rows_of(theirs, 2 * KROWS),
        q_ref, cot_ref, inner_ref, w_ref, share_ref, 1, dst, jnp.zeros(dq_ref.shape, F32), *scratch,
    )


def backward_mine(
    mine, q_ref, cot_ref, inner_ref, w_ref, share_ref, dq_ref, out, dq_out, stage, *scratch
):
    dq = backward(
        rows_of(mine, 0), rows_of(mine, 2 * KROWS),
        q_ref, cot_ref, inner_ref, w_ref, share_ref, 0, out, dq_ref[...], *scratch,
    )
    stage[...] = (dq * INV).T
    for s in range(out.shape[0]):
        dq_out[s] = stage[PIECE * s : PIECE * s + PIECE, :].astype(BF)


def gather_out(mine, dq, pieces, got, theirs, out):
    first = part_here() == 0
    for s in range(out.shape[0]):
        both = (mine[s].astype(F32) + theirs[s].astype(F32)).astype(BF)
        out[s, 0:64, :] = both[:, 0:HD]
        out[s, 64:128, :] = both[:, HD:]
        second = jnp.where(first, pieces[s, 8:16, :].astype(F32), got[s, 0:8, :].astype(F32)).astype(BF)
        for low, lanes in ((128, slice(0, HD)), (152, slice(HD, 2 * HD))):
            out[s, low : low + 8, :] = pieces[s, 0:8, lanes]
            out[s, low + 8 : low + 16, :] = second[:, lanes]
            out[s, low + 16 : low + 24, :] = got[s, 8:16, lanes]
        out[s, 176:200, :] = dq[s]


def unpack_grads(r_ref, sent, kept, f_ref):
    half = f_ref.shape[3] // HD
    for head in range(2 * half):
        at, cols = head // half, slice((head % half) * HD, (head % half + 1) * HD)
        first = PARTS * head
        for array, low in ((1, 0), (2, KROWS)):
            rows = slice(low, low + KROWS)
            both = sum(r_ref[first + part, rows, :].astype(F32) for part in range(PARTS))
            f_ref[at, array, :, cols] = both.astype(BF)
        for part in range(PARTS):
            for place, eight in enumerate(EIGHTS[part]):
                if eight is not None:
                    row, low = 8 * eight, 176 + 8 * place
                    f_ref[at, 0, row : row + 8, cols] = r_ref[first + part, low : low + 8, :]
    sent[...] = f_ref[1 - core()]
    kept[...] = f_ref[core()]


def finish_outs(r_ref, primal, tangent, o_ref):
    wide = o_ref.shape[3]
    for head in range(wide // HD):
        cols = slice(head * HD, head * HD + HD)
        for part in range(PARTS):
            for place, unit in enumerate(GAPS[part]):
                if unit is None:
                    continue
                which, eight = unit
                for side in range(2):
                    low = 128 + PIECE * side + 8 * place
                    o_ref[which, side, 8 * eight : 8 * eight + 8, cols] = r_ref[
                        PARTS * head + part, low : low + 8, :
                    ]
    for side, ref in enumerate((primal, tangent)):
        for which, who in enumerate((group(), 1 - group())):
            ref[:, pl.ds(pl.multiple_of(wide * who, HD), wide)] = o_ref[which, side]


def finish_grads(kept, got, dq, dk, dv):
    for at, ref in enumerate((dq, dk, dv)):
        for half in range(2):
            rows = slice(32 * half, 32 * half + 32)
            for piece, who in ((kept, core()), (got, 1 - core())):
                ref[pl.ds(half_row(half, who), 32), :] = piece[at, rows, :]


def shape(*dims, dtype=BF):
    return jax.ShapeDtypeStruct(dims, dtype)


SWAP = [(0, 1), (1, 0)]
BLOCK_AXES = ("zl", "y", "x")


def exchange(array):
    return lax.all_to_all(array, BLOCK_AXES, 0, 0, tiled=True)


def swap(array, axis):
    return lax.ppermute(array, axis, SWAP)


def attention(chips, mine):
    length, tiles = chips * KROWS, chips * PIECE // QT
    rows, subs = tiles * QT, length // SUB
    flops = 2 * length * rows * HD
    gpiece = shape(chips, 16, HD)
    gap_sent, gap_kept = call(
        split_gaps, [(gpiece, VMEM), (gpiece, VMEM)], [ANY], 2, (pltpu.SemaphoreType.DMA((2,)),),
        moved=500_000,
    )(mine)
    gap_got = swap(gap_sent, "zh")
    theirs = swap(mine, "c")
    q, qq = shape(tiles, QT, HD), shape(tiles, QT, 2 * HD)
    w = shape(tiles, length, QT)
    stats, sums, acc = (shape(tiles, n, QT, dtype=F32) for n in (1, 2, 2 * HD))
    tiles_of = (pltpu.VMEM(w.shape, BF), pltpu.SemaphoreType.DMA((tiles,)))
    scratch = (
        pltpu.VMEM((2, length, QT), F32),
        pltpu.VMEM((2, length, QT), BF),
        pltpu.VMEM((length, 2 * HD), BF),
        pltpu.VMEM((2 * HD, length), BF),
    )
    back_scratch = (
        pltpu.VMEM((subs, HD, SUB), BF),
        pltpu.VMEM((subs, SUB, rows), BF),
        pltpu.VMEM((SUB, rows), BF),
    )
    stage = pltpu.VMEM((rows, 2 * HD), F32)
    q, qq, w1, m1, sums1, acc1 = call(
        forward_mine,
        [(q, VMEM), (qq, VMEM), (w, HBM), (stats, VMEM), (sums, VMEM), (acc, VMEM)],
        [VMEM],
        30,
        (stage,) + tiles_of + scratch,
        6 * flops, length * rows, 7_000_000,
    )(mine)
    key_piece = shape(chips, KROWS, 2 * HD)
    w2, pieces, cross, o, share = call(
        forward_theirs,
        [
            (w, VMEM), (shape(chips, PIECE, 2 * HD), VMEM), (shape(chips, 16, 2 * HD), VMEM),
            (acc, VMEM), (shape(2, tiles, 1, QT, dtype=F32), VMEM),
        ],
        [VMEM] * 6,
        30,
        (
            pltpu.VMEM(stats.shape, F32), pltpu.VMEM(sums.shape, F32), pltpu.VMEM(acc.shape, F32),
            stage,
        ) + scratch,
        6 * flops, length * rows, 7_000_000,
    )(theirs, q, qq, m1, sums1, acc1)
    cross = swap(cross, "zh")
    dst, cot, inner, dq = call(
        backward_theirs,
        [
            (key_piece, VMEM), (shape(rows, HD), VMEM), (stats, VMEM),
            (shape(HD, rows, dtype=F32), VMEM),
        ],
        [VMEM] * 7,
        30,
        (pltpu.VMEM((rows, HD), F32),) + back_scratch,
        8 * flops, 0, 7_000_000,
    )(theirs, gap_kept, gap_got, q, o, w2, share)
    partner = swap(dst, "c")
    out, dq = call(
        backward_mine,
        [(key_piece, VMEM), (shape(chips, PIECE, HD), VMEM)],
        [VMEM] * 7,
        30,
        (pltpu.VMEM((rows, HD), F32),) + back_scratch,
        8 * flops, 0, 7_000_000,
    )(mine, q, cot, inner, w1, share, dq)
    return call(gather_out, [(shape(chips, 200, HD), VMEM)], [VMEM] * 5, 8)(
        out, dq, pieces, cross, partner
    )[0]


def per_device(q, k, v, tq, tk, tv, gap):
    chips = lax.axis_size(BLOCK_AXES)
    local, feat = q.shape
    wide = gap.shape[1] // 2
    piece = shape(6, KROWS, feat)
    arrays = [
        pltpu.with_memory_space_constraint(one, pltpu.HBM) for one in (q, k, v, tq, tk, tv, gap)
    ]
    sems = pltpu.SemaphoreType.DMA((6, 2))
    sent = call(send_tokens, [(piece, VMEM)], [HBM] * 6, 2, (sems,))(*arrays[:6])[0]
    got = swap(sent, "c")
    kept, gap_here = call(
        keep_tokens,
        [(piece, VMEM), (shape(2, 32, wide), VMEM)],
        [HBM] * 7,
        2,
        (sems, pltpu.SemaphoreType.DMA((2,))),
    )(*arrays)
    packed = call(
        pack_heads,
        [(shape(chips, SLOT, HD), VMEM)],
        [VMEM] * 3,
        8,
        (pltpu.VMEM((2,) + piece.shape, BF),),
    )(kept, got, gap_here)[0]
    mine = exchange(packed)

    back = exchange(attention(chips, mine))

    fpiece = shape(3, KROWS, feat)
    sent, kept = call(
        unpack_grads, [(fpiece, VMEM), (fpiece, VMEM)], [VMEM], 8,
        (pltpu.VMEM((2,) + fpiece.shape, BF),),
    )(back)
    got = swap(sent, "c")
    small, large = shape(32, 2 * wide), shape(local, feat)
    primal, tangent = call(
        finish_outs, [(small, VMEM)] * 2, [VMEM], 8, (pltpu.VMEM((2, 2, 32, wide), BF),)
    )(back)
    dq, dk, dv = call(finish_grads, [(large, VMEM)] * 3, [VMEM] * 2, 8)(kept, got)
    return primal, tangent, dq, dk, dv


def solution(mesh):
    sizes = (2, 4, 4, 2, 2)
    inner = Mesh(mesh.devices.reshape(sizes), BLOCK_AXES + ("zh", "c"))
    both = P(BLOCK_AXES, ("zh", "c"))
    rows = P(BLOCK_AXES + ("zh", "c"), None)

    return jax.shard_map(
        per_device,
        mesh=inner,
        in_specs=(both,) * 6 + (rows,),
        out_specs=(rows, rows, both, both, both),
        check_vma=False,
    )
```

```python
import math

import jax
import jax.numpy as jnp
from jax import lax
from jax.experimental import pallas as pl
from jax.experimental.pallas import tpu as pltpu
from jax.sharding import Mesh, PartitionSpec as P


BF = jnp.bfloat16
F32 = jnp.float32
HD = 128
LOSS = 64.0
PARTS = 3
PIECE = 24
EIGHTS = ((0, 1, 4), (2, 5, None), (3, 6, 7))
GAPS = (((0, 0), (0, 1), (1, 0)), ((0, 2), (1, 1), None), ((0, 3), (1, 2), (1, 3)))
SLOT = 328
KROWS = 64
QT = 256
SUB = 512
INV = 1.0 / math.sqrt(HD)
EXP_SCALE = INV * math.log2(math.e)
VMEM = pl.BlockSpec(memory_space=pltpu.VMEM)
HBM = pl.BlockSpec(memory_space=pltpu.HBM)
ANY = pl.BlockSpec(memory_space=pl.ANY)


def call(body, outs, ins, limit, scratch=(), flops=0, exps=0, moved=1_000_000, aliases=None):
    return pl.pallas_call(
        body,
        out_shape=[
            pltpu.HBM(one.shape, one.dtype) if place is HBM else one for one, place in outs
        ],
        in_specs=ins,
        out_specs=[place for _, place in outs],
        scratch_shapes=list(scratch),
        input_output_aliases=aliases or {},
        compiler_params=pltpu.CompilerParams(vmem_limit_bytes=limit * 1024 * 1024),
        cost_estimate=pl.CostEstimate(flops=flops, bytes_accessed=moved, transcendentals=exps),
    )


def nt(a, b):
    return lax.dot_general(a, b, (((1,), (1,)), ((), ())), preferred_element_type=F32)


def nn(a, b):
    return lax.dot_general(a, b, (((1,), (0,)), ((), ())), preferred_element_type=F32)


def core():
    return lax.axis_index("c")


def group():
    return lax.axis_index("zh")


def half_row(half, who):
    return pl.multiple_of(64 * lax.rem(group() + half, 2) + 32 * who, 32)


def part_here():
    place = lax.axis_index("zl") * 16 + lax.axis_index("y") * 4 + lax.axis_index("x")
    return lax.rem(place, PARTS)


def split_tokens(arrays, dst, who, sems):
    return [
        pltpu.make_async_copy(
            ref.at[pl.ds(half_row(half, who), 32), :],
            dst.at[at, 32 * half : 32 * half + 32, :],
            sems.at[at, half],
        )
        for at, ref in enumerate(arrays)
        for half in range(2)
    ]


def run_all(copies):
    for copy in copies:
        copy.start()
    for copy in copies:
        copy.wait()


def send_tokens(*refs):
    *arrays, sent, sems = refs
    run_all(split_tokens(arrays, sent, 1 - core(), sems))


def keep_tokens(*refs):
    *arrays, gap, kept, gap_here, sems, gap_sems = refs
    copies = split_tokens(arrays, kept, core(), sems)
    wide = gap_here.shape[2]
    for at, who in enumerate((group(), 1 - group())):
        lanes = pl.ds(pl.multiple_of(who * wide, HD), wide)
        copies.append(pltpu.make_async_copy(gap.at[:, lanes], gap_here.at[at], gap_sems.at[at]))
    run_all(copies)


def pack_heads(kept, got, gap, out, e_ref):
    e_ref[core()] = kept[...]
    e_ref[1 - core()] = got[...]
    half = e_ref.shape[3] // HD
    zero = jnp.zeros((8, HD), BF)
    for chip in range(out.shape[0]):
        head, part = chip // PARTS, chip % PARTS
        if head >= 2 * half:
            out[chip] = jnp.zeros(out.shape[1:], BF)
            continue
        at, cols = head // half, slice((head % half) * HD, (head % half + 1) * HD)
        for to, array in enumerate((1, 4, 2, 5)):
            out[chip, KROWS * to : KROWS * to + KROWS, :] = e_ref[at, array, :, cols]
        gcols = slice(head * HD, head * HD + HD)
        for to in range(3):
            eight = EIGHTS[part][to]
            for low, array in ((256, 0), (280, 3)):
                rows = slice(low + 8 * to, low + 8 * to + 8)
                if eight is None:
                    out[chip, rows, :] = zero
                else:
                    out[chip, rows, :] = e_ref[at, array, 8 * eight : 8 * eight + 8, cols]
            rows = slice(304 + 8 * to, 312 + 8 * to)
            if GAPS[part][to] is None:
                out[chip, rows, :] = zero
            else:
                which, eight = GAPS[part][to]
                out[chip, rows, :] = gap[which, 8 * eight : 8 * eight + 8, gcols]


def fold(x, op):
    return op(x.reshape(x.shape[0] // 8, 8, x.shape[1]), axis=0)


def forward(keys, q_ref, qq_ref, w_ref, m_ref, sums_ref, acc_ref, s_ref, wt_ref, kk_ref, vt_ref,
            done=None, close=None):
    tiles = q_ref.shape[0]
    per = SUB // KROWS
    subs = kk_ref.shape[0] // SUB
    ats = [slice(SUB * i, SUB * i + SUB) for i in range(subs)]

    def scores(t, i, peak):
        s = nt(kk_ref[ats[i], 0:HD], q_ref[t])
        s_ref[t % 2, ats[i], :] = s
        return jnp.maximum(peak, fold(s, jnp.max))

    def values(t, i):
        both = nn(vt_ref[:, ats[i]], w_ref[t, ats[i], :])
        tan = nn(vt_ref[0:HD, ats[i]], wt_ref[t % 2, ats[i], :]) * INV
        if i == 0:
            acc_ref[t, 0:HD, :] = both[0:HD]
            acc_ref[t, HD:, :] = both[HD:] + tan
        else:
            acc_ref[t, 0:HD, :] += both[0:HD]
            acc_ref[t, HD:, :] += both[HD:] + tan

    lowest = jnp.full((8, QT), -jnp.inf, F32)
    peak = lowest
    for i in range(subs):
        slots = slice(per * i, per * i + per)
        for half in range(2):
            lanes = slice(HD * half, HD * half + HD)
            kk_ref[ats[i], lanes] = keys[slots, KROWS * half : KROWS * half + KROWS, :].reshape(SUB, HD)
            v = keys[slots, KROWS * (2 + half) : KROWS * (3 + half), :].reshape(SUB, HD)
            vt_ref[lanes, ats[i]] = v.astype(F32).T.astype(BF)
        peak = scores(0, i, peak)
    for t in range(tiles):
        top = jnp.max(peak, axis=0, keepdims=True)
        m_ref[t] = top
        peak = lowest
        total = jnp.zeros((8, QT), F32)
        tan_total = jnp.zeros((8, QT), F32)
        for i in range(subs):
            w = jnp.exp2((s_ref[t % 2, ats[i], :] - top) * EXP_SCALE)
            wt = w * nt(kk_ref[ats[i], :], qq_ref[t])
            total = total + fold(w, jnp.sum)
            tan_total = tan_total + fold(wt, jnp.sum)
            w_ref[t, ats[i], :] = w.astype(BF)
            wt_ref[t % 2, ats[i], :] = wt.astype(BF)
            if t + 1 < tiles:
                peak = scores(t + 1, i, peak)
            if t > 0:
                values(t - 1, i)
        sums_ref[t, 0:1, :] = jnp.sum(total, axis=0, keepdims=True)
        sums_ref[t, 1:2, :] = jnp.sum(tan_total, axis=0, keepdims=True) * INV
        if done is not None:
            done(t)
        if close is not None and t > 0:
            close(t - 1)
    for i in range(subs):
        values(tiles - 1, i)
    if close is not None:
        close(tiles - 1)


def forward_mine(
    mine, q_ref, qq_ref, w_hbm, m_ref, sums_ref, acc_ref, gap_sent, gap_kept,
    stage, w_ref, sems, *scratch
):
    for s in range(mine.shape[0]):
        gap_sent[s] = mine[s, 312:328, :]
        gap_kept[s] = mine[s, 304:320, :]
        stage[PIECE * s : PIECE * s + PIECE, 0:HD] = mine[s, 256:280, :].astype(F32)
        stage[PIECE * s : PIECE * s + PIECE, HD:] = mine[s, 280:304, :].astype(F32)
    tiles = q_ref.shape[0]
    for t in range(tiles):
        rows = slice(QT * t, QT * t + QT)
        q_ref[t] = stage[rows, 0:HD].astype(BF)
        qq_ref[t, :, 0:HD] = stage[rows, HD:].astype(BF)
        qq_ref[t, :, HD:] = stage[rows, 0:HD].astype(BF)
    copies = [pltpu.make_async_copy(w_ref.at[t], w_hbm.at[t], sems.at[t]) for t in range(tiles)]
    forward(
        mine, q_ref, qq_ref, w_ref, m_ref, sums_ref, acc_ref, *scratch,
        done=lambda t: copies[t].start(),
    )
    for copy in copies:
        copy.wait()


def rows_of(ref, low):
    return lambda at, slots: ref[slots, low : low + KROWS, :].reshape(SUB, HD)


def backward(key, value, q_ref, cot_ref, inner_ref, w_ref, share_ref, side, dst, dq, kt_ref, ds_ref, p_ref):
    tiles = q_ref.shape[0]
    per = SUB // KROWS
    subs = ds_ref.shape[0]
    q_all = q_ref[...].reshape(tiles * QT, HD)
    for i in range(subs):
        at, slots = slice(SUB * i, SUB * i + SUB), slice(per * i, per * i + per)
        v = value(at, slots)
        kt_ref[i] = key(at, slots).astype(F32).T.astype(BF)
        for t in range(tiles):
            cols = slice(QT * t, QT * t + QT)
            p = w_ref[t, at, :].astype(F32) * share_ref[side, t]
            ds = p * (nt(v, cot_ref[cols, :]) - inner_ref[t])
            p_ref[:, cols] = p.astype(BF)
            ds_ref[i, :, cols] = ds.astype(BF)
        dk = nn(ds_ref[i], q_all) * INV
        dv = nn(p_ref[...], cot_ref[...])
        dst[slots, 0:KROWS, 0:HD] = dk.astype(BF).reshape(per, KROWS, HD)
        dst[slots, 0:KROWS, HD:] = dv.astype(BF).reshape(per, KROWS, HD)
    for i in range(subs):
        dq = dq + nn(kt_ref[i], ds_ref[i])
    return dq


def forward_theirs(
    theirs, q_ref, qq_ref, m1_ref, sums1_ref, acc1_ref,
    w_ref, pieces, cross, o_ref, share_ref,
    m_ref, sums_ref, acc_ref, stage, *scratch
):
    def close(t):
        rows = slice(QT * t, QT * t + QT)
        top = jnp.maximum(m1_ref[t], m_ref[t])
        f1 = jnp.exp2((m1_ref[t] - top) * EXP_SCALE)
        f2 = jnp.exp2((m_ref[t] - top) * EXP_SCALE)
        sums = sums1_ref[t] * f1 + sums_ref[t] * f2
        inverse = 1.0 / sums[0:1]
        s1, s2 = f1 * inverse, f2 * inverse
        share_ref[0, t] = s1
        share_ref[1, t] = s2
        both = acc1_ref[t] * s1 + acc_ref[t] * s2
        tangent = both[HD:] - (sums[1:2] * inverse) * both[0:HD]
        o_ref[t, 0:HD, :] = both[0:HD].astype(BF).astype(F32)
        o_ref[t, HD:, :] = tangent.astype(BF).astype(F32)
        stage[rows, :] = o_ref[t].T

    forward(
        theirs, q_ref, qq_ref, w_ref, m_ref, sums_ref, acc_ref, *scratch, close=close
    )
    for s in range(pieces.shape[0]):
        low = PIECE * s
        pieces[s] = stage[low : low + PIECE, :].astype(BF)
        cross[s] = stage[low + 8 : low + PIECE, :].astype(BF)


def backward_theirs(
    theirs, gap_kept, gap_got, q_ref, o_ref, w_ref, share_ref,
    dst, cot_ref, inner_ref, dq_ref, stage, *scratch
):
    first = part_here() == 0
    for s in range(gap_kept.shape[0]):
        low = PIECE * s
        own, got = gap_kept[s].astype(F32), gap_got[s].astype(F32)
        stage[low : low + 8, :] = own[0:8]
        stage[low + 8 : low + 16, :] = jnp.where(first, own[8:16], got[0:8])
        stage[low + 16 : low + 24, :] = got[8:16]
    for t in range(q_ref.shape[0]):
        rows = slice(QT * t, QT * t + QT)
        place = lax.rem(QT * t + lax.broadcasted_iota(jnp.int32, (1, QT), 1), PIECE)
        short = jnp.where(place >= 16, 1, 0) * jnp.where(part_here() == 1, 1, 0)
        mask = jnp.where(short == 1, 0.0, 1.0)
        cot = (LOSS * (stage[rows, :].T + o_ref[t, HD:, :])) * mask
        cot = cot.astype(BF).astype(F32)
        inner_ref[t] = jnp.sum(cot * o_ref[t, 0:HD, :], axis=0, keepdims=True)
        cot_ref[rows, :] = cot.T.astype(BF)
    dq_ref[...] = backward(
        rows_of(theirs, 0), rows_of(theirs, 2 * KROWS),
        q_ref, cot_ref, inner_ref, w_ref, share_ref, 1, dst, jnp.zeros(dq_ref.shape, F32), *scratch,
    )


def backward_mine(
    mine, q_ref, cot_ref, inner_ref, w_ref, share_ref, dq_ref, out, dq_out, stage, *scratch
):
    dq = backward(
        rows_of(mine, 0), rows_of(mine, 2 * KROWS),
        q_ref, cot_ref, inner_ref, w_ref, share_ref, 0, out, dq_ref[...], *scratch,
    )
    stage[...] = (dq * INV).T
    for s in range(out.shape[0]):
        dq_out[s] = stage[PIECE * s : PIECE * s + PIECE, :].astype(BF)


def gather_out(mine, dq, pieces, got, theirs, out):
    first = part_here() == 0
    for s in range(out.shape[0]):
        both = (mine[s].astype(F32) + theirs[s].astype(F32)).astype(BF)
        out[s, 0:64, :] = both[:, 0:HD]
        out[s, 64:128, :] = both[:, HD:]
        second = jnp.where(first, pieces[s, 8:16, :].astype(F32), got[s, 0:8, :].astype(F32)).astype(BF)
        for low, lanes in ((128, slice(0, HD)), (152, slice(HD, 2 * HD))):
            out[s, low : low + 8, :] = pieces[s, 0:8, lanes]
            out[s, low + 8 : low + 16, :] = second[:, lanes]
            out[s, low + 16 : low + 24, :] = got[s, 8:16, lanes]
        out[s, 176:200, :] = dq[s]


def unpack_grads(r_ref, sent, kept, f_ref):
    half = f_ref.shape[3] // HD
    for head in range(2 * half):
        at, cols = head // half, slice((head % half) * HD, (head % half + 1) * HD)
        first = PARTS * head
        for array, low in ((1, 0), (2, KROWS)):
            rows = slice(low, low + KROWS)
            both = sum(r_ref[first + part, rows, :].astype(F32) for part in range(PARTS))
            f_ref[at, array, :, cols] = both.astype(BF)
        for part in range(PARTS):
            for place, eight in enumerate(EIGHTS[part]):
                if eight is not None:
                    row, low = 8 * eight, 176 + 8 * place
                    f_ref[at, 0, row : row + 8, cols] = r_ref[first + part, low : low + 8, :]
    sent[...] = f_ref[1 - core()]
    kept[...] = f_ref[core()]


def place_grads(piece, who, outs, sems):
    return [
        pltpu.make_async_copy(
            piece.at[at, 32 * half : 32 * half + 32, :],
            ref.at[pl.ds(half_row(half, who), 32), :],
            sems.at[at, half],
        )
        for at, ref in enumerate(outs)
        for half in range(2)
    ]


def finish_outs(r_ref, kept, primal, tangent, dq, dk, dv, o_ref, sems):
    copies = place_grads(kept, core(), (dq, dk, dv), sems)
    for copy in copies:
        copy.start()
    wide = o_ref.shape[3]
    for head in range(wide // HD):
        cols = slice(head * HD, head * HD + HD)
        for part in range(PARTS):
            for place, unit in enumerate(GAPS[part]):
                if unit is None:
                    continue
                which, eight = unit
                for side in range(2):
                    low = 128 + PIECE * side + 8 * place
                    o_ref[which, side, 8 * eight : 8 * eight + 8, cols] = r_ref[
                        PARTS * head + part, low : low + 8, :
                    ]
    for side, ref in enumerate((primal, tangent)):
        for which, who in enumerate((group(), 1 - group())):
            ref[:, pl.ds(pl.multiple_of(wide * who, HD), wide)] = o_ref[which, side]
    for copy in copies:
        copy.wait()


def finish_grads(got, dq_in, dk_in, dv_in, dq, dk, dv, sems):
    run_all(place_grads(got, 1 - core(), (dq, dk, dv), sems))


def shape(*dims, dtype=BF):
    return jax.ShapeDtypeStruct(dims, dtype)


SWAP = [(0, 1), (1, 0)]
BLOCK_AXES = ("zl", "y", "x")


def exchange(array):
    return lax.all_to_all(array, BLOCK_AXES, 0, 0, tiled=True)


def swap(array, axis):
    return lax.ppermute(array, axis, SWAP)


def attention(chips, mine):
    length, tiles = chips * KROWS, chips * PIECE // QT
    rows, subs = tiles * QT, length // SUB
    flops = 2 * length * rows * HD
    gpiece = shape(chips, 16, HD)
    theirs = swap(mine, "c")
    q, qq = shape(tiles, QT, HD), shape(tiles, QT, 2 * HD)
    w = shape(tiles, length, QT)
    stats, sums, acc = (shape(tiles, n, QT, dtype=F32) for n in (1, 2, 2 * HD))
    tiles_of = (pltpu.VMEM(w.shape, BF), pltpu.SemaphoreType.DMA((tiles,)))
    scratch = (
        pltpu.VMEM((2, length, QT), F32),
        pltpu.VMEM((2, length, QT), BF),
        pltpu.VMEM((length, 2 * HD), BF),
        pltpu.VMEM((2 * HD, length), BF),
    )
    back_scratch = (
        pltpu.VMEM((subs, HD, SUB), BF),
        pltpu.VMEM((subs, SUB, rows), BF),
        pltpu.VMEM((SUB, rows), BF),
    )
    stage = pltpu.VMEM((rows, 2 * HD), F32)
    q, qq, w1, m1, sums1, acc1, gap_sent, gap_kept = call(
        forward_mine,
        [(q, VMEM), (qq, VMEM), (w, HBM), (stats, VMEM), (sums, VMEM), (acc, VMEM)]
        + [(gpiece, VMEM)] * 2,
        [VMEM],
        30,
        (stage,) + tiles_of + scratch,
        6 * flops, length * rows, 7_000_000,
    )(mine)
    gap_got = swap(gap_sent, "zh")
    key_piece = shape(chips, KROWS, 2 * HD)
    w2, pieces, cross, o, share = call(
        forward_theirs,
        [
            (w, VMEM), (shape(chips, PIECE, 2 * HD), VMEM), (shape(chips, 16, 2 * HD), VMEM),
            (acc, VMEM), (shape(2, tiles, 1, QT, dtype=F32), VMEM),
        ],
        [VMEM] * 6,
        30,
        (
            pltpu.VMEM(stats.shape, F32), pltpu.VMEM(sums.shape, F32), pltpu.VMEM(acc.shape, F32),
            stage,
        ) + scratch,
        6 * flops, length * rows, 7_000_000,
    )(theirs, q, qq, m1, sums1, acc1)
    cross = swap(cross, "zh")
    dst, cot, inner, dq = call(
        backward_theirs,
        [
            (key_piece, VMEM), (shape(rows, HD), VMEM), (stats, VMEM),
            (shape(HD, rows, dtype=F32), VMEM),
        ],
        [VMEM] * 7,
        30,
        (pltpu.VMEM((rows, HD), F32),) + back_scratch,
        8 * flops, 0, 7_000_000,
    )(theirs, gap_kept, gap_got, q, o, w2, share)
    partner = swap(dst, "c")
    out, dq = call(
        backward_mine,
        [(key_piece, VMEM), (shape(chips, PIECE, HD), VMEM)],
        [VMEM] * 7,
        30,
        (pltpu.VMEM((rows, HD), F32),) + back_scratch,
        8 * flops, 0, 7_000_000,
    )(mine, q, cot, inner, w1, share, dq)
    return call(gather_out, [(shape(chips, 200, HD), VMEM)], [VMEM] * 5, 8)(
        out, dq, pieces, cross, partner
    )[0]


def per_device(q, k, v, tq, tk, tv, gap):
    chips = lax.axis_size(BLOCK_AXES)
    local, feat = q.shape
    wide = gap.shape[1] // 2
    piece = shape(6, KROWS, feat)
    arrays = [
        pltpu.with_memory_space_constraint(one, pltpu.HBM) for one in (q, k, v, tq, tk, tv, gap)
    ]
    sems = pltpu.SemaphoreType.DMA((6, 2))
    sent = call(send_tokens, [(piece, VMEM)], [HBM] * 6, 2, (sems,))(*arrays[:6])[0]
    got = swap(sent, "c")
    kept, gap_here = call(
        keep_tokens,
        [(piece, VMEM), (shape(2, 32, wide), VMEM)],
        [HBM] * 7,
        2,
        (sems, pltpu.SemaphoreType.DMA((2,))),
    )(*arrays)
    packed = call(
        pack_heads,
        [(shape(chips, SLOT, HD), VMEM)],
        [VMEM] * 3,
        8,
        (pltpu.VMEM((2,) + piece.shape, BF),),
    )(kept, got, gap_here)[0]
    mine = exchange(packed)

    back = exchange(attention(chips, mine))

    fpiece = shape(3, KROWS, feat)
    sent, kept = call(
        unpack_grads, [(fpiece, VMEM), (fpiece, VMEM)], [VMEM], 8,
        (pltpu.VMEM((2,) + fpiece.shape, BF),),
    )(back)
    got = swap(sent, "c")
    small, large = shape(32, 2 * wide), shape(local, feat)
    sems = pltpu.SemaphoreType.DMA((3, 2))
    primal, tangent, *grads = call(
        finish_outs, [(small, VMEM)] * 2 + [(large, HBM)] * 3, [VMEM] * 2, 8,
        (pltpu.VMEM((2, 2, 32, wide), BF), sems),
    )(back, kept)
    dq, dk, dv = call(
        finish_grads, [(large, HBM)] * 3, [VMEM] + [HBM] * 3, 4, (sems,), aliases={1: 0, 2: 1, 3: 2}
    )(got, *grads)
    return primal, tangent, dq, dk, dv


def solution(mesh):
    sizes = (2, 4, 4, 2, 2)
    inner = Mesh(mesh.devices.reshape(sizes), BLOCK_AXES + ("zh", "c"))
    both = P(BLOCK_AXES, ("zh", "c"))
    rows = P(BLOCK_AXES + ("zh", "c"), None)

    return jax.shard_map(
        per_device,
        mesh=inner,
        in_specs=(both,) * 6 + (rows,),
        out_specs=(rows, rows, both, both, both),
        check_vma=False,
    )
```

```python
import math

import jax
import jax.numpy as jnp
from jax import lax
from jax.experimental import pallas as pl
from jax.experimental.pallas import tpu as pltpu
from jax.sharding import Mesh, PartitionSpec as P


BF = jnp.bfloat16
F32 = jnp.float32
HD = 128
LOSS = 64.0
PARTS = 3
PIECE = 24
EIGHTS = ((0, 1, 4), (2, 5, None), (3, 6, 7))
GAPS = (((0, 0), (0, 1), (1, 0)), ((0, 2), (1, 1), None), ((0, 3), (1, 2), (1, 3)))
SLOT = 328
KROWS = 64
QT = 256
SUB = 512
INV = 1.0 / math.sqrt(HD)
EXP_SCALE = INV * math.log2(math.e)
VMEM = pl.BlockSpec(memory_space=pltpu.VMEM)
HBM = pl.BlockSpec(memory_space=pltpu.HBM)
ANY = pl.BlockSpec(memory_space=pl.ANY)


def call(body, outs, ins, limit, scratch=(), flops=0, exps=0, moved=1_000_000, aliases=None):
    return pl.pallas_call(
        body,
        out_shape=[
            pltpu.HBM(one.shape, one.dtype) if place is HBM else one for one, place in outs
        ],
        in_specs=ins,
        out_specs=[place for _, place in outs],
        scratch_shapes=list(scratch),
        input_output_aliases=aliases or {},
        compiler_params=pltpu.CompilerParams(vmem_limit_bytes=limit * 1024 * 1024),
        cost_estimate=pl.CostEstimate(flops=flops, bytes_accessed=moved, transcendentals=exps),
    )


def nt(a, b):
    return lax.dot_general(a, b, (((1,), (1,)), ((), ())), preferred_element_type=F32)


def nn(a, b):
    return lax.dot_general(a, b, (((1,), (0,)), ((), ())), preferred_element_type=F32)


def core():
    return lax.axis_index("c")


def group():
    return lax.axis_index("zh")


def half_row(half, who):
    return pl.multiple_of(64 * lax.rem(group() + half, 2) + 32 * who, 32)


def part_here():
    place = lax.axis_index("x") * 8 + lax.axis_index("zl") * 4 + lax.axis_index("y")
    return lax.rem(place, PARTS)


def split_tokens(arrays, dst, who, sems):
    return [
        pltpu.make_async_copy(
            ref.at[pl.ds(half_row(half, who), 32), :],
            dst.at[at, 32 * half : 32 * half + 32, :],
            sems.at[at, half],
        )
        for at, ref in enumerate(arrays)
        for half in range(2)
    ]


def run_all(copies):
    for copy in copies:
        copy.start()
    for copy in copies:
        copy.wait()


def send_tokens(*refs):
    *arrays, sent, sems = refs
    run_all(split_tokens(arrays, sent, 1 - core(), sems))


def keep_tokens(*refs):
    *arrays, gap, kept, gap_here, sems, gap_sems = refs
    copies = split_tokens(arrays, kept, core(), sems)
    wide = gap_here.shape[2]
    for at, who in enumerate((group(), 1 - group())):
        lanes = pl.ds(pl.multiple_of(who * wide, HD), wide)
        copies.append(pltpu.make_async_copy(gap.at[:, lanes], gap_here.at[at], gap_sems.at[at]))
    run_all(copies)


def pack_heads(kept, got, gap, out, e_ref):
    e_ref[core()] = kept[...]
    e_ref[1 - core()] = got[...]
    half = e_ref.shape[3] // HD
    zero = jnp.zeros((8, HD), BF)
    for chip in range(out.shape[0]):
        head, part = chip // PARTS, chip % PARTS
        if head >= 2 * half:
            out[chip] = jnp.zeros(out.shape[1:], BF)
            continue
        at, cols = head // half, slice((head % half) * HD, (head % half + 1) * HD)
        for to, array in enumerate((1, 4, 2, 5)):
            out[chip, KROWS * to : KROWS * to + KROWS, :] = e_ref[at, array, :, cols]
        gcols = slice(head * HD, head * HD + HD)
        for to in range(3):
            eight = EIGHTS[part][to]
            for low, array in ((256, 0), (280, 3)):
                rows = slice(low + 8 * to, low + 8 * to + 8)
                if eight is None:
                    out[chip, rows, :] = zero
                else:
                    out[chip, rows, :] = e_ref[at, array, 8 * eight : 8 * eight + 8, cols]
            rows = slice(304 + 8 * to, 312 + 8 * to)
            if GAPS[part][to] is None:
                out[chip, rows, :] = zero
            else:
                which, eight = GAPS[part][to]
                out[chip, rows, :] = gap[which, 8 * eight : 8 * eight + 8, gcols]


def fold(x, op):
    return op(x.reshape(x.shape[0] // 8, 8, x.shape[1]), axis=0)


def forward(keys, q_ref, qq_ref, w_ref, m_ref, sums_ref, acc_ref, s_ref, wt_ref, kk_ref, vt_ref,
            done=None, close=None):
    tiles = q_ref.shape[0]
    per = SUB // KROWS
    subs = kk_ref.shape[0] // SUB
    ats = [slice(SUB * i, SUB * i + SUB) for i in range(subs)]

    def scores(t, i, peak):
        s = nt(kk_ref[ats[i], 0:HD], q_ref[t])
        s_ref[t % 2, ats[i], :] = s
        return jnp.maximum(peak, fold(s, jnp.max))

    def values(t, i):
        both = nn(vt_ref[:, ats[i]], w_ref[t, ats[i], :])
        tan = nn(vt_ref[0:HD, ats[i]], wt_ref[t % 2, ats[i], :]) * INV
        if i == 0:
            acc_ref[t, 0:HD, :] = both[0:HD]
            acc_ref[t, HD:, :] = both[HD:] + tan
        else:
            acc_ref[t, 0:HD, :] += both[0:HD]
            acc_ref[t, HD:, :] += both[HD:] + tan

    lowest = jnp.full((8, QT), -jnp.inf, F32)
    peak = lowest
    for i in range(subs):
        slots = slice(per * i, per * i + per)
        for half in range(2):
            lanes = slice(HD * half, HD * half + HD)
            kk_ref[ats[i], lanes] = keys[slots, KROWS * half : KROWS * half + KROWS, :].reshape(SUB, HD)
            v = keys[slots, KROWS * (2 + half) : KROWS * (3 + half), :].reshape(SUB, HD)
            vt_ref[lanes, ats[i]] = v.astype(F32).T.astype(BF)
        peak = scores(0, i, peak)
    for t in range(tiles):
        top = jnp.max(peak, axis=0, keepdims=True)
        m_ref[t] = top
        peak = lowest
        total = jnp.zeros((8, QT), F32)
        tan_total = jnp.zeros((8, QT), F32)
        for i in range(subs):
            w = jnp.exp2((s_ref[t % 2, ats[i], :] - top) * EXP_SCALE)
            wt = w * nt(kk_ref[ats[i], :], qq_ref[t])
            total = total + fold(w, jnp.sum)
            tan_total = tan_total + fold(wt, jnp.sum)
            w_ref[t, ats[i], :] = w.astype(BF)
            wt_ref[t % 2, ats[i], :] = wt.astype(BF)
            if t + 1 < tiles:
                peak = scores(t + 1, i, peak)
            if t > 0:
                values(t - 1, i)
        sums_ref[t, 0:1, :] = jnp.sum(total, axis=0, keepdims=True)
        sums_ref[t, 1:2, :] = jnp.sum(tan_total, axis=0, keepdims=True) * INV
        if done is not None:
            done(t)
        if close is not None and t > 0:
            close(t - 1)
    for i in range(subs):
        values(tiles - 1, i)
    if close is not None:
        close(tiles - 1)


def forward_mine(
    mine, q_ref, qq_ref, w_hbm, m_ref, sums_ref, acc_ref, gap_sent, gap_kept,
    stage, w_ref, sems, *scratch
):
    for s in range(mine.shape[0]):
        gap_sent[s] = mine[s, 312:328, :]
        gap_kept[s] = mine[s, 304:320, :]
        stage[PIECE * s : PIECE * s + PIECE, 0:HD] = mine[s, 256:280, :].astype(F32)
        stage[PIECE * s : PIECE * s + PIECE, HD:] = mine[s, 280:304, :].astype(F32)
    tiles = q_ref.shape[0]
    for t in range(tiles):
        rows = slice(QT * t, QT * t + QT)
        q_ref[t] = stage[rows, 0:HD].astype(BF)
        qq_ref[t, :, 0:HD] = stage[rows, HD:].astype(BF)
        qq_ref[t, :, HD:] = stage[rows, 0:HD].astype(BF)
    copies = [pltpu.make_async_copy(w_ref.at[t], w_hbm.at[t], sems.at[t]) for t in range(tiles)]
    forward(
        mine, q_ref, qq_ref, w_ref, m_ref, sums_ref, acc_ref, *scratch,
        done=lambda t: copies[t].start(),
    )
    for copy in copies:
        copy.wait()


def rows_of(ref, low):
    return lambda at, slots: ref[slots, low : low + KROWS, :].reshape(SUB, HD)


def backward(key, value, q_ref, cot_ref, inner_ref, w_ref, share_ref, side, dst, dq, kt_ref, ds_ref, p_ref):
    tiles = q_ref.shape[0]
    per = SUB // KROWS
    subs = ds_ref.shape[0]
    q_all = q_ref[...].reshape(tiles * QT, HD)
    for i in range(subs):
        at, slots = slice(SUB * i, SUB * i + SUB), slice(per * i, per * i + per)
        v = value(at, slots)
        kt_ref[i] = key(at, slots).astype(F32).T.astype(BF)
        for t in range(tiles):
            cols = slice(QT * t, QT * t + QT)
            p = w_ref[t, at, :].astype(F32) * share_ref[side, t]
            ds = p * (nt(v, cot_ref[cols, :]) - inner_ref[t])
            p_ref[:, cols] = p.astype(BF)
            ds_ref[i, :, cols] = ds.astype(BF)
        dk = nn(ds_ref[i], q_all) * INV
        dv = nn(p_ref[...], cot_ref[...])
        dst[slots, 0:KROWS, 0:HD] = dk.astype(BF).reshape(per, KROWS, HD)
        dst[slots, 0:KROWS, HD:] = dv.astype(BF).reshape(per, KROWS, HD)
    for i in range(subs):
        dq = dq + nn(kt_ref[i], ds_ref[i])
    return dq


def forward_theirs(
    theirs, q_ref, qq_ref, m1_ref, sums1_ref, acc1_ref,
    w_ref, pieces, cross, o_ref, share_ref,
    m_ref, sums_ref, acc_ref, stage, *scratch
):
    def close(t):
        rows = slice(QT * t, QT * t + QT)
        top = jnp.maximum(m1_ref[t], m_ref[t])
        f1 = jnp.exp2((m1_ref[t] - top) * EXP_SCALE)
        f2 = jnp.exp2((m_ref[t] - top) * EXP_SCALE)
        sums = sums1_ref[t] * f1 + sums_ref[t] * f2
        inverse = 1.0 / sums[0:1]
        s1, s2 = f1 * inverse, f2 * inverse
        share_ref[0, t] = s1
        share_ref[1, t] = s2
        both = acc1_ref[t] * s1 + acc_ref[t] * s2
        tangent = both[HD:] - (sums[1:2] * inverse) * both[0:HD]
        o_ref[t, 0:HD, :] = both[0:HD].astype(BF).astype(F32)
        o_ref[t, HD:, :] = tangent.astype(BF).astype(F32)
        stage[rows, :] = o_ref[t].T

    forward(
        theirs, q_ref, qq_ref, w_ref, m_ref, sums_ref, acc_ref, *scratch, close=close
    )
    for s in range(pieces.shape[0]):
        low = PIECE * s
        pieces[s] = stage[low : low + PIECE, :].astype(BF)
        cross[s] = stage[low + 8 : low + PIECE, :].astype(BF)


def backward_theirs(
    theirs, gap_kept, gap_got, q_ref, o_ref, w_ref, share_ref,
    dst, cot_ref, inner_ref, dq_ref, stage, *scratch
):
    first = part_here() == 0
    for s in range(gap_kept.shape[0]):
        low = PIECE * s
        own, got = gap_kept[s].astype(F32), gap_got[s].astype(F32)
        stage[low : low + 8, :] = own[0:8]
        stage[low + 8 : low + 16, :] = jnp.where(first, own[8:16], got[0:8])
        stage[low + 16 : low + 24, :] = got[8:16]
    for t in range(q_ref.shape[0]):
        rows = slice(QT * t, QT * t + QT)
        place = lax.rem(QT * t + lax.broadcasted_iota(jnp.int32, (1, QT), 1), PIECE)
        short = jnp.where(place >= 16, 1, 0) * jnp.where(part_here() == 1, 1, 0)
        mask = jnp.where(short == 1, 0.0, 1.0)
        cot = (LOSS * (stage[rows, :].T + o_ref[t, HD:, :])) * mask
        cot = cot.astype(BF).astype(F32)
        inner_ref[t] = jnp.sum(cot * o_ref[t, 0:HD, :], axis=0, keepdims=True)
        cot_ref[rows, :] = cot.T.astype(BF)
    dq_ref[...] = backward(
        rows_of(theirs, 0), rows_of(theirs, 2 * KROWS),
        q_ref, cot_ref, inner_ref, w_ref, share_ref, 1, dst, jnp.zeros(dq_ref.shape, F32), *scratch,
    )


def backward_mine(
    mine, q_ref, cot_ref, inner_ref, w_ref, share_ref, dq_ref, out, dq_out, stage, *scratch
):
    dq = backward(
        rows_of(mine, 0), rows_of(mine, 2 * KROWS),
        q_ref, cot_ref, inner_ref, w_ref, share_ref, 0, out, dq_ref[...], *scratch,
    )
    stage[...] = (dq * INV).T
    for s in range(out.shape[0]):
        dq_out[s] = stage[PIECE * s : PIECE * s + PIECE, :].astype(BF)


def gather_out(mine, dq, pieces, got, theirs, out):
    first = part_here() == 0
    for s in range(out.shape[0]):
        both = (mine[s].astype(F32) + theirs[s].astype(F32)).astype(BF)
        out[s, 0:64, :] = both[:, 0:HD]
        out[s, 64:128, :] = both[:, HD:]
        second = jnp.where(first, pieces[s, 8:16, :].astype(F32), got[s, 0:8, :].astype(F32)).astype(BF)
        for low, lanes in ((128, slice(0, HD)), (152, slice(HD, 2 * HD))):
            out[s, low : low + 8, :] = pieces[s, 0:8, lanes]
            out[s, low + 8 : low + 16, :] = second[:, lanes]
            out[s, low + 16 : low + 24, :] = got[s, 8:16, lanes]
        out[s, 176:200, :] = dq[s]


def unpack_grads(r_ref, sent, kept, f_ref):
    half = f_ref.shape[3] // HD
    for head in range(2 * half):
        at, cols = head // half, slice((head % half) * HD, (head % half + 1) * HD)
        first = PARTS * head
        for array, low in ((1, 0), (2, KROWS)):
            rows = slice(low, low + KROWS)
            both = sum(r_ref[first + part, rows, :].astype(F32) for part in range(PARTS))
            f_ref[at, array, :, cols] = both.astype(BF)
        for part in range(PARTS):
            for place, eight in enumerate(EIGHTS[part]):
                if eight is not None:
                    row, low = 8 * eight, 176 + 8 * place
                    f_ref[at, 0, row : row + 8, cols] = r_ref[first + part, low : low + 8, :]
    sent[...] = f_ref[1 - core()]
    kept[...] = f_ref[core()]


def place_grads(piece, who, outs, sems):
    return [
        pltpu.make_async_copy(
            piece.at[at, 32 * half : 32 * half + 32, :],
            ref.at[pl.ds(half_row(half, who), 32), :],
            sems.at[at, half],
        )
        for at, ref in enumerate(outs)
        for half in range(2)
    ]


def finish_outs(r_ref, kept, primal, tangent, dq, dk, dv, o_ref, sems, out_sems):
    copies = place_grads(kept, core(), (dq, dk, dv), sems)
    for copy in copies:
        copy.start()
    wide = o_ref.shape[3]
    for head in range(wide // HD):
        cols = slice(head * HD, head * HD + HD)
        for part in range(PARTS):
            for place, unit in enumerate(GAPS[part]):
                if unit is None:
                    continue
                which, eight = unit
                for side in range(2):
                    low = 128 + PIECE * side + 8 * place
                    o_ref[which, side, 8 * eight : 8 * eight + 8, cols] = r_ref[
                        PARTS * head + part, low : low + 8, :
                    ]
    for side, ref in enumerate((primal, tangent)):
        for which, who in enumerate((group(), 1 - group())):
            lanes = pl.ds(pl.multiple_of(wide * who, HD), wide)
            copies.append(
                pltpu.make_async_copy(o_ref.at[which, side], ref.at[:, lanes], out_sems.at[which, side])
            )
            copies[-1].start()
    for copy in copies:
        copy.wait()


def finish_grads(got, dq_in, dk_in, dv_in, dq, dk, dv, sems):
    run_all(place_grads(got, 1 - core(), (dq, dk, dv), sems))


def shape(*dims, dtype=BF):
    return jax.ShapeDtypeStruct(dims, dtype)


SWAP = [(0, 1), (1, 0)]
BLOCK_AXES = ("zl", "y", "x")
CHIP_AXES = ("x", "zl", "y")


def exchange(array):
    return lax.all_to_all(array, CHIP_AXES, 0, 0, tiled=True)


def swap(array, axis):
    return lax.ppermute(array, axis, SWAP)


def attention(chips, mine):
    length, tiles = chips * KROWS, chips * PIECE // QT
    rows, subs = tiles * QT, length // SUB
    flops = 2 * length * rows * HD
    gpiece = shape(chips, 16, HD)
    theirs = swap(mine, "c")
    q, qq = shape(tiles, QT, HD), shape(tiles, QT, 2 * HD)
    w = shape(tiles, length, QT)
    stats, sums, acc = (shape(tiles, n, QT, dtype=F32) for n in (1, 2, 2 * HD))
    tiles_of = (pltpu.VMEM(w.shape, BF), pltpu.SemaphoreType.DMA((tiles,)))
    scratch = (
        pltpu.VMEM((2, length, QT), F32),
        pltpu.VMEM((2, length, QT), BF),
        pltpu.VMEM((length, 2 * HD), BF),
        pltpu.VMEM((2 * HD, length), BF),
    )
    back_scratch = (
        pltpu.VMEM((subs, HD, SUB), BF),
        pltpu.VMEM((subs, SUB, rows), BF),
        pltpu.VMEM((SUB, rows), BF),
    )
    stage = pltpu.VMEM((rows, 2 * HD), F32)
    q, qq, w1, m1, sums1, acc1, gap_sent, gap_kept = call(
        forward_mine,
        [(q, VMEM), (qq, VMEM), (w, HBM), (stats, VMEM), (sums, VMEM), (acc, VMEM)]
        + [(gpiece, VMEM)] * 2,
        [VMEM],
        30,
        (stage,) + tiles_of + scratch,
        6 * flops, length * rows, 7_000_000,
    )(mine)
    gap_got = swap(gap_sent, "zh")
    key_piece = shape(chips, KROWS, 2 * HD)
    w2, pieces, cross, o, share = call(
        forward_theirs,
        [
            (w, VMEM), (shape(chips, PIECE, 2 * HD), VMEM), (shape(chips, 16, 2 * HD), VMEM),
            (acc, VMEM), (shape(2, tiles, 1, QT, dtype=F32), VMEM),
        ],
        [VMEM] * 6,
        30,
        (
            pltpu.VMEM(stats.shape, F32), pltpu.VMEM(sums.shape, F32), pltpu.VMEM(acc.shape, F32),
            stage,
        ) + scratch,
        6 * flops, length * rows, 7_000_000,
    )(theirs, q, qq, m1, sums1, acc1)
    cross = swap(cross, "zh")
    dst, cot, inner, dq = call(
        backward_theirs,
        [
            (key_piece, VMEM), (shape(rows, HD), VMEM), (stats, VMEM),
            (shape(HD, rows, dtype=F32), VMEM),
        ],
        [VMEM] * 7,
        30,
        (pltpu.VMEM((rows, HD), F32),) + back_scratch,
        8 * flops, 0, 7_000_000,
    )(theirs, gap_kept, gap_got, q, o, w2, share)
    partner = swap(dst, "c")
    out, dq = call(
        backward_mine,
        [(key_piece, VMEM), (shape(chips, PIECE, HD), VMEM)],
        [VMEM] * 7,
        30,
        (pltpu.VMEM((rows, HD), F32),) + back_scratch,
        8 * flops, 0, 7_000_000,
    )(mine, q, cot, inner, w1, share, dq)
    return call(gather_out, [(shape(chips, 200, HD), VMEM)], [VMEM] * 5, 8)(
        out, dq, pieces, cross, partner
    )[0]


def per_device(q, k, v, tq, tk, tv, gap):
    chips = lax.axis_size(BLOCK_AXES)
    local, feat = q.shape
    wide = gap.shape[1] // 2
    piece = shape(6, KROWS, feat)
    arrays = [
        pltpu.with_memory_space_constraint(one, pltpu.HBM) for one in (q, k, v, tq, tk, tv, gap)
    ]
    sems = pltpu.SemaphoreType.DMA((6, 2))
    sent = call(send_tokens, [(piece, VMEM)], [HBM] * 6, 2, (sems,))(*arrays[:6])[0]
    got = swap(sent, "c")
    kept, gap_here = call(
        keep_tokens,
        [(piece, VMEM), (shape(2, 32, wide), VMEM)],
        [HBM] * 7,
        2,
        (sems, pltpu.SemaphoreType.DMA((2,))),
    )(*arrays)
    packed = call(
        pack_heads,
        [(shape(chips, SLOT, HD), VMEM)],
        [VMEM] * 3,
        8,
        (pltpu.VMEM((2,) + piece.shape, BF),),
    )(kept, got, gap_here)[0]
    mine = exchange(packed)

    back = exchange(attention(chips, mine))

    fpiece = shape(3, KROWS, feat)
    sent, kept = call(
        unpack_grads, [(fpiece, VMEM), (fpiece, VMEM)], [VMEM], 8,
        (pltpu.VMEM((2,) + fpiece.shape, BF),),
    )(back)
    got = swap(sent, "c")
    small, large = shape(32, 2 * wide), shape(local, feat)
    sems = pltpu.SemaphoreType.DMA((3, 2))
    primal, tangent, *grads = call(
        finish_outs, [(small, HBM)] * 2 + [(large, HBM)] * 3, [VMEM] * 2, 8,
        (pltpu.VMEM((2, 2, 32, wide), BF), sems, pltpu.SemaphoreType.DMA((2, 2))),
    )(back, kept)
    dq, dk, dv = call(
        finish_grads, [(large, HBM)] * 3, [VMEM] + [HBM] * 3, 4, (sems,), aliases={1: 0, 2: 1, 3: 2}
    )(got, *grads)
    return primal, tangent, dq, dk, dv


def solution(mesh):
    sizes = (2, 4, 4, 2, 2)
    inner = Mesh(mesh.devices.reshape(sizes), BLOCK_AXES + ("zh", "c"))
    both = P(BLOCK_AXES, ("zh", "c"))
    rows = P(BLOCK_AXES + ("zh", "c"), None)

    return jax.shard_map(
        per_device,
        mesh=inner,
        in_specs=(both,) * 6 + (rows,),
        out_specs=(rows, rows, both, both, both),
        check_vma=False,
    )
```

```python
import math

import jax
import jax.numpy as jnp
from jax import lax
from jax.experimental import pallas as pl
from jax.experimental.pallas import tpu as pltpu
from jax.sharding import Mesh, PartitionSpec as P


BF = jnp.bfloat16
F32 = jnp.float32
HD = 128
LOSS = 64.0
PARTS = 3
PIECE = 24
EIGHTS = ((0, 1, 4), (2, 5, None), (3, 6, 7))
GAPS = (((0, 0), (0, 1), (1, 0)), ((0, 2), (1, 1), None), ((0, 3), (1, 2), (1, 3)))
SLOT = 328
KROWS = 64
QT = 256
SUB = 512
INV = 1.0 / math.sqrt(HD)
EXP_SCALE = INV * math.log2(math.e)
VMEM = pl.BlockSpec(memory_space=pltpu.VMEM)
HBM = pl.BlockSpec(memory_space=pltpu.HBM)
ANY = pl.BlockSpec(memory_space=pl.ANY)


def call(body, outs, ins, limit, scratch=(), flops=0, exps=0, moved=1_000_000, aliases=None):
    return pl.pallas_call(
        body,
        out_shape=[
            pltpu.HBM(one.shape, one.dtype) if place is HBM else one for one, place in outs
        ],
        in_specs=ins,
        out_specs=[place for _, place in outs],
        scratch_shapes=list(scratch),
        input_output_aliases=aliases or {},
        compiler_params=pltpu.CompilerParams(vmem_limit_bytes=limit * 1024 * 1024),
        cost_estimate=pl.CostEstimate(flops=flops, bytes_accessed=moved, transcendentals=exps),
    )


def nt(a, b):
    return lax.dot_general(a, b, (((1,), (1,)), ((), ())), preferred_element_type=F32)


def nn(a, b):
    return lax.dot_general(a, b, (((1,), (0,)), ((), ())), preferred_element_type=F32)


def core():
    return lax.axis_index("c")


def group():
    return lax.axis_index("zh")


def half_row(half, who):
    return pl.multiple_of(64 * lax.rem(group() + half, 2) + 32 * who, 32)


def part_here():
    place = lax.axis_index("zl") * 16 + lax.axis_index("y") * 4 + lax.axis_index("x")
    return lax.rem(place, PARTS)


def split_tokens(arrays, dst, who, sems):
    return [
        pltpu.make_async_copy(
            ref.at[pl.ds(half_row(half, who), 32), :],
            dst.at[at, 32 * half : 32 * half + 32, :],
            sems.at[at, half],
        )
        for at, ref in enumerate(arrays)
        for half in range(2)
    ]


def run_all(copies):
    for copy in copies:
        copy.start()
    for copy in copies:
        copy.wait()


def send_tokens(*refs):
    *arrays, sent, sems = refs
    run_all(split_tokens(arrays, sent, 1 - core(), sems))


def keep_tokens(*refs):
    *arrays, gap, kept, gap_here, sems, gap_sems = refs
    copies = split_tokens(arrays, kept, core(), sems)
    wide = gap_here.shape[2]
    for at, who in enumerate((group(), 1 - group())):
        lanes = pl.ds(pl.multiple_of(who * wide, HD), wide)
        copies.append(pltpu.make_async_copy(gap.at[:, lanes], gap_here.at[at], gap_sems.at[at]))
    run_all(copies)


def pack_heads(kept, got, gap, out, e_ref):
    e_ref[core()] = kept[...]
    e_ref[1 - core()] = got[...]
    half = e_ref.shape[3] // HD
    zero = jnp.zeros((8, HD), BF)
    for chip in range(out.shape[0]):
        head, part = chip // PARTS, chip % PARTS
        if head >= 2 * half:
            out[chip] = jnp.zeros(out.shape[1:], BF)
            continue
        at, cols = head // half, slice((head % half) * HD, (head % half + 1) * HD)
        for to, array in enumerate((1, 4, 2, 5)):
            out[chip, KROWS * to : KROWS * to + KROWS, :] = e_ref[at, array, :, cols]
        gcols = slice(head * HD, head * HD + HD)
        for to in range(3):
            eight = EIGHTS[part][to]
            for low, array in ((256, 0), (280, 3)):
                rows = slice(low + 8 * to, low + 8 * to + 8)
                if eight is None:
                    out[chip, rows, :] = zero
                else:
                    out[chip, rows, :] = e_ref[at, array, 8 * eight : 8 * eight + 8, cols]
            rows = slice(304 + 8 * to, 312 + 8 * to)
            if GAPS[part][to] is None:
                out[chip, rows, :] = zero
            else:
                which, eight = GAPS[part][to]
                out[chip, rows, :] = gap[which, 8 * eight : 8 * eight + 8, gcols]


def split_gaps(mine, sent, kept, sems):
    run_all(
        [
            pltpu.make_async_copy(mine.at[:, low : low + 16, :], dst, sems.at[at])
            for at, (dst, low) in enumerate(((sent, 312), (kept, 304)))
        ]
    )


def fold(x, op):
    return op(x.reshape(x.shape[0] // 8, 8, x.shape[1]), axis=0)


def forward(keys, q_ref, qq_ref, w_ref, m_ref, sums_ref, acc_ref, s_ref, wt_ref, kk_ref, vt_ref,
            done=None, close=None):
    tiles = q_ref.shape[0]
    per = SUB // KROWS
    subs = kk_ref.shape[0] // SUB
    ats = [slice(SUB * i, SUB * i + SUB) for i in range(subs)]

    def scores(t, i, peak):
        s = nt(kk_ref[ats[i], 0:HD], q_ref[t])
        s_ref[t % 2, ats[i], :] = s
        return jnp.maximum(peak, fold(s, jnp.max))

    def values(t, i):
        both = nn(vt_ref[:, ats[i]], w_ref[t, ats[i], :])
        tan = nn(vt_ref[0:HD, ats[i]], wt_ref[t % 2, ats[i], :]) * INV
        if i == 0:
            acc_ref[t, 0:HD, :] = both[0:HD]
            acc_ref[t, HD:, :] = both[HD:] + tan
        else:
            acc_ref[t, 0:HD, :] += both[0:HD]
            acc_ref[t, HD:, :] += both[HD:] + tan

    lowest = jnp.full((8, QT), -jnp.inf, F32)
    peak = lowest
    for i in range(subs):
        slots = slice(per * i, per * i + per)
        for half in range(2):
            lanes = slice(HD * half, HD * half + HD)
            kk_ref[ats[i], lanes] = keys[slots, KROWS * half : KROWS * half + KROWS, :].reshape(SUB, HD)
            v = keys[slots, KROWS * (2 + half) : KROWS * (3 + half), :].reshape(SUB, HD)
            vt_ref[lanes, ats[i]] = v.astype(F32).T.astype(BF)
        peak = scores(0, i, peak)
    for t in range(tiles):
        top = jnp.max(peak, axis=0, keepdims=True)
        m_ref[t] = top
        peak = lowest
        total = jnp.zeros((8, QT), F32)
        tan_total = jnp.zeros((8, QT), F32)
        for i in range(subs):
            w = jnp.exp2((s_ref[t % 2, ats[i], :] - top) * EXP_SCALE)
            wt = w * nt(kk_ref[ats[i], :], qq_ref[t])
            total = total + fold(w, jnp.sum)
            tan_total = tan_total + fold(wt, jnp.sum)
            w_ref[t, ats[i], :] = w.astype(BF)
            wt_ref[t % 2, ats[i], :] = wt.astype(BF)
            if t + 1 < tiles:
                peak = scores(t + 1, i, peak)
            if t > 0:
                values(t - 1, i)
        sums_ref[t, 0:1, :] = jnp.sum(total, axis=0, keepdims=True)
        sums_ref[t, 1:2, :] = jnp.sum(tan_total, axis=0, keepdims=True) * INV
        if done is not None:
            done(t)
        if close is not None and t > 0:
            close(t - 1)
    for i in range(subs):
        values(tiles - 1, i)
    if close is not None:
        close(tiles - 1)


def forward_mine(mine, q_ref, qq_ref, w_hbm, m_ref, sums_ref, acc_ref, stage, w_ref, sems, *scratch):
    for s in range(mine.shape[0]):
        stage[PIECE * s : PIECE * s + PIECE, 0:HD] = mine[s, 256:280, :].astype(F32)
        stage[PIECE * s : PIECE * s + PIECE, HD:] = mine[s, 280:304, :].astype(F32)
    tiles = q_ref.shape[0]
    for t in range(tiles):
        rows = slice(QT * t, QT * t + QT)
        q_ref[t] = stage[rows, 0:HD].astype(BF)
        qq_ref[t, :, 0:HD] = stage[rows, HD:].astype(BF)
        qq_ref[t, :, HD:] = stage[rows, 0:HD].astype(BF)
    copies = [pltpu.make_async_copy(w_ref.at[t], w_hbm.at[t], sems.at[t]) for t in range(tiles)]
    forward(
        mine, q_ref, qq_ref, w_ref, m_ref, sums_ref, acc_ref, *scratch,
        done=lambda t: copies[t].start(),
    )
    for copy in copies:
        copy.wait()


def rows_of(ref, low):
    return lambda at, slots: ref[slots, low : low + KROWS, :].reshape(SUB, HD)


def backward(key, value, q_ref, cot_ref, inner_ref, w_ref, share_ref, side, dst, dq, kt_ref, ds_ref, p_ref):
    tiles = q_ref.shape[0]
    per = SUB // KROWS
    subs = ds_ref.shape[0]
    q_all = q_ref[...].reshape(tiles * QT, HD)
    for i in range(subs):
        at, slots = slice(SUB * i, SUB * i + SUB), slice(per * i, per * i + per)
        v = value(at, slots)
        kt_ref[i] = key(at, slots).astype(F32).T.astype(BF)
        for t in range(tiles):
            cols = slice(QT * t, QT * t + QT)
            p = w_ref[t, at, :].astype(F32) * share_ref[side, t]
            ds = p * (nt(v, cot_ref[cols, :]) - inner_ref[t])
            p_ref[:, cols] = p.astype(BF)
            ds_ref[i, :, cols] = ds.astype(BF)
        dk = nn(ds_ref[i], q_all) * INV
        dv = nn(p_ref[...], cot_ref[...])
        dst[slots, 0:KROWS, 0:HD] = dk.astype(BF).reshape(per, KROWS, HD)
        dst[slots, 0:KROWS, HD:] = dv.astype(BF).reshape(per, KROWS, HD)
    for i in range(subs):
        dq = dq + nn(kt_ref[i], ds_ref[i])
    return dq


def forward_theirs(
    theirs, q_ref, qq_ref, m1_ref, sums1_ref, acc1_ref,
    w_ref, pieces, cross, o_ref, share_ref,
    m_ref, sums_ref, acc_ref, stage, *scratch
):
    def close(t):
        rows = slice(QT * t, QT * t + QT)
        top = jnp.maximum(m1_ref[t], m_ref[t])
        f1 = jnp.exp2((m1_ref[t] - top) * EXP_SCALE)
        f2 = jnp.exp2((m_ref[t] - top) * EXP_SCALE)
        sums = sums1_ref[t] * f1 + sums_ref[t] * f2
        inverse = 1.0 / sums[0:1]
        s1, s2 = f1 * inverse, f2 * inverse
        share_ref[0, t] = s1
        share_ref[1, t] = s2
        both = acc1_ref[t] * s1 + acc_ref[t] * s2
        tangent = both[HD:] - (sums[1:2] * inverse) * both[0:HD]
        o_ref[t, 0:HD, :] = both[0:HD].astype(BF).astype(F32)
        o_ref[t, HD:, :] = tangent.astype(BF).astype(F32)
        stage[rows, :] = o_ref[t].T

    forward(
        theirs, q_ref, qq_ref, w_ref, m_ref, sums_ref, acc_ref, *scratch, close=close
    )
    for s in range(pieces.shape[0]):
        low = PIECE * s
        pieces[s] = stage[low : low + PIECE, :].astype(BF)
        cross[s] = stage[low + 8 : low + PIECE, :].astype(BF)


def backward_theirs(
    theirs, gap_kept, gap_got, q_ref, o_ref, w_ref, share_ref,
    dst, cot_ref, inner_ref, dq_ref, stage, *scratch
):
    first = part_here() == 0
    for s in range(gap_kept.shape[0]):
        low = PIECE * s
        own, got = gap_kept[s].astype(F32), gap_got[s].astype(F32)
        stage[low : low + 8, :] = own[0:8]
        stage[low + 8 : low + 16, :] = jnp.where(first, own[8:16], got[0:8])
        stage[low + 16 : low + 24, :] = got[8:16]
    for t in range(q_ref.shape[0]):
        rows = slice(QT * t, QT * t + QT)
        place = lax.rem(QT * t + lax.broadcasted_iota(jnp.int32, (1, QT), 1), PIECE)
        short = jnp.where(place >= 16, 1, 0) * jnp.where(part_here() == 1, 1, 0)
        mask = jnp.where(short == 1, 0.0, 1.0)
        cot = (LOSS * (stage[rows, :].T + o_ref[t, HD:, :])) * mask
        cot = cot.astype(BF).astype(F32)
        inner_ref[t] = jnp.sum(cot * o_ref[t, 0:HD, :], axis=0, keepdims=True)
        cot_ref[rows, :] = cot.T.astype(BF)
    dq_ref[...] = backward(
        rows_of(theirs, 0), rows_of(theirs, 2 * KROWS),
        q_ref, cot_ref, inner_ref, w_ref, share_ref, 1, dst, jnp.zeros(dq_ref.shape, F32), *scratch,
    )


def backward_mine(
    mine, q_ref, cot_ref, inner_ref, w_ref, share_ref, dq_ref, out, dq_out, stage, *scratch
):
    dq = backward(
        rows_of(mine, 0), rows_of(mine, 2 * KROWS),
        q_ref, cot_ref, inner_ref, w_ref, share_ref, 0, out, dq_ref[...], *scratch,
    )
    stage[...] = (dq * INV).T
    for s in range(out.shape[0]):
        dq_out[s] = stage[PIECE * s : PIECE * s + PIECE, :].astype(BF)


def gather_out(mine, dq, pieces, got, theirs, out):
    first = part_here() == 0
    for s in range(out.shape[0]):
        both = (mine[s].astype(F32) + theirs[s].astype(F32)).astype(BF)
        out[s, 0:64, :] = both[:, 0:HD]
        out[s, 64:128, :] = both[:, HD:]
        second = jnp.where(first, pieces[s, 8:16, :].astype(F32), got[s, 0:8, :].astype(F32)).astype(BF)
        for low, lanes in ((128, slice(0, HD)), (152, slice(HD, 2 * HD))):
            out[s, low : low + 8, :] = pieces[s, 0:8, lanes]
            out[s, low + 8 : low + 16, :] = second[:, lanes]
            out[s, low + 16 : low + 24, :] = got[s, 8:16, lanes]
        out[s, 176:200, :] = dq[s]


def unpack_grads(r_ref, sent, kept, f_ref):
    half = f_ref.shape[3] // HD
    for head in range(2 * half):
        at, cols = head // half, slice((head % half) * HD, (head % half + 1) * HD)
        first = PARTS * head
        for array, low in ((1, 0), (2, KROWS)):
            rows = slice(low, low + KROWS)
            both = sum(r_ref[first + part, rows, :].astype(F32) for part in range(PARTS))
            f_ref[at, array, :, cols] = both.astype(BF)
        for part in range(PARTS):
            for place, eight in enumerate(EIGHTS[part]):
                if eight is not None:
                    row, low = 8 * eight, 176 + 8 * place
                    f_ref[at, 0, row : row + 8, cols] = r_ref[first + part, low : low + 8, :]
    sent[...] = f_ref[1 - core()]
    kept[...] = f_ref[core()]


def place_grads(piece, who, outs, sems):
    return [
        pltpu.make_async_copy(
            piece.at[at, 32 * half : 32 * half + 32, :],
            ref.at[pl.ds(half_row(half, who), 32), :],
            sems.at[at, half],
        )
        for at, ref in enumerate(outs)
        for half in range(2)
    ]


def finish_outs(r_ref, kept, primal, tangent, dq, dk, dv, o_ref, sems, out_sems):
    copies = place_grads(kept, core(), (dq, dk, dv), sems)
    for copy in copies:
        copy.start()
    wide = o_ref.shape[3]
    for head in range(wide // HD):
        cols = slice(head * HD, head * HD + HD)
        for part in range(PARTS):
            for place, unit in enumerate(GAPS[part]):
                if unit is None:
                    continue
                which, eight = unit
                for side in range(2):
                    low = 128 + PIECE * side + 8 * place
                    o_ref[which, side, 8 * eight : 8 * eight + 8, cols] = r_ref[
                        PARTS * head + part, low : low + 8, :
                    ]
    for side, ref in enumerate((primal, tangent)):
        for which, who in enumerate((group(), 1 - group())):
            lanes = pl.ds(pl.multiple_of(wide * who, HD), wide)
            copies.append(
                pltpu.make_async_copy(o_ref.at[which, side], ref.at[:, lanes], out_sems.at[which, side])
            )
            copies[-1].start()
    for copy in copies:
        copy.wait()


def finish_grads(got, dq_in, dk_in, dv_in, dq, dk, dv, sems):
    run_all(place_grads(got, 1 - core(), (dq, dk, dv), sems))


def shape(*dims, dtype=BF):
    return jax.ShapeDtypeStruct(dims, dtype)


SWAP = [(0, 1), (1, 0)]
BLOCK_AXES = ("zl", "y", "x")


def exchange(array):
    return lax.all_to_all(array, BLOCK_AXES, 0, 0, tiled=True)


def swap(array, axis):
    return lax.ppermute(array, axis, SWAP)


def attention(chips, mine):
    length, tiles = chips * KROWS, chips * PIECE // QT
    rows, subs = tiles * QT, length // SUB
    flops = 2 * length * rows * HD
    gpiece = shape(chips, 16, HD)
    gap_sent, gap_kept = call(
        split_gaps, [(gpiece, VMEM), (gpiece, VMEM)], [ANY], 2, (pltpu.SemaphoreType.DMA((2,)),),
        moved=500_000,
    )(mine)
    gap_got = swap(gap_sent, "zh")
    theirs = swap(mine, "c")
    q, qq = shape(tiles, QT, HD), shape(tiles, QT, 2 * HD)
    w = shape(tiles, length, QT)
    stats, sums, acc = (shape(tiles, n, QT, dtype=F32) for n in (1, 2, 2 * HD))
    tiles_of = (pltpu.VMEM(w.shape, BF), pltpu.SemaphoreType.DMA((tiles,)))
    scratch = (
        pltpu.VMEM((2, length, QT), F32),
        pltpu.VMEM((2, length, QT), BF),
        pltpu.VMEM((length, 2 * HD), BF),
        pltpu.VMEM((2 * HD, length), BF),
    )
    back_scratch = (
        pltpu.VMEM((subs, HD, SUB), BF),
        pltpu.VMEM((subs, SUB, rows), BF),
        pltpu.VMEM((SUB, rows), BF),
    )
    stage = pltpu.VMEM((rows, 2 * HD), F32)
    q, qq, w1, m1, sums1, acc1 = call(
        forward_mine,
        [(q, VMEM), (qq, VMEM), (w, HBM), (stats, VMEM), (sums, VMEM), (acc, VMEM)],
        [VMEM],
        30,
        (stage,) + tiles_of + scratch,
        6 * flops, length * rows, 7_000_000,
    )(mine)
    key_piece = shape(chips, KROWS, 2 * HD)
    w2, pieces, cross, o, share = call(
        forward_theirs,
        [
            (w, VMEM), (shape(chips, PIECE, 2 * HD), VMEM), (shape(chips, 16, 2 * HD), VMEM),
            (acc, VMEM), (shape(2, tiles, 1, QT, dtype=F32), VMEM),
        ],
        [VMEM] * 6,
        30,
        (
            pltpu.VMEM(stats.shape, F32), pltpu.VMEM(sums.shape, F32), pltpu.VMEM(acc.shape, F32),
            stage,
        ) + scratch,
        6 * flops, length * rows, 7_000_000,
    )(theirs, q, qq, m1, sums1, acc1)
    cross = swap(cross, "zh")
    dst, cot, inner, dq = call(
        backward_theirs,
        [
            (key_piece, VMEM), (shape(rows, HD), VMEM), (stats, VMEM),
            (shape(HD, rows, dtype=F32), VMEM),
        ],
        [VMEM] * 7,
        30,
        (pltpu.VMEM((rows, HD), F32),) + back_scratch,
        8 * flops, 0, 7_000_000,
    )(theirs, gap_kept, gap_got, q, o, w2, share)
    partner = swap(dst, "c")
    out, dq = call(
        backward_mine,
        [(key_piece, VMEM), (shape(chips, PIECE, HD), VMEM)],
        [VMEM] * 7,
        30,
        (pltpu.VMEM((rows, HD), F32),) + back_scratch,
        8 * flops, 0, 7_000_000,
    )(mine, q, cot, inner, w1, share, dq)
    return call(gather_out, [(shape(chips, 200, HD), VMEM)], [VMEM] * 5, 8)(
        out, dq, pieces, cross, partner
    )[0]


def per_device(q, k, v, tq, tk, tv, gap):
    chips = lax.axis_size(BLOCK_AXES)
    local, feat = q.shape
    wide = gap.shape[1] // 2
    piece = shape(6, KROWS, feat)
    arrays = [
        pltpu.with_memory_space_constraint(one, pltpu.HBM) for one in (q, k, v, tq, tk, tv, gap)
    ]
    sems = pltpu.SemaphoreType.DMA((6, 2))
    sent = call(send_tokens, [(piece, VMEM)], [HBM] * 6, 2, (sems,))(*arrays[:6])[0]
    got = swap(sent, "c")
    kept, gap_here = call(
        keep_tokens,
        [(piece, VMEM), (shape(2, 32, wide), VMEM)],
        [HBM] * 7,
        2,
        (sems, pltpu.SemaphoreType.DMA((2,))),
    )(*arrays)
    packed = call(
        pack_heads,
        [(shape(chips, SLOT, HD), VMEM)],
        [VMEM] * 3,
        8,
        (pltpu.VMEM((2,) + piece.shape, BF),),
    )(kept, got, gap_here)[0]
    mine = exchange(packed)

    back = exchange(attention(chips, mine))

    fpiece = shape(3, KROWS, feat)
    sent, kept = call(
        unpack_grads, [(fpiece, VMEM), (fpiece, VMEM)], [VMEM], 8,
        (pltpu.VMEM((2,) + fpiece.shape, BF),),
    )(back)
    got = swap(sent, "c")
    small, large = shape(32, 2 * wide), shape(local, feat)
    sems = pltpu.SemaphoreType.DMA((3, 2))
    primal, tangent, *grads = call(
        finish_outs, [(small, HBM)] * 2 + [(large, HBM)] * 3, [VMEM] * 2, 8,
        (pltpu.VMEM((2, 2, 32, wide), BF), sems, pltpu.SemaphoreType.DMA((2, 2))),
    )(back, kept)
    dq, dk, dv = call(
        finish_grads, [(large, HBM)] * 3, [VMEM] + [HBM] * 3, 4, (sems,), aliases={1: 0, 2: 1, 3: 2}
    )(got, *grads)
    return primal, tangent, dq, dk, dv


def solution(mesh):
    sizes = (2, 4, 4, 2, 2)
    inner = Mesh(mesh.devices.reshape(sizes), BLOCK_AXES + ("zh", "c"))
    both = P(BLOCK_AXES, ("zh", "c"))
    rows = P(BLOCK_AXES + ("zh", "c"), None)

    return jax.shard_map(
        per_device,
        mesh=inner,
        in_specs=(both,) * 6 + (rows,),
        out_specs=(rows, rows, both, both, both),
        check_vma=False,
    )
```

```python
import math

import jax
import jax.numpy as jnp
from jax import lax
from jax.experimental import pallas as pl
from jax.experimental.pallas import tpu as pltpu
from jax.sharding import Mesh, PartitionSpec as P


BF = jnp.bfloat16
F32 = jnp.float32
HD = 128
LOSS = 64.0
PARTS = 3
PIECE = 24
EIGHTS = ((0, 1, 4), (2, 5, None), (3, 6, 7))
GAPS = (((0, 0), (0, 1), (1, 0)), ((0, 2), (1, 1), None), ((0, 3), (1, 2), (1, 3)))
SLOT = 328
KROWS = 64
QT = 256
SUB = 512
INV = 1.0 / math.sqrt(HD)
EXP_SCALE = INV * math.log2(math.e)
VMEM = pl.BlockSpec(memory_space=pltpu.VMEM)
HBM = pl.BlockSpec(memory_space=pltpu.HBM)
ANY = pl.BlockSpec(memory_space=pl.ANY)


def call(body, outs, ins, limit, scratch=(), flops=0, exps=0, moved=1_000_000):
    return pl.pallas_call(
        body,
        out_shape=[
            pltpu.HBM(one.shape, one.dtype) if place is HBM else one for one, place in outs
        ],
        in_specs=ins,
        out_specs=[place for _, place in outs],
        scratch_shapes=list(scratch),
        compiler_params=pltpu.CompilerParams(vmem_limit_bytes=limit * 1024 * 1024),
        cost_estimate=pl.CostEstimate(flops=flops, bytes_accessed=moved, transcendentals=exps),
    )


def nt(a, b):
    return lax.dot_general(a, b, (((1,), (1,)), ((), ())), preferred_element_type=F32)


def nn(a, b):
    return lax.dot_general(a, b, (((1,), (0,)), ((), ())), preferred_element_type=F32)


def core():
    return lax.axis_index("c")


def group():
    return lax.axis_index("zh")


def half_row(half, who):
    return pl.multiple_of(64 * lax.rem(group() + half, 2) + 32 * who, 32)


def part_here():
    place = lax.axis_index("x") * 8 + lax.axis_index("zl") * 4 + lax.axis_index("y")
    return lax.rem(place, PARTS)


def split_tokens(arrays, dst, who, sems):
    return [
        pltpu.make_async_copy(
            ref.at[pl.ds(half_row(half, who), 32), :],
            dst.at[at, 32 * half : 32 * half + 32, :],
            sems.at[at, half],
        )
        for at, ref in enumerate(arrays)
        for half in range(2)
    ]


def run_all(copies):
    for copy in copies:
        copy.start()
    for copy in copies:
        copy.wait()


def send_tokens(*refs):
    *arrays, sent, sems = refs
    run_all(split_tokens(arrays, sent, 1 - core(), sems))


def keep_tokens(*refs):
    *arrays, gap, kept, gap_here, sems, gap_sems = refs
    copies = split_tokens(arrays, kept, core(), sems)
    wide = gap_here.shape[2]
    for at, who in enumerate((group(), 1 - group())):
        lanes = pl.ds(pl.multiple_of(who * wide, HD), wide)
        copies.append(pltpu.make_async_copy(gap.at[:, lanes], gap_here.at[at], gap_sems.at[at]))
    run_all(copies)


def pack_heads(kept, got, gap, out, e_ref):
    e_ref[core()] = kept[...]
    e_ref[1 - core()] = got[...]
    half = e_ref.shape[3] // HD
    zero = jnp.zeros((8, HD), BF)
    for chip in range(out.shape[0]):
        head, part = chip // PARTS, chip % PARTS
        if head >= 2 * half:
            out[chip] = jnp.zeros(out.shape[1:], BF)
            continue
        at, cols = head // half, slice((head % half) * HD, (head % half + 1) * HD)
        for to, array in enumerate((1, 4, 2, 5)):
            out[chip, KROWS * to : KROWS * to + KROWS, :] = e_ref[at, array, :, cols]
        gcols = slice(head * HD, head * HD + HD)
        for to in range(3):
            eight = EIGHTS[part][to]
            for low, array in ((256, 0), (280, 3)):
                rows = slice(low + 8 * to, low + 8 * to + 8)
                if eight is None:
                    out[chip, rows, :] = zero
                else:
                    out[chip, rows, :] = e_ref[at, array, 8 * eight : 8 * eight + 8, cols]
            rows = slice(304 + 8 * to, 312 + 8 * to)
            if GAPS[part][to] is None:
                out[chip, rows, :] = zero
            else:
                which, eight = GAPS[part][to]
                out[chip, rows, :] = gap[which, 8 * eight : 8 * eight + 8, gcols]


def split_gaps(mine, sent, kept, sems):
    run_all(
        [
            pltpu.make_async_copy(mine.at[:, low : low + 16, :], dst, sems.at[at])
            for at, (dst, low) in enumerate(((sent, 312), (kept, 304)))
        ]
    )


def fold(x, op):
    return op(x.reshape(x.shape[0] // 8, 8, x.shape[1]), axis=0)


def forward(keys, q_ref, qq_ref, w_ref, m_ref, sums_ref, acc_ref, s_ref, wt_ref, kk_ref, vt_ref,
            done=None, close=None):
    tiles = q_ref.shape[0]
    per = SUB // KROWS
    subs = kk_ref.shape[0] // SUB
    ats = [slice(SUB * i, SUB * i + SUB) for i in range(subs)]

    def scores(t, i, peak):
        s = nt(kk_ref[ats[i], 0:HD], q_ref[t])
        s_ref[t % 2, ats[i], :] = s
        return jnp.maximum(peak, fold(s, jnp.max))

    def values(t, i):
        both = nn(vt_ref[:, ats[i]], w_ref[t, ats[i], :])
        tan = nn(vt_ref[0:HD, ats[i]], wt_ref[t % 2, ats[i], :]) * INV
        if i == 0:
            acc_ref[t, 0:HD, :] = both[0:HD]
            acc_ref[t, HD:, :] = both[HD:] + tan
        else:
            acc_ref[t, 0:HD, :] += both[0:HD]
            acc_ref[t, HD:, :] += both[HD:] + tan

    lowest = jnp.full((8, QT), -jnp.inf, F32)
    peak = lowest
    for i in range(subs):
        slots = slice(per * i, per * i + per)
        for half in range(2):
            lanes = slice(HD * half, HD * half + HD)
            kk_ref[ats[i], lanes] = keys[slots, KROWS * half : KROWS * half + KROWS, :].reshape(SUB, HD)
            v = keys[slots, KROWS * (2 + half) : KROWS * (3 + half), :].reshape(SUB, HD)
            vt_ref[lanes, ats[i]] = v.astype(F32).T.astype(BF)
        peak = scores(0, i, peak)
    for t in range(tiles):
        top = jnp.max(peak, axis=0, keepdims=True)
        m_ref[t] = top
        peak = lowest
        total = jnp.zeros((8, QT), F32)
        tan_total = jnp.zeros((8, QT), F32)
        for i in range(subs):
            w = jnp.exp2((s_ref[t % 2, ats[i], :] - top) * EXP_SCALE)
            wt = w * nt(kk_ref[ats[i], :], qq_ref[t])
            total = total + fold(w, jnp.sum)
            tan_total = tan_total + fold(wt, jnp.sum)
            w_ref[t, ats[i], :] = w.astype(BF)
            wt_ref[t % 2, ats[i], :] = wt.astype(BF)
            if t + 1 < tiles:
                peak = scores(t + 1, i, peak)
            if t > 0:
                values(t - 1, i)
        sums_ref[t, 0:1, :] = jnp.sum(total, axis=0, keepdims=True)
        sums_ref[t, 1:2, :] = jnp.sum(tan_total, axis=0, keepdims=True) * INV
        if done is not None:
            done(t)
        if close is not None and t > 0:
            close(t - 1)
    for i in range(subs):
        values(tiles - 1, i)
    if close is not None:
        close(tiles - 1)


def forward_mine(mine, q_ref, qq_ref, w_hbm, m_ref, sums_ref, acc_ref, stage, w_ref, sems, *scratch):
    for s in range(mine.shape[0]):
        stage[PIECE * s : PIECE * s + PIECE, 0:HD] = mine[s, 256:280, :].astype(F32)
        stage[PIECE * s : PIECE * s + PIECE, HD:] = mine[s, 280:304, :].astype(F32)
    tiles = q_ref.shape[0]
    for t in range(tiles):
        rows = slice(QT * t, QT * t + QT)
        q_ref[t] = stage[rows, 0:HD].astype(BF)
        qq_ref[t, :, 0:HD] = stage[rows, HD:].astype(BF)
        qq_ref[t, :, HD:] = stage[rows, 0:HD].astype(BF)
    copies = [pltpu.make_async_copy(w_ref.at[t], w_hbm.at[t], sems.at[t]) for t in range(tiles)]
    forward(
        mine, q_ref, qq_ref, w_ref, m_ref, sums_ref, acc_ref, *scratch,
        done=lambda t: copies[t].start(),
    )
    for copy in copies:
        copy.wait()


def rows_of(ref, low):
    return lambda at, slots: ref[slots, low : low + KROWS, :].reshape(SUB, HD)


def backward(key, value, q_ref, cot_ref, inner_ref, w_ref, share_ref, side, dst, dq, kt_ref, ds_ref, p_ref):
    tiles = q_ref.shape[0]
    per = SUB // KROWS
    subs = ds_ref.shape[0]
    q_all = q_ref[...].reshape(tiles * QT, HD)
    for i in range(subs):
        at, slots = slice(SUB * i, SUB * i + SUB), slice(per * i, per * i + per)
        v = value(at, slots)
        kt_ref[i] = key(at, slots).astype(F32).T.astype(BF)
        for t in range(tiles):
            cols = slice(QT * t, QT * t + QT)
            p = w_ref[t, at, :].astype(F32) * share_ref[side, t]
            ds = p * (nt(v, cot_ref[cols, :]) - inner_ref[t])
            p_ref[:, cols] = p.astype(BF)
            ds_ref[i, :, cols] = ds.astype(BF)
        dk = nn(ds_ref[i], q_all) * INV
        dv = nn(p_ref[...], cot_ref[...])
        dst[slots, 0:KROWS, 0:HD] = dk.astype(BF).reshape(per, KROWS, HD)
        dst[slots, 0:KROWS, HD:] = dv.astype(BF).reshape(per, KROWS, HD)
    for i in range(subs):
        dq = dq + nn(kt_ref[i], ds_ref[i])
    return dq


def forward_theirs(
    theirs, q_ref, qq_ref, m1_ref, sums1_ref, acc1_ref,
    w_ref, pieces, cross, o_ref, share_ref,
    m_ref, sums_ref, acc_ref, stage, *scratch
):
    def close(t):
        rows = slice(QT * t, QT * t + QT)
        top = jnp.maximum(m1_ref[t], m_ref[t])
        f1 = jnp.exp2((m1_ref[t] - top) * EXP_SCALE)
        f2 = jnp.exp2((m_ref[t] - top) * EXP_SCALE)
        sums = sums1_ref[t] * f1 + sums_ref[t] * f2
        inverse = 1.0 / sums[0:1]
        s1, s2 = f1 * inverse, f2 * inverse
        share_ref[0, t] = s1
        share_ref[1, t] = s2
        both = acc1_ref[t] * s1 + acc_ref[t] * s2
        tangent = both[HD:] - (sums[1:2] * inverse) * both[0:HD]
        o_ref[t, 0:HD, :] = both[0:HD].astype(BF).astype(F32)
        o_ref[t, HD:, :] = tangent.astype(BF).astype(F32)
        stage[rows, :] = o_ref[t].T

    forward(
        theirs, q_ref, qq_ref, w_ref, m_ref, sums_ref, acc_ref, *scratch, close=close
    )
    for s in range(pieces.shape[0]):
        low = PIECE * s
        pieces[s] = stage[low : low + PIECE, :].astype(BF)
        cross[s] = stage[low + 8 : low + PIECE, :].astype(BF)


def backward_theirs(
    theirs, gap_kept, gap_got, q_ref, o_ref, w_ref, share_ref,
    dst, cot_ref, inner_ref, dq_ref, stage, *scratch
):
    first = part_here() == 0
    for s in range(gap_kept.shape[0]):
        low = PIECE * s
        own, got = gap_kept[s].astype(F32), gap_got[s].astype(F32)
        stage[low : low + 8, :] = own[0:8]
        stage[low + 8 : low + 16, :] = jnp.where(first, own[8:16], got[0:8])
        stage[low + 16 : low + 24, :] = got[8:16]
    for t in range(q_ref.shape[0]):
        rows = slice(QT * t, QT * t + QT)
        place = lax.rem(QT * t + lax.broadcasted_iota(jnp.int32, (1, QT), 1), PIECE)
        short = jnp.where(place >= 16, 1, 0) * jnp.where(part_here() == 1, 1, 0)
        mask = jnp.where(short == 1, 0.0, 1.0)
        cot = (LOSS * (stage[rows, :].T + o_ref[t, HD:, :])) * mask
        cot = cot.astype(BF).astype(F32)
        inner_ref[t] = jnp.sum(cot * o_ref[t, 0:HD, :], axis=0, keepdims=True)
        cot_ref[rows, :] = cot.T.astype(BF)
    dq_ref[...] = backward(
        rows_of(theirs, 0), rows_of(theirs, 2 * KROWS),
        q_ref, cot_ref, inner_ref, w_ref, share_ref, 1, dst, jnp.zeros(dq_ref.shape, F32), *scratch,
    )


def backward_mine(
    mine, q_ref, cot_ref, inner_ref, w_ref, share_ref, dq_ref, out, dq_out, stage, *scratch
):
    dq = backward(
        rows_of(mine, 0), rows_of(mine, 2 * KROWS),
        q_ref, cot_ref, inner_ref, w_ref, share_ref, 0, out, dq_ref[...], *scratch,
    )
    stage[...] = (dq * INV).T
    for s in range(out.shape[0]):
        dq_out[s] = stage[PIECE * s : PIECE * s + PIECE, :].astype(BF)


def gather_out(mine, dq, pieces, got, theirs, out):
    first = part_here() == 0
    for s in range(out.shape[0]):
        both = (mine[s].astype(F32) + theirs[s].astype(F32)).astype(BF)
        out[s, 0:64, :] = both[:, 0:HD]
        out[s, 64:128, :] = both[:, HD:]
        second = jnp.where(first, pieces[s, 8:16, :].astype(F32), got[s, 0:8, :].astype(F32)).astype(BF)
        for low, lanes in ((128, slice(0, HD)), (152, slice(HD, 2 * HD))):
            out[s, low : low + 8, :] = pieces[s, 0:8, lanes]
            out[s, low + 8 : low + 16, :] = second[:, lanes]
            out[s, low + 16 : low + 24, :] = got[s, 8:16, lanes]
        out[s, 176:200, :] = dq[s]


def unpack_grads(r_ref, sent, kept, f_ref):
    half = f_ref.shape[3] // HD
    for head in range(2 * half):
        at, cols = head // half, slice((head % half) * HD, (head % half + 1) * HD)
        first = PARTS * head
        for array, low in ((1, 0), (2, KROWS)):
            rows = slice(low, low + KROWS)
            both = sum(r_ref[first + part, rows, :].astype(F32) for part in range(PARTS))
            f_ref[at, array, :, cols] = both.astype(BF)
        for part in range(PARTS):
            for place, eight in enumerate(EIGHTS[part]):
                if eight is not None:
                    row, low = 8 * eight, 176 + 8 * place
                    f_ref[at, 0, row : row + 8, cols] = r_ref[first + part, low : low + 8, :]
    sent[...] = f_ref[1 - core()]
    kept[...] = f_ref[core()]


def finish_outs(r_ref, primal, tangent, o_ref):
    wide = o_ref.shape[3]
    for head in range(wide // HD):
        cols = slice(head * HD, head * HD + HD)
        for part in range(PARTS):
            for place, unit in enumerate(GAPS[part]):
                if unit is None:
                    continue
                which, eight = unit
                for side in range(2):
                    low = 128 + PIECE * side + 8 * place
                    o_ref[which, side, 8 * eight : 8 * eight + 8, cols] = r_ref[
                        PARTS * head + part, low : low + 8, :
                    ]
    for side, ref in enumerate((primal, tangent)):
        for which, who in enumerate((group(), 1 - group())):
            ref[:, pl.ds(pl.multiple_of(wide * who, HD), wide)] = o_ref[which, side]


def finish_grads(kept, got, dq, dk, dv):
    for at, ref in enumerate((dq, dk, dv)):
        for half in range(2):
            rows = slice(32 * half, 32 * half + 32)
            for piece, who in ((kept, core()), (got, 1 - core())):
                ref[pl.ds(half_row(half, who), 32), :] = piece[at, rows, :]


def shape(*dims, dtype=BF):
    return jax.ShapeDtypeStruct(dims, dtype)


SWAP = [(0, 1), (1, 0)]
BLOCK_AXES = ("zl", "y", "x")
CHIP_AXES = ("x", "zl", "y")


def exchange(array):
    return lax.all_to_all(array, CHIP_AXES, 0, 0, tiled=True)


def swap(array, axis):
    return lax.ppermute(array, axis, SWAP)


def attention(chips, mine):
    length, tiles = chips * KROWS, chips * PIECE // QT
    rows, subs = tiles * QT, length // SUB
    flops = 2 * length * rows * HD
    gpiece = shape(chips, 16, HD)
    gap_sent, gap_kept = call(
        split_gaps, [(gpiece, VMEM), (gpiece, VMEM)], [ANY], 2, (pltpu.SemaphoreType.DMA((2,)),),
        moved=500_000,
    )(mine)
    gap_got = swap(gap_sent, "zh")
    theirs = swap(mine, "c")
    q, qq = shape(tiles, QT, HD), shape(tiles, QT, 2 * HD)
    w = shape(tiles, length, QT)
    stats, sums, acc = (shape(tiles, n, QT, dtype=F32) for n in (1, 2, 2 * HD))
    tiles_of = (pltpu.VMEM(w.shape, BF), pltpu.SemaphoreType.DMA((tiles,)))
    scratch = (
        pltpu.VMEM((2, length, QT), F32),
        pltpu.VMEM((2, length, QT), BF),
        pltpu.VMEM((length, 2 * HD), BF),
        pltpu.VMEM((2 * HD, length), BF),
    )
    back_scratch = (
        pltpu.VMEM((subs, HD, SUB), BF),
        pltpu.VMEM((subs, SUB, rows), BF),
        pltpu.VMEM((SUB, rows), BF),
    )
    stage = pltpu.VMEM((rows, 2 * HD), F32)
    q, qq, w1, m1, sums1, acc1 = call(
        forward_mine,
        [(q, VMEM), (qq, VMEM), (w, HBM), (stats, VMEM), (sums, VMEM), (acc, VMEM)],
        [VMEM],
        30,
        (stage,) + tiles_of + scratch,
        6 * flops, length * rows, 7_000_000,
    )(mine)
    key_piece = shape(chips, KROWS, 2 * HD)
    w2, pieces, cross, o, share = call(
        forward_theirs,
        [
            (w, VMEM), (shape(chips, PIECE, 2 * HD), VMEM), (shape(chips, 16, 2 * HD), VMEM),
            (acc, VMEM), (shape(2, tiles, 1, QT, dtype=F32), VMEM),
        ],
        [VMEM] * 6,
        30,
        (
            pltpu.VMEM(stats.shape, F32), pltpu.VMEM(sums.shape, F32), pltpu.VMEM(acc.shape, F32),
            stage,
        ) + scratch,
        6 * flops, length * rows, 7_000_000,
    )(theirs, q, qq, m1, sums1, acc1)
    cross = swap(cross, "zh")
    dst, cot, inner, dq = call(
        backward_theirs,
        [
            (key_piece, VMEM), (shape(rows, HD), VMEM), (stats, VMEM),
            (shape(HD, rows, dtype=F32), VMEM),
        ],
        [VMEM] * 7,
        30,
        (pltpu.VMEM((rows, HD), F32),) + back_scratch,
        8 * flops, 0, 7_000_000,
    )(theirs, gap_kept, gap_got, q, o, w2, share)
    partner = swap(dst, "c")
    out, dq = call(
        backward_mine,
        [(key_piece, VMEM), (shape(chips, PIECE, HD), VMEM)],
        [VMEM] * 7,
        30,
        (pltpu.VMEM((rows, HD), F32),) + back_scratch,
        8 * flops, 0, 7_000_000,
    )(mine, q, cot, inner, w1, share, dq)
    return call(gather_out, [(shape(chips, 200, HD), VMEM)], [VMEM] * 5, 8)(
        out, dq, pieces, cross, partner
    )[0]


def per_device(q, k, v, tq, tk, tv, gap):
    chips = lax.axis_size(BLOCK_AXES)
    local, feat = q.shape
    wide = gap.shape[1] // 2
    piece = shape(6, KROWS, feat)
    arrays = [
        pltpu.with_memory_space_constraint(one, pltpu.HBM) for one in (q, k, v, tq, tk, tv, gap)
    ]
    sems = pltpu.SemaphoreType.DMA((6, 2))
    sent = call(send_tokens, [(piece, VMEM)], [HBM] * 6, 2, (sems,))(*arrays[:6])[0]
    got = swap(sent, "c")
    kept, gap_here = call(
        keep_tokens,
        [(piece, VMEM), (shape(2, 32, wide), VMEM)],
        [HBM] * 7,
        2,
        (sems, pltpu.SemaphoreType.DMA((2,))),
    )(*arrays)
    packed = call(
        pack_heads,
        [(shape(chips, SLOT, HD), VMEM)],
        [VMEM] * 3,
        8,
        (pltpu.VMEM((2,) + piece.shape, BF),),
    )(kept, got, gap_here)[0]
    mine = exchange(packed)

    back = exchange(attention(chips, mine))

    fpiece = shape(3, KROWS, feat)
    sent, kept = call(
        unpack_grads, [(fpiece, VMEM), (fpiece, VMEM)], [VMEM], 8,
        (pltpu.VMEM((2,) + fpiece.shape, BF),),
    )(back)
    got = swap(sent, "c")
    small, large = shape(32, 2 * wide), shape(local, feat)
    primal, tangent = call(
        finish_outs, [(small, VMEM)] * 2, [VMEM], 8, (pltpu.VMEM((2, 2, 32, wide), BF),)
    )(back)
    dq, dk, dv = call(finish_grads, [(large, VMEM)] * 3, [VMEM] * 2, 8)(kept, got)
    return primal, tangent, dq, dk, dv


def solution(mesh):
    sizes = (2, 4, 4, 2, 2)
    inner = Mesh(mesh.devices.reshape(sizes), BLOCK_AXES + ("zh", "c"))
    both = P(BLOCK_AXES, ("zh", "c"))
    rows = P(BLOCK_AXES + ("zh", "c"), None)

    return jax.shard_map(
        per_device,
        mesh=inner,
        in_specs=(both,) * 6 + (rows,),
        out_specs=(rows, rows, both, both, both),
        check_vma=False,
    )
```
